128 devices in a mesh: apa: 4 (over x), tick: 32 (over z, y, core).
Axes of the slice: x: 4, y: 4, z: 4, core: 2. Of those that a mesh axis runs over, the one named last changes fastest.
Arguments:
- raw: float32 [61440, 3200], P('apa', 'tick'), may hold values from -90 to 90
- bad: int32 [61440], P('apa'), may hold values 0 or 1
- group_id: int32 [61440], P('apa'), may hold values from 0 to 479, as said below
- chan_plane: int32 [61440], P('apa'), may hold values from 0 to 127, as said below
- chan_wire: int32 [61440], P('apa'), may hold values from 0 to 479, as said below
- plane_offset: int32 [128], replicated, may hold values from 0 to 479
- wire_kernel: float32 [480], replicated, may hold values from -0.2738613 to 0.2738613
- time_kernel: float32 [3200], replicated, may hold values from -0.10606602 to 0.10606602
Outputs:
- deconvolved: float32 [128, 480, 3200], P(('apa', 'tick'))
The draws below stay inside these ranges and needn't reach their ends.
Inputs may be any that keep to these rules, and one draw needn't show every extreme that they name: `group_id`: each block of 15360 consecutive channels holds whole groups of exactly 128 channels each, with the ids of that block's groups only. `chan_plane`: blocks of 15360 consecutive channels form aligned pairs (blocks 2m and 2m + 1); the channels of a pair go to planes 2m 32 to 2m 32 + 2 * 32 - 1 only, and each plane receives exactly 480 channels. A block names each plane of its pair either 240 - 180 or 420 times, the same number for all planes of one run of 32 consecutive planes (aligned runs), so at most 13440 for a run; both counts occur in every draw. `chan_wire`: the channels of one plane have distinct values.
All inputs are finite; a program needn't handle non-finite values. No bound on the sum of `bad` on one device may be relied on, other than what follows from the above.
Results may differ from the reference program's by a relative error of at most 0.000075.
Values sent between devices are 32-bit elements; how exact they have to be, the bound alone decides.
No kernel may reach another device: no remote copies, remote signals or barrier semaphores. Data moves between devices by JAX's collectives and lax.ppermute only.
A program may use at most 128 MiB of HBM per device.

```python
import jax
import jax.numpy as jnp
from jax import lax

WP = 480
TICKS = 3200
GROUP = 128
PLANES = 128
CHANNELS = 61440
CH_DEV = 15360
GROUPS = 480
BASE = 240
SPREAD = 180


def group_table(key):
    key_group = jax.random.fold_in(key, 11)
    block_count = CHANNELS // CH_DEV
    per_block = CH_DEV // GROUP
    block_keys = jax.random.split(key_group, block_count)
    orders = jax.vmap(lambda single: jax.random.permutation(single, CH_DEV))(block_keys)
    block_base = jnp.arange(block_count, dtype=jnp.int32)[:, None] * per_block
    return (orders.astype(jnp.int32) // GROUP + block_base).reshape(-1).astype(jnp.int32)


def map_tables(key):
    key_map = jax.random.fold_in(key, 7)
    block_count = CHANNELS // CH_DEV
    plane_count = CHANNELS // WP
    per_run = plane_count // block_count
    pair_count = block_count // 2
    key_rows, key_cols, key_order, key_wires = jax.random.split(key_map, 4)
    first_row = jnp.where(jax.random.randint(key_rows, (pair_count,), 0, 2) == 0, 1, -1).astype(jnp.int32)
    row_signs = jnp.stack([first_row, -first_row], axis=1).reshape(-1)
    first_col = jnp.where(jax.random.randint(key_cols, (pair_count,), 0, 2) == 0, 1, -1).astype(jnp.int32)
    run_signs = jnp.stack([first_col, -first_col], axis=1).reshape(-1)
    col_signs = jnp.repeat(run_signs, per_run)
    block_pair = jnp.arange(block_count, dtype=jnp.int32) // 2
    plane_pair = jnp.arange(plane_count, dtype=jnp.int32) // per_run // 2
    inside = block_pair[:, None] == plane_pair[None, :]
    counts = jnp.where(inside, BASE + SPREAD * row_signs[:, None] * col_signs[None, :], 0).astype(jnp.int32)

    def block_planes(count_row, single):
        listed = jnp.repeat(jnp.arange(plane_count, dtype=jnp.int32), count_row, total_repeat_length=CH_DEV)
        return jax.random.permutation(single, listed)
    planes = jax.vmap(block_planes)(counts, jax.random.split(key_order, block_count))
    onehot_plane = (planes[:, :, None] == jnp.arange(plane_count, dtype=jnp.int32)[None, None, :]).astype(jnp.int32)
    rank_inside = jnp.sum(jnp.cumsum(onehot_plane, axis=1) * onehot_plane, axis=2) - 1
    before_block = jnp.cumsum(counts, axis=0) - counts
    rank_before = jnp.sum(onehot_plane * before_block[:, None, :], axis=2)
    plane_rank = (rank_inside + rank_before).astype(jnp.int32)
    wire_orders = jax.vmap(lambda single: jax.random.permutation(single, WP))(jax.random.split(key_wires, plane_count))
    wires = wire_orders.astype(jnp.int32)[planes, plane_rank]
    return (planes.reshape(-1).astype(jnp.int32), wires.reshape(-1).astype(jnp.int32))


def draw_group_id(key, part):
    return group_table(key)


def draw_chan_plane(key, part):
    return map_tables(key)[0]


def draw_chan_wire(key, part):
    return map_tables(key)[1]


def draw_raw(key, part):
    group_ids = group_table(key)
    key_raw = jax.random.fold_in(key, 13)
    key_couple, key_sigma, key_common, key_noise = jax.random.split(key_raw, 4)
    coupling = jnp.exp(jax.random.uniform(key_couple, (CHANNELS,), jnp.float32, jnp.log(0.5), jnp.log(2.0)))
    sigma_chan = jnp.exp(jax.random.uniform(key_sigma, (CHANNELS,), jnp.float32, jnp.log(0.3), jnp.log(3.0)))
    envelope = 1.0 + 2.0 * jnp.arange(TICKS, dtype=jnp.float32) / (TICKS - 1)
    common = jnp.clip(2.0 * jax.random.normal(key_common, (GROUPS, TICKS), jnp.float32), -8.0, 8.0)
    noise = jnp.clip(jax.random.normal(key_noise, (CHANNELS, TICKS), jnp.float32), -4.0, 4.0)
    signal = coupling[:, None] * common[group_ids] + sigma_chan[:, None] * noise
    return (envelope[None, :] * signal).astype(jnp.float32)


def with_ends(drawn, rng, least, top_value):
    index_at = [jax.random.randint(jax.random.fold_in(rng, axis), (), 0, length) for axis, length in enumerate(drawn.shape)]
    widest = drawn.shape.index(max(drawn.shape))
    next_to = index_at[:widest] + [(index_at[widest] + 1) % drawn.shape[widest]] + index_at[widest + 1:]
    return drawn.at[tuple(index_at)].set(least).at[tuple(next_to)].set(top_value)


def centred(rng, dims, width, reach, kind=jnp.bfloat16):
    return jnp.clip(width * jax.random.normal(rng, dims, jnp.float32), -reach, reach).astype(kind)


def setup_inputs(seed: int = 0) -> dict:
    keys = jax.random.split(jax.random.key(seed), 9)
    raw = draw_raw(jax.random.fold_in(keys[8], 71), 0)
    bad = with_ends((jax.random.randint(keys[1], (CHANNELS,), 0, 16) < 1).astype(jnp.int32), jax.random.fold_in(keys[1], 1), 0, 1)
    group_id = draw_group_id(jax.random.fold_in(keys[8], 71), 0)
    chan_plane = draw_chan_plane(jax.random.fold_in(keys[8], 71), 0)
    chan_wire = draw_chan_wire(jax.random.fold_in(keys[8], 71), 0)
    plane_offset = with_ends(jax.random.randint(keys[5], (PLANES,), 0, WP), jax.random.fold_in(keys[5], 1), 0, WP - 1).astype(jnp.int32)
    wire_kernel = centred(keys[6], (WP,), (WP ** -0.5), 0.2738613, jnp.float32)
    time_kernel = centred(keys[7], (TICKS,), (TICKS ** -0.5), 0.10606602, jnp.float32)
    return dict(raw=raw, bad=bad, group_id=group_id, chan_plane=chan_plane, chan_wire=chan_wire, plane_offset=plane_offset, wire_kernel=wire_kernel, time_kernel=time_kernel)


epsilon_power = 1e-6
regular_term = 0.25


def reference(raw, bad, group_id, chan_plane, chan_wire, plane_offset, wire_kernel, time_kernel):
    good_mask = jnp.float32(1.0) - bad.astype(jnp.float32)
    common = jax.ops.segment_sum(raw * good_mask[:, None], group_id, num_segments=GROUPS)
    spread_common = common[group_id]
    covar = jnp.sum(raw * spread_common, axis=1) / TICKS
    power = jnp.sum(common * common, axis=1)[group_id] / TICKS
    cleaned = good_mask[:, None] * (raw - (covar / (power + epsilon_power))[:, None] * spread_common)
    wire_index = (chan_wire + plane_offset[chan_plane]) % WP
    slots = (chan_plane * WP + wire_index).astype(jnp.int32)
    planes = jnp.zeros((PLANES * WP, TICKS), jnp.float32).at[slots].set(cleaned).reshape(PLANES, WP, TICKS)
    wire_resp = jnp.fft.fft(wire_kernel)
    time_resp = jnp.fft.fft(time_kernel)
    response = wire_resp[:, None] * time_resp[None, :]
    deconv_filter = jnp.conj(response) / (response.real * response.real + response.imag * response.imag + regular_term)

    def one_plane(plane_block):
        return jnp.real(jnp.fft.ifft2(jnp.fft.fft2(plane_block) * deconv_filter)).astype(jnp.float32)

    return lax.map(one_plane, planes)
```

```python
import math

import jax
import jax.numpy as jnp
import ml_dtypes
import numpy as np
from jax import lax
from jax.experimental import pallas as pl
from jax.experimental.pallas import tpu as pltpu
from jax.sharding import PartitionSpec as P

TICKS = 3200
GROUP = 128
WIRES = 480
SLABS = 32
SLAB = 100
PART = 128
HALF = 256
PIECE = 32
LANES = 5
WIDE = 512
BLOCK = 256
SENT = (32, 32, 24)

highest = lax.Precision.HIGHEST
epsilon_power = 1e-06
regular_term = 0.25
mega = 1024 * 1024


def roomy(size):
    return pltpu.CompilerParams(vmem_limit_bytes=size * mega)


def two_halves(table):
    high = table.astype(ml_dtypes.bfloat16)
    low = (table - high.astype(np.float64)).astype(ml_dtypes.bfloat16)
    return high, low


def split(value):
    high = value.astype(jnp.bfloat16)
    low = (value - high.astype(jnp.float32)).astype(jnp.bfloat16)
    return high, low


def dot(left, right):
    return jnp.dot(left, right, preferred_element_type=jnp.float32)


def three_dot(left_high, left_low, right_high, right_low):
    return dot(left_high, right_high) + (dot(left_high, right_low) + dot(left_low, right_high))


def wire_tables():
    spread = np.outer(np.arange(WIRES // 2 + 1), np.arange(WIRES)) % WIRES
    angle = 2.0 * np.pi * spread / WIRES
    forward = np.zeros((2, HALF, WIRES))
    forward[0, : WIRES // 2 + 1] = np.cos(angle)
    forward[1, : WIRES // 2 + 1] = -np.sin(angle)
    weight = np.full((WIRES // 2 + 1, 1), 2.0)
    weight[0] = weight[-1] = 1.0
    weight /= WIRES * TICKS
    backward = np.zeros((2, HALF, WIRES))
    backward[0, : WIRES // 2 + 1] = weight * np.cos(angle)
    backward[1, : WIRES // 2 + 1] = -weight * np.sin(angle)
    return forward.reshape(2 * HALF, WIRES), backward.reshape(2 * HALF, WIRES).T.copy()


def tick_tables():
    first = np.arange(SLABS)[:, None, None]
    inner = np.arange(SLAB)[None, :, None]
    second = np.arange(SLAB)[None, None, :]
    angle = 2.0 * np.pi * ((inner * first + SLABS * inner * second) % TICKS) / TICKS
    table = np.zeros((SLABS, 2, PART, 2, PART))
    table[:, 0, :SLAB, 0, :SLAB] = np.cos(angle)
    table[:, 1, :SLAB, 1, :SLAB] = np.cos(angle)
    table[:, 0, :SLAB, 1, :SLAB] = -np.sin(angle)
    table[:, 1, :SLAB, 0, :SLAB] = np.sin(angle)
    table = table.reshape(SLABS, HALF, HALF)
    return table, np.swapaxes(table, 1, 2).copy()


def row_order():
    row = np.arange(WIRES)
    place = row - 320
    late = np.where(place % 32 < 20, 320 + place // 32 * 20 + place % 32, 420 + place // 32 * 12 + place % 32 - 20)
    return np.where(row < 320, row, late).astype(np.int32)


def rank_kernel(plane_ref, base_ref, cross_ref, place_ref, count_ref):
    tri_row = lax.broadcasted_iota(jnp.int32, (BLOCK, BLOCK), 0)
    tri_col = lax.broadcasted_iota(jnp.int32, (BLOCK, BLOCK), 1)
    earlier = (tri_row < tri_col).astype(jnp.float32).astype(jnp.bfloat16)
    names = lax.broadcasted_iota(jnp.int32, (2 * SLABS, BLOCK), 0)
    pair_base = base_ref[0]
    cross_side = cross_ref[0]
    chan_count = plane_ref.shape[1]
    local = plane_ref[...] - pair_base
    is_cross = (local // SLABS == cross_side).astype(jnp.float32)
    cross_count = jnp.sum(is_cross, axis=1, keepdims=True) * (1.0 / SLABS)
    before = jnp.zeros((2 * SLABS, 1), jnp.float32)
    for block in range(chan_count // BLOCK):
        part = slice(block * BLOCK, (block + 1) * BLOCK)
        member = (names == local[:, part]).astype(jnp.float32)
        prefix = dot(member.astype(jnp.bfloat16), earlier) + before
        rank = jnp.sum(member * prefix, axis=0, keepdims=True)
        before = before + jnp.sum(member, axis=1, keepdims=True)
        order = (rank + (1.0 - is_cross[:, part]) * cross_count).astype(jnp.int32)
        near = order - 320
        far = order - 420
        near_piece = (near * 205) >> 12
        far_piece = (far * 171) >> 11
        near_row = 320 + near_piece * 32 + (near - near_piece * 20)
        far_row = 340 + far_piece * 32 + (far - far_piece * 12)
        row = jnp.where(order < 320, order, jnp.where(order < 420, near_row, far_row))
        place_ref[:, part] = (local[:, part] % SLABS) * WIRES + row
    count_ref[...] = jnp.broadcast_to(cross_count.astype(jnp.int32), count_ref.shape)


def rank_rows(chan_plane, pair_base, cross_side):
    chan_count = chan_plane.shape[0]
    scalar = pl.BlockSpec(memory_space=pltpu.SMEM)
    whole = pl.BlockSpec(memory_space=pltpu.VMEM)
    place, count = pl.pallas_call(
        rank_kernel,
        in_specs=[whole, scalar, scalar],
        out_specs=[whole, whole],
        out_shape=[
            jax.ShapeDtypeStruct((1, chan_count), jnp.int32),
            jax.ShapeDtypeStruct((8, 128), jnp.int32),
        ],
        compiler_params=roomy(16),
        name="rank_rows",
    )(chan_plane[None, :], pair_base[None], cross_side[None])
    return place[0], count[0, 0]


def pack_kernel(place_ref, group_ref, good_ref, raw_ref, out0, out1, out2, common_ref, source_ref, rows_ref):
    step = pl.program_id(0)
    first = step * BLOCK

    @pl.when(step == 0)
    def clear():
        common_ref[...] = jnp.zeros_like(common_ref)

    group_count = common_ref.shape[0]
    names = lax.broadcasted_iota(jnp.int32, (group_count, BLOCK), 0)
    member = jnp.where(names == group_ref[0], good_ref[0], 0.0).astype(jnp.bfloat16)
    high, low = split(raw_ref[...])
    common_ref[...] += dot(member, high) + dot(member, low)
    for row in range(BLOCK):
        place = place_ref[first + row]
        rows_ref[pl.ds(place, 1), pl.ds(0, SLAB)] = raw_ref[pl.ds(row, 1), :]
        source_ref[place] = first + row

    @pl.when(step == pl.num_programs(0) - 1)
    def lay():
        def one_slot(slot, carry):
            start = pl.multiple_of(slot * WIRES, PIECE)
            for which, out in enumerate((out0, out1, out2)):
                for piece in range(LANES):
                    at = start + (which * LANES + piece) * PIECE
                    out[slot, :, piece * SLAB : (piece + 1) * SLAB] = rows_ref[pl.ds(at, PIECE), pl.ds(0, SLAB)]
            return carry

        lax.fori_loop(0, SLABS, one_slot, 0)


def pack_rows(raw, place, local_group, good_mask):
    chan_count = raw.shape[0]
    group_count = chan_count // GROUP
    steps = chan_count // BLOCK
    packed = jax.ShapeDtypeStruct((SLABS, PIECE, WIDE), jnp.float32)
    fixed = pl.BlockSpec((SLABS, PIECE, WIDE), lambda step, table: (0, 0, 0))
    line = pl.BlockSpec((1, 1, BLOCK), lambda step, table: (step, 0, 0))
    return pl.pallas_call(
        pack_kernel,
        grid_spec=pltpu.PrefetchScalarGridSpec(
            num_scalar_prefetch=1,
            grid=(steps,),
            in_specs=[line, line, pl.BlockSpec((BLOCK, SLAB), lambda step, table: (step, 0))],
            out_specs=[
                fixed,
                fixed,
                fixed,
                pl.BlockSpec((group_count, SLAB), lambda step, table: (0, 0)),
                pl.BlockSpec(memory_space=pltpu.SMEM),
            ],
            scratch_shapes=[pltpu.VMEM((chan_count, 128), jnp.float32)],
        ),
        out_shape=[
            packed,
            packed,
            packed,
            jax.ShapeDtypeStruct((group_count, SLAB), jnp.float32),
            jax.ShapeDtypeStruct((chan_count,), jnp.int32),
        ],
        compiler_params=roomy(40),
        name="pack_rows",
    )(place, local_group.reshape(steps, 1, BLOCK), good_mask.reshape(steps, 1, BLOCK), raw)


def clean_kernel(rows_ref, common_ref, member_ref, good_ref, out_ref, spread_ref, weight_ref, keep_ref):
    member = member_ref[...]

    def gather(slab, sums):
        covar, power = sums
        high, low = split(common_ref[slab])
        spread = dot(member, high) + dot(member, low)
        for piece in range(LANES):
            spread_ref[slab, :, piece * SLAB : (piece + 1) * SLAB] = spread[piece * PIECE : (piece + 1) * PIECE]
        value = rows_ref[slab]
        grouped = spread_ref[slab]
        return covar + value * grouped, power + grouped * grouped

    zero = jnp.zeros((PIECE, WIDE), jnp.float32)
    covar, power = lax.fori_loop(0, SLABS, gather, (zero, zero))
    for piece in range(LANES):
        part = slice(piece * SLAB, (piece + 1) * SLAB)
        covar_row = jnp.sum(covar[:, part], axis=1, keepdims=True) / TICKS
        power_row = jnp.sum(power[:, part], axis=1, keepdims=True) / TICKS
        weight = covar_row / (power_row + epsilon_power)
        weight_ref[:, part] = jnp.broadcast_to(weight, (PIECE, SLAB))
        keep_ref[:, part] = jnp.broadcast_to(good_ref[piece * PIECE : (piece + 1) * PIECE, :], (PIECE, SLAB))

    def apply(slab, carry):
        out_ref[slab] = keep_ref[...] * (rows_ref[slab] - weight_ref[...] * spread_ref[slab])
        return carry

    lax.fori_loop(0, SLABS, apply, 0)


def clean_rows(rows, commons, member, good):
    whole = pl.BlockSpec(memory_space=pltpu.VMEM)
    return pl.pallas_call(
        clean_kernel,
        in_specs=[whole] * 4,
        out_specs=whole,
        out_shape=jax.ShapeDtypeStruct(rows.shape, jnp.float32),
        scratch_shapes=[
            pltpu.VMEM(rows.shape, jnp.float32),
            pltpu.VMEM((PIECE, WIDE), jnp.float32),
            pltpu.VMEM((PIECE, WIDE), jnp.float32),
        ],
        compiler_params=roomy(24),
        name="clean_rows",
    )(rows, commons, member, good)


def wire_kernel_forward(own0, own1, own2, got0, got1, got2, take_ref, high_ref, low_ref, out_ref, rows_ref):
    @pl.when(pl.program_id(0) == 0)
    def clear():
        rows_ref[...] = jnp.zeros_like(rows_ref)

    for slab in range(2):
        for which, (own, got) in enumerate(((own0, got0), (own1, got1), (own2, got2))):
            sent = SENT[which]
            for piece in range(LANES):
                part = slice(piece * SLAB, (piece + 1) * SLAB)
                at = (which * LANES + piece) * PIECE
                mine = own[slab, :, part]
                theirs = got[slab, :, part]
                take = take_ref[at : at + sent, :] > 0.5
                lanes = slice(slab * PART, slab * PART + SLAB)
                rows_ref[at : at + sent, lanes] = jnp.where(take, theirs, mine[:sent])
                if sent < PIECE:
                    rows_ref[at + sent : at + PIECE, lanes] = mine[sent:]
    row_high, row_low = split(rows_ref[...])
    result = three_dot(high_ref[...], low_ref[...], row_high, row_low)
    for slab in range(2):
        for part in range(2):
            out_ref[slab, part] = result[part * HALF : (part + 1) * HALF, slab * PART : (slab + 1) * PART]


def wire_forward(own, got, take, high, low):
    def slabs(size):
        return pl.BlockSpec((2, size, WIDE), lambda step: (step, 0, 0))

    fixed = pl.BlockSpec((2 * HALF, WIRES), lambda step: (0, 0))
    return pl.pallas_call(
        wire_kernel_forward,
        grid=(SLABS // 2,),
        in_specs=[slabs(PIECE)] * 3
        + [slabs(size) for size in SENT]
        + [pl.BlockSpec((WIRES, 1), lambda step: (0, 0)), fixed, fixed],
        out_specs=pl.BlockSpec((2, 2, HALF, PART), lambda step: (step, 0, 0, 0)),
        out_shape=jax.ShapeDtypeStruct((SLABS, 2, HALF, PART), jnp.float32),
        scratch_shapes=[pltpu.VMEM((WIRES, 2 * PART), jnp.float32)],
        compiler_params=roomy(24),
        name="wire_forward",
    )(*own, *got, take, high, low)


def add(first, second):
    return (first[0] + second[0], first[1] + second[1])


def sub(first, second):
    return (first[0] - second[0], first[1] - second[1])


def turn(value, sign):
    if sign < 0:
        return (value[1], -value[0])
    return (-value[1], value[0])


def scaled(value, angle):
    real, imag = math.cos(angle), math.sin(angle)
    if abs(angle) < 1e-12:
        return value
    return (value[0] * real - value[1] * imag, value[0] * imag + value[1] * real)


def four_point(items, sign):
    even_sum, even_diff = add(items[0], items[2]), sub(items[0], items[2])
    odd_sum, odd_diff = add(items[1], items[3]), turn(sub(items[1], items[3]), sign)
    return [add(even_sum, odd_sum), add(even_diff, odd_diff), sub(even_sum, odd_sum), sub(even_diff, odd_diff)]


def eighth(value, count, sign):
    root = math.sqrt(0.5)
    if count == 0:
        return value
    if count == 2:
        return turn(value, sign)
    real, imag = value
    if count == 1:
        return ((real - sign * imag) * root, (imag + sign * real) * root)
    return ((-real - sign * imag) * root, (sign * real - imag) * root)


def eight_point(items, sign):
    even = four_point(items[0::2], sign)
    odd = four_point(items[1::2], sign)
    odd = [eighth(value, count, sign) for count, value in enumerate(odd)]
    return [add(even[k], odd[k]) for k in range(4)] + [sub(even[k], odd[k]) for k in range(4)]


def slab_points(load, store, middle_ref, sign):
    for low in range(8):
        outs = four_point([load(8 * high + low) for high in range(4)], sign)
        for k, value in enumerate(outs):
            value = scaled(value, sign * 2.0 * math.pi * low * k / 32)
            middle_ref[8 * k + low, 0] = value[0]
            middle_ref[8 * k + low, 1] = value[1]
    for k in range(4):
        outs = eight_point([(middle_ref[8 * k + low, 0], middle_ref[8 * k + low, 1]) for low in range(8)], sign)
        for big, value in enumerate(outs):
            store(k + 4 * big, value)


ROWS = 32


def slab_kernel_forward(in_ref, out_ref, middle_ref):
    def some(index, carry):
        rows = pl.ds(pl.multiple_of(index * 8, 8), 8)

        def load(item):
            return (in_ref[item, 0, rows, :], in_ref[item, 1, rows, :])

        def store(item, value):
            out_ref[item, rows, 0:PART] = value[0]
            out_ref[item, rows, PART : 2 * PART] = value[1]

        slab_points(load, store, middle_ref, -1)
        return carry

    lax.fori_loop(0, ROWS // 8, some, 0)


def slab_kernel_backward(in_ref, out_ref, middle_ref):
    def some(index, carry):
        rows = pl.ds(pl.multiple_of(index * 8, 8), 8)

        def load(item):
            return (in_ref[item, rows, 0:PART], in_ref[item, rows, PART : 2 * PART])

        def store(item, value):
            out_ref[item, 0, rows, :] = value[0]
            out_ref[item, 1, rows, :] = value[1]

        slab_points(load, store, middle_ref, 1)
        return carry

    lax.fori_loop(0, ROWS // 8, some, 0)


def slab_transform(data, forward):
    parted = pl.BlockSpec((SLABS, 2, ROWS, PART), lambda step: (0, 0, step, 0))
    joined = pl.BlockSpec((SLABS, ROWS, HALF), lambda step: (0, step, 0))
    shape = (SLABS, HALF, HALF) if forward else (SLABS, 2, HALF, PART)
    return pl.pallas_call(
        slab_kernel_forward if forward else slab_kernel_backward,
        grid=(HALF // ROWS,),
        in_specs=[parted if forward else joined],
        out_specs=joined if forward else parted,
        out_shape=jax.ShapeDtypeStruct(shape, jnp.float32),
        scratch_shapes=[pltpu.VMEM((SLABS, 2, 8, PART), jnp.float32)],
        compiler_params=roomy(24),
        name="slab_forward" if forward else "slab_backward",
    )(data)


def filter_kernel(in_ref, high_ref, low_ref, filter_ref, back_high_ref, back_low_ref, out_ref):
    for item in range(in_ref.shape[0]):
        data_high, data_low = split(in_ref[item])
        spectrum = three_dot(data_high, data_low, high_ref[item], low_ref[item])
        real, imag = spectrum[:, :PART], spectrum[:, PART:]
        filter_real, filter_imag = filter_ref[item, :, :PART], filter_ref[item, :, PART:]
        mixed = jnp.concatenate(
            [real * filter_real - imag * filter_imag, real * filter_imag + imag * filter_real], axis=1
        )
        mixed_high, mixed_low = split(mixed)
        out_ref[item] = three_dot(mixed_high, mixed_low, back_high_ref[item], back_low_ref[item])


def filter_ticks(data, high, low, filters, back_high, back_low):
    some = pl.BlockSpec((2, HALF, HALF), lambda step: (step, 0, 0))
    return pl.pallas_call(
        filter_kernel,
        grid=(SLABS // 2,),
        in_specs=[some] * 6,
        out_specs=some,
        out_shape=jax.ShapeDtypeStruct((SLABS, HALF, HALF), jnp.float32),
        compiler_params=roomy(24),
        name="filter_ticks",
    )(data, high, low, filters, back_high, back_low)


def wire_kernel_backward(in_ref, high_ref, low_ref, out_ref):
    for pair in range(SLABS // 2):
        both = jnp.concatenate(
            [in_ref[2 * pair + slab].reshape(2 * HALF, PART) for slab in range(2)], axis=1
        )
        data_high, data_low = split(both)
        result = three_dot(high_ref[...], low_ref[...], data_high, data_low)
        for slab in range(2):
            at = (2 * pair + slab) * SLAB
            out_ref[:, at : at + SLAB] = result[:, slab * PART : slab * PART + SLAB]


def wire_backward(data, high, low):
    whole = pl.BlockSpec(memory_space=pltpu.VMEM)
    return pl.pallas_call(
        wire_kernel_backward,
        in_specs=[whole] * 3,
        out_specs=whole,
        out_shape=jax.ShapeDtypeStruct((WIRES, TICKS), jnp.float32),
        compiler_params=roomy(40),
        name="wire_backward",
    )(data, high, low)


def make_filter(wire_kernel, time_kernel):
    forward, _ = wire_tables()
    wire_resp = jnp.dot(forward.astype(np.float32), wire_kernel, precision=highest).reshape(2, 1, HALF, 1)
    first = np.arange(SLABS)
    angle = 2.0 * np.pi * (np.outer(first, first) % SLABS) / SLABS
    slabs = time_kernel.reshape(SLABS, SLAB)
    real = jnp.dot(np.cos(angle).astype(np.float32), slabs, precision=highest)
    imag = jnp.dot(-np.sin(angle).astype(np.float32), slabs, precision=highest)
    twist = 2.0 * np.pi * np.outer(first, np.arange(SLAB)) / TICKS
    cosine, sine = np.cos(twist).astype(np.float32), np.sin(twist).astype(np.float32)
    real, imag = real * cosine + imag * sine, imag * cosine - real * sine
    inner = np.arange(SLAB)
    angle = 2.0 * np.pi * (np.outer(inner, inner) % SLAB) / SLAB
    cosine, sine = np.cos(angle).astype(np.float32), np.sin(angle).astype(np.float32)
    both = jnp.dot(
        jnp.concatenate([real, imag], axis=1),
        np.block([[cosine, -sine], [sine, cosine]]).astype(np.float32),
        precision=highest,
    )
    time_resp = jnp.pad(both.reshape(SLABS, 2, SLAB), ((0, 0), (0, 0), (0, PART - SLAB)))
    time_real, time_imag = time_resp[:, 0][:, None, :], time_resp[:, 1][:, None, :]
    real = wire_resp[0] * time_real - wire_resp[1] * time_imag
    imag = wire_resp[0] * time_imag + wire_resp[1] * time_real
    denominator = real * real + imag * imag + regular_term
    return jnp.concatenate([real / denominator, -imag / denominator], axis=2)


def deconvolve(own, got, take, wires, filters):
    wire_high, wire_low = two_halves(wire_tables()[0])
    picked = (jnp.arange(WIRES, dtype=jnp.int32)[:, None] == wires[None, :]).astype(jnp.bfloat16)
    high = dot(jnp.asarray(wire_high), picked).astype(jnp.bfloat16)
    low = dot(jnp.asarray(wire_low), picked).astype(jnp.bfloat16)
    back_high, back_low = two_halves(wire_tables()[1])
    tick_forward, tick_backward = tick_tables()
    spectrum = wire_forward(own, got, take, high, low)
    spectrum = slab_transform(spectrum, True)
    spectrum = filter_ticks(spectrum, *two_halves(tick_forward), filters, *two_halves(tick_backward))
    spectrum = slab_transform(spectrum, False)
    return wire_backward(spectrum, back_high, back_low)


def shards(raw, bad, group_id, chan_plane, chan_wire, plane_offset, wire_kernel, time_kernel):
    chan_count = raw.shape[0]
    group_count = chan_count // GROUP
    apa_index = lax.axis_index("apa")
    tick_index = lax.axis_index("tick")
    swap = [(i, i ^ 1) for i in range(lax.axis_size("apa"))]
    local_group = group_id - apa_index * group_count
    good_mask = 1.0 - bad.astype(jnp.float32)
    pair_base = (apa_index // 2 * 2 * SLABS).astype(jnp.int32)
    cross_side = (1 - apa_index % 2).astype(jnp.int32)
    place, cross_count = rank_rows(chan_plane, pair_base, cross_side)
    *packed, common, source = pack_rows(raw, place, local_group, good_mask)
    commons = lax.all_gather(common, "tick")
    mine = lax.dynamic_slice(source, (tick_index * WIRES,), (WIRES,))
    row_group = jnp.take(local_group, mine)
    row_good = jnp.take(good_mask, mine)[:, None]
    row_plane = jnp.take(chan_plane, mine)
    row_wire = (jnp.take(chan_wire, mine) + jnp.take(plane_offset, row_plane)) % WIRES
    member = (row_group[:, None] == jnp.arange(group_count, dtype=jnp.int32)[None, :]).astype(jnp.bfloat16)
    take = jnp.asarray(row_order()) < cross_count
    wires = jnp.where(take, lax.ppermute(row_wire, "apa", swap), row_wire)
    filters = make_filter(wire_kernel, time_kernel)
    own, got = [], []
    for which, rows in enumerate(packed):
        rows = lax.all_to_all(rows, "tick", split_axis=0, concat_axis=0, tiled=True)
        part = slice(which * PIECE * LANES, (which + 1) * PIECE * LANES)
        cleaned = clean_rows(rows, commons, member[part], row_good[part])
        own.append(cleaned)
        got.append(lax.ppermute(cleaned[:, : SENT[which]], "apa", swap))
    return deconvolve(own, got, take.astype(jnp.float32)[:, None], wires, filters)[None]


def solution(mesh):
    placed = (P("apa", "tick"), P("apa"), P("apa"), P("apa"), P("apa"), P(), P(), P())
    return jax.shard_map(
        shards,
        mesh=mesh,
        in_specs=placed,
        out_specs=P(("apa", "tick"), None, None),
        check_vma=False,
    )
```

```python
import math

import jax
import jax.numpy as jnp
import ml_dtypes
import numpy as np
from jax import lax
from jax.experimental import pallas as pl
from jax.experimental.pallas import tpu as pltpu
from jax.sharding import PartitionSpec as P

TICKS = 3200
GROUP = 128
WIRES = 480
SLABS = 32
SLAB = 100
PART = 128
HALF = 256
EARLY = 40
LATE = 60
EARLY_ROWS = 160
LATE_ROWS = 80
BLOCK = 256
SENT = (80, 80, 56)

highest = lax.Precision.HIGHEST
epsilon_power = 1e-06
regular_term = 0.25
mega = 1024 * 1024


def roomy(size):
    return pltpu.CompilerParams(vmem_limit_bytes=size * mega)


def two_halves(table):
    high = table.astype(ml_dtypes.bfloat16)
    low = (table - high.astype(np.float64)).astype(ml_dtypes.bfloat16)
    return high, low


def split(value):
    high = value.astype(jnp.bfloat16)
    low = (value - high.astype(jnp.float32)).astype(jnp.bfloat16)
    return high, low


def dot(left, right):
    return jnp.dot(left, right, preferred_element_type=jnp.float32)


def three_dot(left_high, left_low, right_high, right_low):
    return dot(left_high, right_high) + (dot(left_high, right_low) + dot(left_low, right_high))


def wire_tables():
    spread = np.outer(np.arange(WIRES // 2 + 1), np.arange(WIRES)) % WIRES
    angle = 2.0 * np.pi * spread / WIRES
    forward = np.zeros((2, HALF, WIRES))
    forward[0, : WIRES // 2 + 1] = np.cos(angle)
    forward[1, : WIRES // 2 + 1] = -np.sin(angle)
    weight = np.full((WIRES // 2 + 1, 1), 2.0)
    weight[0] = weight[-1] = 1.0
    weight /= WIRES * TICKS
    backward = np.zeros((2, HALF, WIRES))
    backward[0, : WIRES // 2 + 1] = weight * np.cos(angle)
    backward[1, : WIRES // 2 + 1] = -weight * np.sin(angle)
    return forward.reshape(2 * HALF, WIRES), backward.reshape(2 * HALF, WIRES).T.copy()


def tick_tables():
    first = np.arange(SLABS)[:, None, None]
    inner = np.arange(SLAB)[None, :, None]
    second = np.arange(SLAB)[None, None, :]
    angle = 2.0 * np.pi * ((inner * first + SLABS * inner * second) % TICKS) / TICKS
    table = np.zeros((SLABS, 2, PART, 2, PART))
    table[:, 0, :SLAB, 0, :SLAB] = np.cos(angle)
    table[:, 1, :SLAB, 1, :SLAB] = np.cos(angle)
    table[:, 0, :SLAB, 1, :SLAB] = -np.sin(angle)
    table[:, 1, :SLAB, 0, :SLAB] = np.sin(angle)
    table = table.reshape(SLABS, HALF, HALF)
    return table, np.swapaxes(table, 1, 2).copy()


def row_order():
    row = np.arange(WIRES)
    piece = (row >= 400).astype(np.int32)
    place = row - 320 - 80 * piece
    late = np.where(place < 50, 320 + 50 * piece + place, 420 + 30 * piece + place - 50)
    return np.where(row < 320, row, late).astype(np.int32)


def rank_kernel(plane_ref, base_ref, cross_ref, place_ref, count_ref):
    tri_row = lax.broadcasted_iota(jnp.int32, (BLOCK, BLOCK), 0)
    tri_col = lax.broadcasted_iota(jnp.int32, (BLOCK, BLOCK), 1)
    earlier = (tri_row < tri_col).astype(jnp.float32).astype(jnp.bfloat16)
    names = lax.broadcasted_iota(jnp.int32, (2 * SLABS, BLOCK), 0)
    pair_base = base_ref[0]
    cross_side = cross_ref[0]
    chan_count = plane_ref.shape[1]
    local = plane_ref[...] - pair_base
    is_cross = (local // SLABS == cross_side).astype(jnp.float32)
    cross_count = jnp.sum(is_cross, axis=1, keepdims=True) * (1.0 / SLABS)
    before = jnp.zeros((2 * SLABS, 1), jnp.float32)
    for block in range(chan_count // BLOCK):
        part = slice(block * BLOCK, (block + 1) * BLOCK)
        member = (names == local[:, part]).astype(jnp.float32)
        prefix = dot(member.astype(jnp.bfloat16), earlier) + before
        rank = jnp.sum(member * prefix, axis=0, keepdims=True)
        before = before + jnp.sum(member, axis=1, keepdims=True)
        order = (rank + (1.0 - is_cross[:, part]) * cross_count).astype(jnp.int32)
        near_row = order + jnp.where(order >= 370, 30, 0)
        far_row = order - 50 + jnp.where(order >= 450, 50, 0)
        row = jnp.where(order < 320, order, jnp.where(order < 420, near_row, far_row))
        place_ref[:, part] = (local[:, part] % SLABS) * WIRES + row
    count_ref[...] = jnp.broadcast_to(cross_count.astype(jnp.int32), count_ref.shape)


def rank_rows(chan_plane, pair_base, cross_side):
    chan_count = chan_plane.shape[0]
    scalar = pl.BlockSpec(memory_space=pltpu.SMEM)
    whole = pl.BlockSpec(memory_space=pltpu.VMEM)
    place, count = pl.pallas_call(
        rank_kernel,
        in_specs=[whole, scalar, scalar],
        out_specs=[whole, whole],
        out_shape=[
            jax.ShapeDtypeStruct((1, chan_count), jnp.int32),
            jax.ShapeDtypeStruct((8, 128), jnp.int32),
        ],
        compiler_params=roomy(16),
        name="rank_rows",
    )(chan_plane[None, :], pair_base[None], cross_side[None])
    return place[0], count[0, 0]


def lay_early(slot, rows_ref):
    start = pl.multiple_of(slot * WIRES, 32)
    for piece in range(3):
        yield piece, rows_ref[pl.ds(start + piece * EARLY_ROWS, EARLY_ROWS), 0:EARLY]


def pack_kernel(place_ref, group_ref, good_ref, raw_ref, early, out0, out1, out2, common_ref, source_ref, rows_ref, turn_ref):
    step = pl.program_id(0)
    first = step * BLOCK

    @pl.when(step == 0)
    def clear():
        common_ref[...] = jnp.zeros_like(common_ref)

    turn_ref[:, 0:SLAB] = raw_ref[...].T
    group_count = common_ref.shape[0]
    names = lax.broadcasted_iota(jnp.int32, (group_count, BLOCK), 0)
    member = jnp.where(names == group_ref[0], good_ref[0], 0.0).astype(jnp.bfloat16)
    high, low = split(turn_ref[:, 0:SLAB])
    common_ref[...] += dot(member, high) + dot(member, low)
    for row in range(BLOCK):
        place = place_ref[first + row]
        rows_ref[pl.ds(place, 1), :] = turn_ref[pl.ds(row, 1), :]
        source_ref[place] = first + row

    @pl.when(step == pl.num_programs(0) - 1)
    def lay():
        def one_slot(slot, carry):
            for piece, value in lay_early(slot, rows_ref):
                early[slot, :, piece * EARLY : (piece + 1) * EARLY] = value
            start = pl.multiple_of(slot * WIRES, 32)
            for which, out in enumerate((out0, out1, out2)):
                for piece in range(2):
                    at = start + (which * 2 + piece) * LATE_ROWS
                    out[slot, :, piece * LATE : (piece + 1) * LATE] = rows_ref[pl.ds(at, LATE_ROWS), EARLY:SLAB]
            return carry

        lax.fori_loop(0, SLABS, one_slot, 0)


def pack_rows(raw_turned, place, local_group, good_mask):
    chan_count = raw_turned.shape[1]
    group_count = chan_count // GROUP
    steps = chan_count // BLOCK
    sizes = (EARLY_ROWS, LATE_ROWS, LATE_ROWS, LATE_ROWS)
    line = pl.BlockSpec((1, 1, BLOCK), lambda step, table: (step, 0, 0))
    return pl.pallas_call(
        pack_kernel,
        grid_spec=pltpu.PrefetchScalarGridSpec(
            num_scalar_prefetch=1,
            grid=(steps,),
            in_specs=[line, line, pl.BlockSpec((SLAB, BLOCK), lambda step, table: (0, step))],
            out_specs=[pl.BlockSpec((SLABS, size, PART), lambda step, table: (0, 0, 0)) for size in sizes]
            + [
                pl.BlockSpec((group_count, SLAB), lambda step, table: (0, 0)),
                pl.BlockSpec(memory_space=pltpu.SMEM),
            ],
            scratch_shapes=[pltpu.VMEM((chan_count, PART), jnp.float32), pltpu.VMEM((BLOCK, PART), jnp.float32)],
        ),
        out_shape=[jax.ShapeDtypeStruct((SLABS, size, PART), jnp.float32) for size in sizes]
        + [
            jax.ShapeDtypeStruct((group_count, SLAB), jnp.float32),
            jax.ShapeDtypeStruct((chan_count,), jnp.int32),
        ],
        compiler_params=roomy(40),
        name="pack_rows",
    )(place, local_group.reshape(steps, 1, BLOCK), good_mask.reshape(steps, 1, BLOCK), raw_turned)


def merge_kernel(place_ref, raw_ref, own_ref, take_ref, out_ref, rows_ref, turn_ref):
    step = pl.program_id(0)
    first = step * BLOCK
    turn_ref[:, 0:EARLY] = raw_ref[...].T
    for row in range(BLOCK):
        place = place_ref[first + row]
        rows_ref[pl.ds(place, 1), :] = turn_ref[pl.ds(row, 1), :]

    @pl.when(step == pl.num_programs(0) - 1)
    def lay():
        def one_slot(slot, carry):
            for piece, value in lay_early(slot, rows_ref):
                part = slice(piece * EARLY, (piece + 1) * EARLY)
                take = take_ref[piece * EARLY_ROWS : (piece + 1) * EARLY_ROWS, :] > 0.5
                out_ref[slot, :, part] = jnp.where(take, value, own_ref[slot, :, part])
            return carry

        lax.fori_loop(0, SLABS, one_slot, 0)


def merge_rows(raw_turned, place, own, take):
    chan_count = raw_turned.shape[1]
    steps = chan_count // BLOCK
    fixed = pl.BlockSpec((SLABS, EARLY_ROWS, PART), lambda step, table: (0, 0, 0))
    return pl.pallas_call(
        merge_kernel,
        grid_spec=pltpu.PrefetchScalarGridSpec(
            num_scalar_prefetch=1,
            grid=(steps,),
            in_specs=[
                pl.BlockSpec((EARLY, BLOCK), lambda step, table: (0, step)),
                fixed,
                pl.BlockSpec((WIRES, 1), lambda step, table: (0, 0)),
            ],
            out_specs=fixed,
            scratch_shapes=[pltpu.VMEM((chan_count, PART), jnp.float32), pltpu.VMEM((BLOCK, PART), jnp.float32)],
        ),
        out_shape=jax.ShapeDtypeStruct((SLABS, EARLY_ROWS, PART), jnp.float32),
        compiler_params=roomy(32),
        name="merge_rows",
    )(place, raw_turned, own, take)


def spread_common(common_ref, member, both_ref):
    for slab in range(2):
        both_ref[:, slab * PART : slab * PART + SLAB] = common_ref[slab]
    high, low = split(both_ref[...])
    return dot(member, high) + dot(member, low)


def weigh_kernel(early, own0, own1, own2, got0, got1, got2, take_ref, common_ref, member_ref, out_ref, weight_ref, both_ref, covar_ref, power_ref):
    step = pl.program_id(0)

    @pl.when(step == 0)
    def clear():
        both_ref[...] = jnp.zeros_like(both_ref)
        covar_ref[...] = jnp.zeros_like(covar_ref)
        power_ref[...] = jnp.zeros_like(power_ref)

    for slab in range(2):
        base = slab * PART
        out_ref[0, :, base + SLAB : base + PART] = jnp.zeros((WIRES, PART - SLAB), jnp.float32)
        for piece in range(3):
            rows = slice(piece * EARLY_ROWS, (piece + 1) * EARLY_ROWS)
            out_ref[0, rows, base : base + EARLY] = early[slab, :, piece * EARLY : (piece + 1) * EARLY]
        for which, (own, got) in enumerate(((own0, got0), (own1, got1), (own2, got2))):
            sent = SENT[which]
            for piece in range(2):
                part = slice(piece * LATE, (piece + 1) * LATE)
                at = (which * 2 + piece) * LATE_ROWS
                take = take_ref[at : at + sent, :] > 0.5
                lanes = slice(base + EARLY, base + SLAB)
                out_ref[0, at : at + sent, lanes] = jnp.where(take, got[slab, :, part], own[slab, 0:sent, part])
                if sent < LATE_ROWS:
                    out_ref[0, at + sent : at + LATE_ROWS, lanes] = own[slab, sent:LATE_ROWS, part]
    spread = spread_common(common_ref, member_ref[...], both_ref)
    covar_ref[...] += out_ref[0] * spread
    power_ref[...] += spread * spread

    @pl.when(step == pl.num_programs(0) - 1)
    def close():
        covar = jnp.sum(covar_ref[...], axis=1, keepdims=True) / TICKS
        power = jnp.sum(power_ref[...], axis=1, keepdims=True) / TICKS
        weight_ref[...] = covar / (power + epsilon_power)


def weigh_rows(early, own, got, take, commons, member):
    def slabs(size, lanes=PART):
        return pl.BlockSpec((2, size, lanes), lambda step: (step, 0, 0))

    def fixed(*shape):
        return pl.BlockSpec(shape, lambda step: (0,) * len(shape))

    pair_groups = commons.shape[1]
    return pl.pallas_call(
        weigh_kernel,
        grid=(SLABS // 2,),
        in_specs=[slabs(EARLY_ROWS)]
        + [slabs(LATE_ROWS)] * 3
        + [slabs(size) for size in SENT]
        + [fixed(WIRES, 1), slabs(pair_groups, SLAB), fixed(WIRES, pair_groups)],
        out_specs=[pl.BlockSpec((1, WIRES, HALF), lambda step: (step, 0, 0)), fixed(WIRES, 1)],
        out_shape=[
            jax.ShapeDtypeStruct((SLABS // 2, WIRES, HALF), jnp.float32),
            jax.ShapeDtypeStruct((WIRES, 1), jnp.float32),
        ],
        scratch_shapes=[
            pltpu.VMEM((pair_groups, HALF), jnp.float32),
            pltpu.VMEM((WIRES, HALF), jnp.float32),
            pltpu.VMEM((WIRES, HALF), jnp.float32),
        ],
        compiler_params=roomy(24),
        name="weigh_rows",
    )(early, *own, *got, take, commons, member)


def wire_kernel_forward(rows_ref, weight_ref, good_ref, common_ref, member_ref, high_ref, low_ref, out_ref, both_ref):
    @pl.when(pl.program_id(0) == 0)
    def clear():
        both_ref[...] = jnp.zeros_like(both_ref)

    spread = spread_common(common_ref, member_ref[...], both_ref)
    cleaned = good_ref[...] * (rows_ref[0] - weight_ref[...] * spread)
    row_high, row_low = split(cleaned)
    result = three_dot(high_ref[...], low_ref[...], row_high, row_low)
    for slab in range(2):
        for part in range(2):
            out_ref[slab, part] = result[part * HALF : (part + 1) * HALF, slab * PART : (slab + 1) * PART]


def wire_forward(rows, weight, good, commons, member, high, low):
    def fixed(*shape):
        return pl.BlockSpec(shape, lambda step: (0,) * len(shape))

    pair_groups = commons.shape[1]
    return pl.pallas_call(
        wire_kernel_forward,
        grid=(SLABS // 2,),
        in_specs=[
            pl.BlockSpec((1, WIRES, HALF), lambda step: (step, 0, 0)),
            fixed(WIRES, 1),
            fixed(WIRES, 1),
            pl.BlockSpec((2, pair_groups, SLAB), lambda step: (step, 0, 0)),
            fixed(WIRES, pair_groups),
            fixed(2 * HALF, WIRES),
            fixed(2 * HALF, WIRES),
        ],
        out_specs=pl.BlockSpec((2, 2, HALF, PART), lambda step: (step, 0, 0, 0)),
        out_shape=jax.ShapeDtypeStruct((SLABS, 2, HALF, PART), jnp.float32),
        scratch_shapes=[pltpu.VMEM((pair_groups, HALF), jnp.float32)],
        compiler_params=roomy(24),
        name="wire_forward",
    )(rows, weight, good, commons, member, high, low)


def add(first, second):
    return (first[0] + second[0], first[1] + second[1])


def sub(first, second):
    return (first[0] - second[0], first[1] - second[1])


def turn(value, sign):
    if sign < 0:
        return (value[1], -value[0])
    return (-value[1], value[0])


def scaled(value, angle):
    real, imag = math.cos(angle), math.sin(angle)
    if abs(angle) < 1e-12:
        return value
    return (value[0] * real - value[1] * imag, value[0] * imag + value[1] * real)


def four_point(items, sign):
    even_sum, even_diff = add(items[0], items[2]), sub(items[0], items[2])
    odd_sum, odd_diff = add(items[1], items[3]), turn(sub(items[1], items[3]), sign)
    return [add(even_sum, odd_sum), add(even_diff, odd_diff), sub(even_sum, odd_sum), sub(even_diff, odd_diff)]


def eighth(value, count, sign):
    root = math.sqrt(0.5)
    if count == 0:
        return value
    if count == 2:
        return turn(value, sign)
    real, imag = value
    if count == 1:
        return ((real - sign * imag) * root, (imag + sign * real) * root)
    return ((-real - sign * imag) * root, (sign * real - imag) * root)


def eight_point(items, sign):
    even = four_point(items[0::2], sign)
    odd = four_point(items[1::2], sign)
    odd = [eighth(value, count, sign) for count, value in enumerate(odd)]
    return [add(even[k], odd[k]) for k in range(4)] + [sub(even[k], odd[k]) for k in range(4)]


def slab_points(load, store, middle_ref, sign):
    for low in range(8):
        outs = four_point([load(8 * high + low) for high in range(4)], sign)
        for k, value in enumerate(outs):
            value = scaled(value, sign * 2.0 * math.pi * low * k / 32)
            middle_ref[8 * k + low, 0] = value[0]
            middle_ref[8 * k + low, 1] = value[1]
    for k in range(4):
        outs = eight_point([(middle_ref[8 * k + low, 0], middle_ref[8 * k + low, 1]) for low in range(8)], sign)
        for big, value in enumerate(outs):
            store(k + 4 * big, value)


ROWS = 32


def slab_kernel_forward(in_ref, out_ref, middle_ref):
    def some(index, carry):
        rows = pl.ds(pl.multiple_of(index * 8, 8), 8)

        def load(item):
            return (in_ref[item, 0, rows, :], in_ref[item, 1, rows, :])

        def store(item, value):
            out_ref[item, rows, 0:PART] = value[0]
            out_ref[item, rows, PART : 2 * PART] = value[1]

        slab_points(load, store, middle_ref, -1)
        return carry

    lax.fori_loop(0, ROWS // 8, some, 0)


def slab_kernel_backward(in_ref, out_ref, middle_ref):
    def some(index, carry):
        rows = pl.ds(pl.multiple_of(index * 8, 8), 8)

        def load(item):
            return (in_ref[item, rows, 0:PART], in_ref[item, rows, PART : 2 * PART])

        def store(item, value):
            out_ref[item, 0, rows, :] = value[0]
            out_ref[item, 1, rows, :] = value[1]

        slab_points(load, store, middle_ref, 1)
        return carry

    lax.fori_loop(0, ROWS // 8, some, 0)


def slab_transform(data, forward):
    parted = pl.BlockSpec((SLABS, 2, ROWS, PART), lambda step: (0, 0, step, 0))
    joined = pl.BlockSpec((SLABS, ROWS, HALF), lambda step: (0, step, 0))
    shape = (SLABS, HALF, HALF) if forward else (SLABS, 2, HALF, PART)
    return pl.pallas_call(
        slab_kernel_forward if forward else slab_kernel_backward,
        grid=(HALF // ROWS,),
        in_specs=[parted if forward else joined],
        out_specs=joined if forward else parted,
        out_shape=jax.ShapeDtypeStruct(shape, jnp.float32),
        scratch_shapes=[pltpu.VMEM((SLABS, 2, 8, PART), jnp.float32)],
        compiler_params=roomy(24),
        name="slab_forward" if forward else "slab_backward",
    )(data)


def filter_kernel(in_ref, high_ref, low_ref, filter_ref, back_high_ref, back_low_ref, out_ref):
    for item in range(in_ref.shape[0]):
        data_high, data_low = split(in_ref[item])
        spectrum = three_dot(data_high, data_low, high_ref[item], low_ref[item])
        real, imag = spectrum[:, :PART], spectrum[:, PART:]
        filter_real, filter_imag = filter_ref[item, :, :PART], filter_ref[item, :, PART:]
        mixed = jnp.concatenate(
            [real * filter_real - imag * filter_imag, real * filter_imag + imag * filter_real], axis=1
        )
        mixed_high, mixed_low = split(mixed)
        out_ref[item] = three_dot(mixed_high, mixed_low, back_high_ref[item], back_low_ref[item])


def filter_ticks(data, high, low, filters, back_high, back_low):
    some = pl.BlockSpec((2, HALF, HALF), lambda step: (step, 0, 0))
    return pl.pallas_call(
        filter_kernel,
        grid=(SLABS // 2,),
        in_specs=[some] * 6,
        out_specs=some,
        out_shape=jax.ShapeDtypeStruct((SLABS, HALF, HALF), jnp.float32),
        compiler_params=roomy(24),
        name="filter_ticks",
    )(data, high, low, filters, back_high, back_low)


def wire_kernel_backward(in_ref, high_ref, low_ref, out_ref):
    for pair in range(SLABS // 2):
        both = jnp.concatenate(
            [in_ref[2 * pair + slab].reshape(2 * HALF, PART) for slab in range(2)], axis=1
        )
        data_high, data_low = split(both)
        result = three_dot(high_ref[...], low_ref[...], data_high, data_low)
        for slab in range(2):
            at = (2 * pair + slab) * SLAB
            out_ref[:, at : at + SLAB] = result[:, slab * PART : slab * PART + SLAB]


def wire_backward(data, high, low):
    whole = pl.BlockSpec(memory_space=pltpu.VMEM)
    return pl.pallas_call(
        wire_kernel_backward,
        in_specs=[whole] * 3,
        out_specs=whole,
        out_shape=jax.ShapeDtypeStruct((WIRES, TICKS), jnp.float32),
        compiler_params=roomy(40),
        name="wire_backward",
    )(data, high, low)


def make_filter(wire_kernel, time_kernel):
    forward, _ = wire_tables()
    wire_resp = jnp.dot(forward.astype(np.float32), wire_kernel, precision=highest).reshape(2, 1, HALF, 1)
    first = np.arange(SLABS)
    angle = 2.0 * np.pi * (np.outer(first, first) % SLABS) / SLABS
    slabs = time_kernel.reshape(SLABS, SLAB)
    real = jnp.dot(np.cos(angle).astype(np.float32), slabs, precision=highest)
    imag = jnp.dot(-np.sin(angle).astype(np.float32), slabs, precision=highest)
    twist = 2.0 * np.pi * np.outer(first, np.arange(SLAB)) / TICKS
    cosine, sine = np.cos(twist).astype(np.float32), np.sin(twist).astype(np.float32)
    real, imag = real * cosine + imag * sine, imag * cosine - real * sine
    inner = np.arange(SLAB)
    angle = 2.0 * np.pi * (np.outer(inner, inner) % SLAB) / SLAB
    cosine, sine = np.cos(angle).astype(np.float32), np.sin(angle).astype(np.float32)
    both = jnp.dot(
        jnp.concatenate([real, imag], axis=1),
        np.block([[cosine, -sine], [sine, cosine]]).astype(np.float32),
        precision=highest,
    )
    time_resp = jnp.pad(both.reshape(SLABS, 2, SLAB), ((0, 0), (0, 0), (0, PART - SLAB)))
    time_real, time_imag = time_resp[:, 0][:, None, :], time_resp[:, 1][:, None, :]
    real = wire_resp[0] * time_real - wire_resp[1] * time_imag
    imag = wire_resp[0] * time_imag + wire_resp[1] * time_real
    denominator = real * real + imag * imag + regular_term
    return jnp.concatenate([real / denominator, -imag / denominator], axis=2)


def picked_tables(wires):
    wire_high, wire_low = two_halves(wire_tables()[0])
    picked = (jnp.arange(WIRES, dtype=jnp.int32)[:, None] == wires[None, :]).astype(jnp.bfloat16)
    return dot(jnp.asarray(wire_high), picked).astype(jnp.bfloat16), dot(jnp.asarray(wire_low), picked).astype(
        jnp.bfloat16
    )


def deconvolve(spectrum, filters):
    back_high, back_low = two_halves(wire_tables()[1])
    tick_forward, tick_backward = tick_tables()
    spectrum = slab_transform(spectrum, True)
    spectrum = filter_ticks(spectrum, *two_halves(tick_forward), filters, *two_halves(tick_backward))
    spectrum = slab_transform(spectrum, False)
    return wire_backward(spectrum, back_high, back_low)


def shards(raw, bad, group_id, chan_plane, chan_wire, plane_offset, wire_kernel, time_kernel):
    chan_count = raw.shape[0]
    group_count = chan_count // GROUP
    apa_index = lax.axis_index("apa")
    tick_index = lax.axis_index("tick")
    parity = apa_index % 2
    swap = [(i, i ^ 1) for i in range(lax.axis_size("apa"))]
    raw_turned = raw.T
    early_got = lax.ppermute(raw_turned[:EARLY], "apa", swap)
    local_group = group_id - apa_index * group_count
    good_mask = 1.0 - bad.astype(jnp.float32)
    pair_base = (apa_index // 2 * 2 * SLABS).astype(jnp.int32)
    place, cross_count = rank_rows(chan_plane, pair_base, (1 - parity).astype(jnp.int32))
    place_got = lax.ppermute(place, "apa", swap)
    early_own, late0, late1, late2, common, source = pack_rows(raw_turned, place, local_group, good_mask)
    common_got = lax.ppermute(common, "apa", swap)
    first = jnp.where(parity == 0, common, common_got)
    second = jnp.where(parity == 0, common_got, common)
    commons = lax.all_gather(jnp.concatenate([first, second], axis=0), "tick")
    mine = lax.dynamic_slice(source, (tick_index * WIRES,), (WIRES,))
    row_group = jnp.take(local_group, mine) + parity * group_count
    row_bad = jnp.take(bad, mine)
    row_plane = jnp.take(chan_plane, mine)
    row_wire = (jnp.take(chan_wire, mine) + jnp.take(plane_offset, row_plane)) % WIRES
    facts = jnp.stack([row_wire, row_group, row_bad])
    take = jnp.asarray(row_order()) < cross_count
    facts = jnp.where(take[None, :], lax.ppermute(facts, "apa", swap), facts)
    row_take = take.astype(jnp.float32)[:, None]
    row_good = 1.0 - facts[2].astype(jnp.float32)[:, None]
    member = (facts[1][:, None] == jnp.arange(2 * group_count, dtype=jnp.int32)[None, :]).astype(jnp.bfloat16)
    high, low = picked_tables(facts[0])
    filters = make_filter(wire_kernel, time_kernel)
    own, got = [], []
    for which, rows in enumerate((late0, late1, late2)):
        rows = lax.all_to_all(rows, "tick", split_axis=0, concat_axis=0, tiled=True)
        own.append(rows)
        got.append(lax.ppermute(rows[:, : SENT[which]], "apa", swap))
    early = merge_rows(early_got, place_got, early_own, row_take)
    early = lax.all_to_all(early, "tick", split_axis=0, concat_axis=0, tiled=True)
    rows, weight = weigh_rows(early, own, got, row_take, commons, member)
    spectrum = wire_forward(rows, weight, row_good, commons, member, high, low)
    return deconvolve(spectrum, filters)[None]


def solution(mesh):
    placed = (P("apa", "tick"), P("apa"), P("apa"), P("apa"), P("apa"), P(), P(), P())
    return jax.shard_map(
        shards,
        mesh=mesh,
        in_specs=placed,
        out_specs=P(("apa", "tick"), None, None),
        check_vma=False,
    )
```

```python
import functools
import math

import jax
import jax.numpy as jnp
import ml_dtypes
import numpy as np
from jax import lax
from jax.experimental import pallas as pl
from jax.experimental.pallas import tpu as pltpu
from jax.sharding import PartitionSpec as P

TICKS = 3200
GROUP = 128
WIRES = 480
SLABS = 32
SLAB = 100
PART = 128
HALF = 256
EARLY = 40
LATE = 60
EARLY_ROWS = 160
LATE_ROWS = 120
BLOCK = 256
WIDE = 512
SENT = (120, 96)

highest = lax.Precision.HIGHEST
epsilon_power = 1e-06
regular_term = 0.25
mega = 1024 * 1024


def roomy(size):
    return pltpu.CompilerParams(vmem_limit_bytes=size * mega)


def two_halves(table):
    high = table.astype(ml_dtypes.bfloat16)
    low = (table - high.astype(np.float64)).astype(ml_dtypes.bfloat16)
    return high, low


def split(value):
    high = value.astype(jnp.bfloat16)
    low = (value - high.astype(jnp.float32)).astype(jnp.bfloat16)
    return high, low


def dot(left, right):
    return jnp.dot(left, right, preferred_element_type=jnp.float32)


def three_dot(left_high, left_low, right_high, right_low):
    return dot(left_high, right_high) + (dot(left_high, right_low) + dot(left_low, right_high))


def wire_tables():
    spread = np.outer(np.arange(WIRES // 2 + 1), np.arange(WIRES)) % WIRES
    angle = 2.0 * np.pi * spread / WIRES
    forward = np.zeros((2, HALF, WIRES))
    forward[0, : WIRES // 2 + 1] = np.cos(angle)
    forward[1, : WIRES // 2 + 1] = -np.sin(angle)
    weight = np.full((WIRES // 2 + 1, 1), 2.0)
    weight[0] = weight[-1] = 1.0
    weight /= WIRES * TICKS
    backward = np.zeros((2, HALF, WIRES))
    backward[0, : WIRES // 2 + 1] = weight * np.cos(angle)
    backward[1, : WIRES // 2 + 1] = -weight * np.sin(angle)
    return forward.reshape(2 * HALF, WIRES), backward.reshape(2 * HALF, WIRES).T.copy()


def tick_tables():
    angle = 2.0 * np.pi * (np.outer(np.arange(SLAB), np.arange(SLAB)) % SLAB) / SLAB
    table = np.zeros((2, PART, 2, PART))
    table[0, :SLAB, 0, :SLAB] = table[1, :SLAB, 1, :SLAB] = np.cos(angle)
    table[0, :SLAB, 1, :SLAB] = -np.sin(angle)
    table[1, :SLAB, 0, :SLAB] = np.sin(angle)
    table = table.reshape(HALF, HALF)
    twist = 2.0 * np.pi * np.outer(np.arange(SLABS), np.arange(PART)) / TICKS
    return table, table.T.copy(), np.stack([np.cos(twist), np.sin(twist)], axis=1).astype(np.float32)[:, :, None, :]


def row_order():
    row = np.arange(WIRES)
    piece = (row >= 360).astype(np.int32)
    place = row - 240 - 120 * piece
    late = np.where(place < 90, 240 + 90 * piece + place, 420 + 30 * piece + place - 90)
    return np.where(row < 240, row, late).astype(np.int32)


def rank_kernel(plane_ref, base_ref, cross_ref, place_ref, count_ref):
    tri_row = lax.broadcasted_iota(jnp.int32, (BLOCK, BLOCK), 0)
    tri_col = lax.broadcasted_iota(jnp.int32, (BLOCK, BLOCK), 1)
    earlier = (tri_row < tri_col).astype(jnp.float32).astype(jnp.bfloat16)
    names = lax.broadcasted_iota(jnp.int32, (2 * SLABS, BLOCK), 0)
    pair_base = base_ref[0]
    cross_side = cross_ref[0]
    chan_count = plane_ref.shape[1]
    local = plane_ref[...] - pair_base
    is_cross = (local // SLABS == cross_side).astype(jnp.float32)
    cross_count = jnp.sum(is_cross, axis=1, keepdims=True) * (1.0 / SLABS)
    before = jnp.zeros((2 * SLABS, 1), jnp.float32)
    for block in range(chan_count // BLOCK):
        part = slice(block * BLOCK, (block + 1) * BLOCK)
        member = (names == local[:, part]).astype(jnp.float32)
        prefix = dot(member.astype(jnp.bfloat16), earlier) + before
        rank = jnp.sum(member * prefix, axis=0, keepdims=True)
        before = before + jnp.sum(member, axis=1, keepdims=True)
        order = (rank + (1.0 - is_cross[:, part]) * cross_count).astype(jnp.int32)
        near_row = order + jnp.where(order >= 330, 30, 0)
        far_row = order - 90 + jnp.where(order >= 450, 90, 0)
        row = jnp.where(order < 240, order, jnp.where(order < 420, near_row, far_row))
        place_ref[:, part] = (local[:, part] % SLABS) * WIRES + row
    count_ref[...] = jnp.broadcast_to(cross_count.astype(jnp.int32), count_ref.shape)


def rank_rows(chan_plane, pair_base, cross_side):
    chan_count = chan_plane.shape[0]
    scalar = pl.BlockSpec(memory_space=pltpu.SMEM)
    whole = pl.BlockSpec(memory_space=pltpu.VMEM)
    place, count = pl.pallas_call(
        rank_kernel,
        in_specs=[whole, scalar, scalar],
        out_specs=[whole, whole],
        out_shape=[
            jax.ShapeDtypeStruct((1, chan_count), jnp.int32),
            jax.ShapeDtypeStruct((8, 128), jnp.int32),
        ],
        compiler_params=roomy(16),
        name="rank_rows",
    )(chan_plane[None, :], pair_base[None], cross_side[None])
    return place[0], count[0, 0]


def whole(count):
    return [pl.BlockSpec(memory_space=pltpu.VMEM)] * count


def turned_scatter(place_ref, raw_ref, rows_ref, even_ref, odd_ref):
    ticks, chan_count = raw_ref.shape
    steps = chan_count // WIDE

    def turn_block(step, to_ref):
        at = pl.multiple_of(step * WIDE, WIDE)
        to_ref[:, 0:ticks] = raw_ref[:, pl.ds(at, WIDE)].T

    def move(step, from_ref):
        first = step * WIDE
        for row in range(WIDE):
            rows_ref[pl.ds(place_ref[first + row], 1), :] = from_ref[pl.ds(row, 1), :]

    turn_block(0, even_ref)

    def both(half, carry):
        turn_block(2 * half + 1, odd_ref)
        move(2 * half, even_ref)
        turn_block(jnp.minimum(2 * half + 2, steps - 2), even_ref)
        move(2 * half + 1, odd_ref)
        return carry

    lax.fori_loop(0, steps // 2, both, 0)


def pack_kernel(place_ref, raw_ref, rows_ref, even_ref, odd_ref):
    turned_scatter(place_ref, raw_ref, rows_ref, even_ref, odd_ref)


def pack_rows(place, raw_turned):
    chan_count = raw_turned.shape[1]
    return pl.pallas_call(
        pack_kernel,
        in_specs=[pl.BlockSpec(memory_space=pltpu.SMEM)] + whole(1),
        out_specs=whole(1)[0],
        out_shape=jax.ShapeDtypeStruct((chan_count, PART), jnp.float32),
        scratch_shapes=[pltpu.VMEM((WIDE, PART), jnp.float32)] * 2,
        compiler_params=roomy(32),
        name="pack_rows",
    )(place, raw_turned)


def late_kernel(which, rows_ref, out_ref):
    def one_slot(slot, carry):
        start = pl.multiple_of(slot * WIRES, 8)
        for piece in range(2):
            at = start + (which * 2 + piece) * LATE_ROWS
            out_ref[slot, :, piece * LATE : (piece + 1) * LATE] = rows_ref[pl.ds(at, LATE_ROWS), EARLY:SLAB]
        return carry

    lax.fori_loop(0, SLABS, one_slot, 0)


def lay_late(rows, which):
    return pl.pallas_call(
        functools.partial(late_kernel, which),
        in_specs=whole(1),
        out_specs=whole(1)[0],
        out_shape=jax.ShapeDtypeStruct((SLABS, LATE_ROWS, PART), jnp.float32),
        compiler_params=roomy(24),
        name="lay_late",
    )(rows)


def merge_kernel(place_ref, raw_ref, own_ref, take_ref, out_ref, rows_ref, even_ref, odd_ref):
    turned_scatter(place_ref, raw_ref, rows_ref, even_ref, odd_ref)

    def one_slot(slot, carry):
        start = pl.multiple_of(slot * WIRES, 8)
        for piece in range(3):
            rows = pl.ds(start + piece * EARLY_ROWS, EARLY_ROWS)
            take = take_ref[piece * EARLY_ROWS : (piece + 1) * EARLY_ROWS, :] > 0.5
            value = jnp.where(take, rows_ref[rows, 0:EARLY], own_ref[rows, 0:EARLY])
            out_ref[slot, :, piece * EARLY : (piece + 1) * EARLY] = value
        return carry

    lax.fori_loop(0, SLABS, one_slot, 0)


def merge_rows(place, raw_turned, own, take):
    chan_count = raw_turned.shape[1]
    return pl.pallas_call(
        merge_kernel,
        in_specs=[pl.BlockSpec(memory_space=pltpu.SMEM)] + whole(3),
        out_specs=whole(1)[0],
        out_shape=jax.ShapeDtypeStruct((SLABS, EARLY_ROWS, PART), jnp.float32),
        scratch_shapes=[pltpu.VMEM((chan_count, PART), jnp.float32)] + [pltpu.VMEM((WIDE, PART), jnp.float32)] * 2,
        compiler_params=roomy(40),
        name="merge_rows",
    )(place, raw_turned, own, take)


def across(left, right):
    return lax.dot_general(left, right, (((1,), (1,)), ((), ())), preferred_element_type=jnp.float32)


def group_kernel(raw_ref, group_ref, good_ref, out_ref):
    group_count = out_ref.shape[0]
    names = lax.broadcasted_iota(jnp.int32, (group_count, WIDE), 0)

    def some(step, total):
        part = pl.ds(pl.multiple_of(step * WIDE, WIDE), WIDE)
        member = jnp.where(names == group_ref[:, part], good_ref[:, part], 0.0).astype(jnp.bfloat16)
        high, low = split(raw_ref[:, part])
        return total + (across(member, high) + across(member, low))

    out_ref[...] = lax.fori_loop(0, raw_ref.shape[1] // WIDE, some, jnp.zeros(out_ref.shape, jnp.float32))


def sum_groups(raw_turned, local_group, good_mask):
    group_count = raw_turned.shape[1] // GROUP
    return pl.pallas_call(
        group_kernel,
        in_specs=whole(3),
        out_specs=whole(1)[0],
        out_shape=jax.ShapeDtypeStruct((group_count, SLAB), jnp.float32),
        compiler_params=roomy(24),
        name="sum_groups",
    )(raw_turned, local_group[None, :], good_mask[None, :])


def facts_kernel(place_ref, facts_ref, out_ref):
    names = lax.broadcasted_iota(jnp.int32, (WIRES, BLOCK), 0)

    def some(step, total):
        part = pl.ds(pl.multiple_of(step * BLOCK, BLOCK), BLOCK)
        member = (names == place_ref[:, part]).astype(jnp.float32).astype(jnp.bfloat16)
        return total + across(facts_ref[:, part].astype(jnp.bfloat16), member)

    out_ref[...] = lax.fori_loop(0, place_ref.shape[1] // BLOCK, some, jnp.zeros(out_ref.shape, jnp.float32))


def pick_facts(place, facts):
    return pl.pallas_call(
        facts_kernel,
        in_specs=whole(2),
        out_specs=whole(1)[0],
        out_shape=jax.ShapeDtypeStruct((facts.shape[0], WIRES), jnp.float32),
        compiler_params=roomy(16),
        name="pick_facts",
    )(place[None, :], facts)


def add(first, second):
    return (first[0] + second[0], first[1] + second[1])


def sub(first, second):
    return (first[0] - second[0], first[1] - second[1])


def turn(value, sign):
    if sign < 0:
        return (value[1], -value[0])
    return (-value[1], value[0])


def scaled(value, angle):
    real, imag = math.cos(angle), math.sin(angle)
    if abs(angle) < 1e-12:
        return value
    return (value[0] * real - value[1] * imag, value[0] * imag + value[1] * real)


def four_point(items, sign):
    even_sum, even_diff = add(items[0], items[2]), sub(items[0], items[2])
    odd_sum, odd_diff = add(items[1], items[3]), turn(sub(items[1], items[3]), sign)
    return [add(even_sum, odd_sum), add(even_diff, odd_diff), sub(even_sum, odd_sum), sub(even_diff, odd_diff)]


def eighth(value, count, sign):
    root = math.sqrt(0.5)
    if count == 0:
        return value
    if count == 2:
        return turn(value, sign)
    real, imag = value
    if count == 1:
        return ((real - sign * imag) * root, (imag + sign * real) * root)
    return ((-real - sign * imag) * root, (sign * real - imag) * root)


def eight_point(items, sign):
    even = four_point(items[0::2], sign)
    odd = four_point(items[1::2], sign)
    odd = [eighth(value, count, sign) for count, value in enumerate(odd)]
    return [add(even[k], odd[k]) for k in range(4)] + [sub(even[k], odd[k]) for k in range(4)]


def slab_points(load, store, middle_ref, sign):
    for low in range(8):
        outs = four_point([load(8 * high + low) for high in range(4)], sign)
        for k, value in enumerate(outs):
            value = scaled(value, sign * 2.0 * math.pi * low * k / 32)
            middle_ref[8 * k + low, 0] = value[0]
            middle_ref[8 * k + low, 1] = value[1]
    for k in range(4):
        outs = eight_point([(middle_ref[8 * k + low, 0], middle_ref[8 * k + low, 1]) for low in range(8)], sign)
        for big, value in enumerate(outs):
            store(k + 4 * big, value)


def tail_kernel(
    early,
    own0,
    own1,
    got0,
    got1,
    take_ref,
    good_ref,
    common_ref,
    member_ref,
    high_ref,
    low_ref,
    filter_ref,
    twist_ref,
    tick_high_ref,
    tick_low_ref,
    untick_high_ref,
    untick_low_ref,
    back_high_ref,
    back_low_ref,
    out_ref,
    rows_ref,
    plane_ref,
    both_ref,
    covar_ref,
    power_ref,
    middle_ref,
):
    both_ref[...] = jnp.zeros_like(both_ref)
    covar_ref[...] = jnp.zeros_like(covar_ref)
    power_ref[...] = jnp.zeros_like(power_ref)

    def spread_common(pair):
        for slab in range(2):
            both_ref[:, slab * PART : slab * PART + SLAB] = common_ref[2 * pair + slab]
        high, low = split(both_ref[...])
        return dot(member_ref[...], high) + dot(member_ref[...], low)

    def assemble(pair, carry):
        for half in range(2):
            slab = 2 * pair + half
            base = half * PART
            rows_ref[pair, :, base + SLAB : base + PART] = jnp.zeros((WIRES, PART - SLAB), jnp.float32)
            for piece in range(3):
                rows = slice(piece * EARLY_ROWS, (piece + 1) * EARLY_ROWS)
                rows_ref[pair, rows, base : base + EARLY] = early[slab, :, piece * EARLY : (piece + 1) * EARLY]
            for which, (own, got) in enumerate(((own0, got0), (own1, got1))):
                sent = SENT[which]
                for piece in range(2):
                    part = slice(piece * LATE, (piece + 1) * LATE)
                    at = (which * 2 + piece) * LATE_ROWS
                    take = take_ref[at : at + sent, :] > 0.5
                    lanes = slice(base + EARLY, base + SLAB)
                    rows_ref[pair, at : at + sent, lanes] = jnp.where(take, got[slab, :, part], own[slab, 0:sent, part])
                    if sent < LATE_ROWS:
                        rows_ref[pair, at + sent : at + LATE_ROWS, lanes] = own[slab, sent:LATE_ROWS, part]
        spread = spread_common(pair)
        covar_ref[...] += rows_ref[pair] * spread
        power_ref[...] += spread * spread
        return carry

    lax.fori_loop(0, SLABS // 2, assemble, 0)
    covar = jnp.sum(covar_ref[...], axis=1, keepdims=True) / TICKS
    power = jnp.sum(power_ref[...], axis=1, keepdims=True) / TICKS
    weight = covar / (power + epsilon_power)

    def to_wires(pair, carry):
        cleaned = good_ref[...] * (rows_ref[pair] - weight * spread_common(pair))
        row_high, row_low = split(cleaned)
        result = three_dot(high_ref[...], low_ref[...], row_high, row_low)
        for slab in range(2):
            for part in range(2):
                plane_ref[2 * pair + slab, part] = result[
                    part * HALF : (part + 1) * HALF, slab * PART : (slab + 1) * PART
                ]
        return carry

    lax.fori_loop(0, SLABS // 2, to_wires, 0)

    def slabs_over(index, carry, sign):
        rows = pl.ds(pl.multiple_of(index * 8, 8), 8)

        def load(item):
            real, imag = plane_ref[item, 0, rows, :], plane_ref[item, 1, rows, :]
            if sign < 0:
                return (real, imag)
            cosine, sine = twist_ref[item, 0], twist_ref[item, 1]
            return (real * cosine - imag * sine, real * sine + imag * cosine)

        def store(item, value):
            real, imag = value
            if sign < 0:
                cosine, sine = twist_ref[item, 0], twist_ref[item, 1]
                real, imag = real * cosine + imag * sine, imag * cosine - real * sine
            plane_ref[item, 0, rows, :] = real
            plane_ref[item, 1, rows, :] = imag

        slab_points(load, store, middle_ref, sign)
        return carry

    lax.fori_loop(0, HALF // 8, functools.partial(slabs_over, sign=-1), 0)

    def filtered(item, carry):
        data_high, data_low = split(jnp.concatenate([plane_ref[item, 0], plane_ref[item, 1]], axis=1))
        spectrum = three_dot(data_high, data_low, tick_high_ref[...], tick_low_ref[...])
        real, imag = spectrum[:, :PART], spectrum[:, PART:]
        filter_real, filter_imag = filter_ref[item, :, :PART], filter_ref[item, :, PART:]
        mixed = jnp.concatenate(
            [real * filter_real - imag * filter_imag, real * filter_imag + imag * filter_real], axis=1
        )
        mixed_high, mixed_low = split(mixed)
        result = three_dot(mixed_high, mixed_low, untick_high_ref[...], untick_low_ref[...])
        plane_ref[item, 0] = result[:, :PART]
        plane_ref[item, 1] = result[:, PART:]
        return carry

    lax.fori_loop(0, SLABS, filtered, 0)
    lax.fori_loop(0, HALF // 8, functools.partial(slabs_over, sign=1), 0)
    for pair in range(SLABS // 2):
        both = jnp.concatenate(
            [plane_ref[2 * pair + slab].reshape(2 * HALF, PART) for slab in range(2)], axis=1
        )
        data_high, data_low = split(both)
        result = three_dot(back_high_ref[...], back_low_ref[...], data_high, data_low)
        for slab in range(2):
            at = (2 * pair + slab) * SLAB
            out_ref[:, at : at + SLAB] = result[:, slab * PART : slab * PART + SLAB]


def tail(early, own, got, take, good, commons, member, high, low, filters):
    back_high, back_low = two_halves(wire_tables()[1])
    tick, untick, twist = tick_tables()
    tables = (twist, *two_halves(tick), *two_halves(untick), back_high, back_low)
    operands = (early, *own, *got, take, good, commons, member, high, low, filters, *tables)
    return pl.pallas_call(
        tail_kernel,
        in_specs=whole(len(operands)),
        out_specs=whole(1)[0],
        out_shape=jax.ShapeDtypeStruct((WIRES, TICKS), jnp.float32),
        scratch_shapes=[
            pltpu.VMEM((SLABS // 2, WIRES, HALF), jnp.float32),
            pltpu.VMEM((SLABS, 2, HALF, PART), jnp.float32),
            pltpu.VMEM((commons.shape[1], HALF), jnp.float32),
            pltpu.VMEM((WIRES, HALF), jnp.float32),
            pltpu.VMEM((WIRES, HALF), jnp.float32),
            pltpu.VMEM((SLABS, 2, 8, PART), jnp.float32),
        ],
        compiler_params=roomy(60),
        name="deconvolve",
    )(*operands)


def make_filter(wire_kernel, time_kernel):
    forward, _ = wire_tables()
    wire_resp = jnp.dot(forward.astype(np.float32), wire_kernel, precision=highest).reshape(2, 1, HALF, 1)
    first = np.arange(SLABS)
    angle = 2.0 * np.pi * (np.outer(first, first) % SLABS) / SLABS
    slabs = time_kernel.reshape(SLABS, SLAB)
    real = jnp.dot(np.cos(angle).astype(np.float32), slabs, precision=highest)
    imag = jnp.dot(-np.sin(angle).astype(np.float32), slabs, precision=highest)
    twist = 2.0 * np.pi * np.outer(first, np.arange(SLAB)) / TICKS
    cosine, sine = np.cos(twist).astype(np.float32), np.sin(twist).astype(np.float32)
    real, imag = real * cosine + imag * sine, imag * cosine - real * sine
    inner = np.arange(SLAB)
    angle = 2.0 * np.pi * (np.outer(inner, inner) % SLAB) / SLAB
    cosine, sine = np.cos(angle).astype(np.float32), np.sin(angle).astype(np.float32)
    both = jnp.dot(
        jnp.concatenate([real, imag], axis=1),
        np.block([[cosine, -sine], [sine, cosine]]).astype(np.float32),
        precision=highest,
    )
    time_resp = jnp.pad(both.reshape(SLABS, 2, SLAB), ((0, 0), (0, 0), (0, PART - SLAB)))
    time_real, time_imag = time_resp[:, 0][:, None, :], time_resp[:, 1][:, None, :]
    real = wire_resp[0] * time_real - wire_resp[1] * time_imag
    imag = wire_resp[0] * time_imag + wire_resp[1] * time_real
    denominator = real * real + imag * imag + regular_term
    return jnp.concatenate([real / denominator, -imag / denominator], axis=2)


def picked_tables(wires):
    wire_high, wire_low = two_halves(wire_tables()[0])
    picked = (jnp.arange(WIRES, dtype=jnp.int32)[:, None] == wires[None, :]).astype(jnp.bfloat16)
    return dot(jnp.asarray(wire_high), picked).astype(jnp.bfloat16), dot(jnp.asarray(wire_low), picked).astype(
        jnp.bfloat16
    )


def shards(raw, bad, group_id, chan_plane, chan_wire, plane_offset, wire_kernel, time_kernel):
    chan_count = raw.shape[0]
    group_count = chan_count // GROUP
    apa_index = lax.axis_index("apa")
    tick_index = lax.axis_index("tick")
    parity = apa_index % 2
    swap = [(i, i ^ 1) for i in range(lax.axis_size("apa"))]
    raw_turned = raw.T
    early_got = lax.ppermute(raw_turned[:EARLY], "apa", swap)
    local_group = group_id - apa_index * group_count
    good_mask = 1.0 - bad.astype(jnp.float32)
    pair_base = (apa_index // 2 * 2 * SLABS).astype(jnp.int32)
    place, cross_count = rank_rows(chan_plane, pair_base, (1 - parity).astype(jnp.int32))
    place_got = lax.ppermute(place, "apa", swap)
    rows = pack_rows(place, raw_turned)
    late0, late1 = lay_late(rows, 0), lay_late(rows, 1)
    common = sum_groups(raw_turned, local_group, good_mask)
    common_got = lax.ppermute(common, "apa", swap)
    first = jnp.where(parity == 0, common, common_got)
    second = jnp.where(parity == 0, common_got, common)
    commons = lax.all_gather(jnp.concatenate([first, second], axis=0), "tick")
    blank = jnp.zeros_like(bad)
    facts = jnp.stack([chan_wire >> 5, chan_wire & 31, local_group, bad, chan_plane - pair_base, blank, blank, blank])
    facts = pick_facts(place - tick_index * WIRES, facts.astype(jnp.float32)).astype(jnp.int32)
    row_offset = jnp.take(plane_offset, facts[4] + pair_base)
    row_wire = (facts[0] * 32 + facts[1] + row_offset) % WIRES
    facts = jnp.stack([row_wire, facts[2] + parity * group_count, facts[3]])
    take = jnp.asarray(row_order()) < cross_count
    facts = jnp.where(take[None, :], lax.ppermute(facts, "apa", swap), facts)
    row_take = take.astype(jnp.float32)[:, None]
    row_good = 1.0 - facts[2].astype(jnp.float32)[:, None]
    member = (facts[1][:, None] == jnp.arange(2 * group_count, dtype=jnp.int32)[None, :]).astype(jnp.bfloat16)
    high, low = picked_tables(facts[0])
    filters = make_filter(wire_kernel, time_kernel)

    def over_ticks(value):
        return lax.all_to_all(value, "tick", split_axis=0, concat_axis=0, tiled=True)

    own0 = over_ticks(late0)
    late1, early_got = lax.optimization_barrier((late1, early_got))
    own1 = over_ticks(late1)
    got0 = lax.ppermute(own0[:, : SENT[0]], "apa", swap)
    early = merge_rows(place_got, early_got, rows, row_take)
    early, got0 = lax.optimization_barrier((early, got0))
    early = over_ticks(early)
    got1 = lax.ppermute(own1[:, : SENT[1]], "apa", swap)
    return tail(early, (own0, own1), (got0, got1), row_take, row_good, commons, member, high, low, filters)[None]


def solution(mesh):
    placed = (P("apa", "tick"), P("apa"), P("apa"), P("apa"), P("apa"), P(), P(), P())
    return jax.shard_map(
        shards,
        mesh=mesh,
        in_specs=placed,
        out_specs=P(("apa", "tick"), None, None),
        check_vma=False,
    )
```

```python
import functools
import math

import jax
import jax.numpy as jnp
import ml_dtypes
import numpy as np
from jax import lax
from jax.experimental import pallas as pl
from jax.experimental.pallas import tpu as pltpu
from jax.sharding import PartitionSpec as P

TICKS = 3200
GROUP = 128
WIRES = 480
SLABS = 32
SLAB = 100
PART = 128
HALF = 256
EARLY = 40
LATE = 60
EARLY_ROWS = 160
LATE_ROWS = (96, 144)
LATE_BASE = (0, 192)
BLOCK = 256
WIDE = 512
SENT = (96, 120)

highest = lax.Precision.HIGHEST
epsilon_power = 1e-06
regular_term = 0.25
mega = 1024 * 1024


light = pl.CostEstimate(flops=1, bytes_accessed=1, transcendentals=0)


def roomy(size):
    return pltpu.CompilerParams(vmem_limit_bytes=size * mega)


def two_halves(table):
    high = table.astype(ml_dtypes.bfloat16)
    low = (table - high.astype(np.float64)).astype(ml_dtypes.bfloat16)
    return high, low


def split(value):
    high = value.astype(jnp.bfloat16)
    low = (value - high.astype(jnp.float32)).astype(jnp.bfloat16)
    return high, low


def dot(left, right):
    return jnp.dot(left, right, preferred_element_type=jnp.float32)


def three_dot(left_high, left_low, right_high, right_low):
    return dot(left_high, right_high) + (dot(left_high, right_low) + dot(left_low, right_high))


def wire_tables():
    spread = np.outer(np.arange(WIRES // 2 + 1), np.arange(WIRES)) % WIRES
    angle = 2.0 * np.pi * spread / WIRES
    forward = np.zeros((2, HALF, WIRES))
    forward[0, : WIRES // 2 + 1] = np.cos(angle)
    forward[1, : WIRES // 2 + 1] = -np.sin(angle)
    weight = np.full((WIRES // 2 + 1, 1), 2.0)
    weight[0] = weight[-1] = 1.0
    weight /= WIRES * TICKS
    backward = np.zeros((2, HALF, WIRES))
    backward[0, : WIRES // 2 + 1] = weight * np.cos(angle)
    backward[1, : WIRES // 2 + 1] = -weight * np.sin(angle)
    return forward.reshape(2 * HALF, WIRES), backward.reshape(2 * HALF, WIRES).T.copy()


def tick_tables():
    angle = 2.0 * np.pi * (np.outer(np.arange(SLAB), np.arange(SLAB)) % SLAB) / SLAB
    table = np.zeros((2, PART, 2, PART))
    table[0, :SLAB, 0, :SLAB] = table[1, :SLAB, 1, :SLAB] = np.cos(angle)
    table[0, :SLAB, 1, :SLAB] = -np.sin(angle)
    table[1, :SLAB, 0, :SLAB] = np.sin(angle)
    table = table.reshape(HALF, HALF)
    twist = 2.0 * np.pi * np.outer(np.arange(SLABS), np.arange(PART)) / TICKS
    return table, table.T.copy(), np.stack([np.cos(twist), np.sin(twist)], axis=1).astype(np.float32)[:, :, None, :]


def row_order():
    row = np.arange(WIRES)
    piece = (row >= 336).astype(np.int32)
    place = row - 192 - 144 * piece
    late = np.where(place < 114, 192 + 114 * piece + place, 420 + 30 * piece + place - 114)
    return np.where(row < 192, row, late).astype(np.int32)


def rank_kernel(plane_ref, base_ref, cross_ref, place_ref, count_ref):
    tri_row = lax.broadcasted_iota(jnp.int32, (BLOCK, BLOCK), 0)
    tri_col = lax.broadcasted_iota(jnp.int32, (BLOCK, BLOCK), 1)
    earlier = (tri_row < tri_col).astype(jnp.float32).astype(jnp.bfloat16)
    names = lax.broadcasted_iota(jnp.int32, (2 * SLABS, BLOCK), 0)
    pair_base = base_ref[0]
    cross_side = cross_ref[0]
    chan_count = plane_ref.shape[1]
    local = plane_ref[...] - pair_base
    is_cross = (local // SLABS == cross_side).astype(jnp.float32)
    cross_count = jnp.sum(is_cross, axis=1, keepdims=True) * (1.0 / SLABS)
    before = jnp.zeros((2 * SLABS, 1), jnp.float32)
    for block in range(chan_count // BLOCK):
        part = slice(block * BLOCK, (block + 1) * BLOCK)
        member = (names == local[:, part]).astype(jnp.float32)
        prefix = dot(member.astype(jnp.bfloat16), earlier) + before
        rank = jnp.sum(member * prefix, axis=0, keepdims=True)
        before = before + jnp.sum(member, axis=1, keepdims=True)
        order = (rank + (1.0 - is_cross[:, part]) * cross_count).astype(jnp.int32)
        near_row = order + jnp.where(order >= 306, 30, 0)
        far_row = order - 114 + jnp.where(order >= 450, 114, 0)
        row = jnp.where(order < 192, order, jnp.where(order < 420, near_row, far_row))
        place_ref[:, part] = (local[:, part] % SLABS) * WIRES + row
    count_ref[...] = jnp.broadcast_to(cross_count.astype(jnp.int32), count_ref.shape)


def rank_rows(chan_plane, pair_base, cross_side):
    chan_count = chan_plane.shape[0]
    scalar = pl.BlockSpec(memory_space=pltpu.SMEM)
    whole = pl.BlockSpec(memory_space=pltpu.VMEM)
    place, count = pl.pallas_call(
        rank_kernel,
        in_specs=[whole, scalar, scalar],
        out_specs=[whole, whole],
        out_shape=[
            jax.ShapeDtypeStruct((1, chan_count), jnp.int32),
            jax.ShapeDtypeStruct((8, 128), jnp.int32),
        ],
        compiler_params=roomy(16),
        name="rank_rows",
    )(chan_plane[None, :], pair_base[None], cross_side[None])
    return place[0], count[0, 0]


def whole(count):
    return [pl.BlockSpec(memory_space=pltpu.VMEM)] * count


def turned_scatter(place_ref, raw_ref, rows_ref, even_ref, odd_ref):
    ticks, chan_count = raw_ref.shape
    steps = chan_count // WIDE

    def turn_block(step, to_ref):
        at = pl.multiple_of(step * WIDE, WIDE)
        to_ref[:, 0:ticks] = raw_ref[:, pl.ds(at, WIDE)].T

    def move(step, from_ref):
        first = step * WIDE
        for row in range(WIDE):
            rows_ref[pl.ds(place_ref[first + row], 1), :] = from_ref[pl.ds(row, 1), :]

    turn_block(0, even_ref)

    def both(half, carry):
        turn_block(2 * half + 1, odd_ref)
        move(2 * half, even_ref)
        turn_block(jnp.minimum(2 * half + 2, steps - 2), even_ref)
        move(2 * half + 1, odd_ref)
        return carry

    lax.fori_loop(0, steps // 2, both, 0)


def late_kernel(which, rows_ref, out_ref):
    size = LATE_ROWS[which]

    def one_slot(slot, carry):
        start = pl.multiple_of(slot * WIRES, 8)
        for piece in range(2):
            at = start + LATE_BASE[which] + piece * size
            out_ref[slot, :, piece * LATE : (piece + 1) * LATE] = rows_ref[pl.ds(at, size), EARLY:SLAB]
        return carry

    lax.fori_loop(0, SLABS, one_slot, 0)


def late_shape(which):
    return jax.ShapeDtypeStruct((SLABS, LATE_ROWS[which], PART), jnp.float32)


def pack_kernel(place_ref, raw_ref, late_ref, rows_out, rows_ref, even_ref, odd_ref, rows_done):
    turned_scatter(place_ref, raw_ref, rows_ref, even_ref, odd_ref)
    keep = pltpu.make_async_copy(rows_ref, rows_out, rows_done)
    keep.start()
    late_kernel(0, rows_ref, late_ref)
    keep.wait()


def pack_rows(place, raw_turned):
    chan_count = raw_turned.shape[1]
    return pl.pallas_call(
        pack_kernel,
        in_specs=[pl.BlockSpec(memory_space=pltpu.SMEM)] + whole(1),
        out_specs=whole(1) + [pl.BlockSpec(memory_space=pl.ANY)],
        out_shape=[late_shape(0), jax.ShapeDtypeStruct((chan_count, PART), jnp.float32)],
        scratch_shapes=[pltpu.VMEM((chan_count, PART), jnp.float32)]
        + [pltpu.VMEM((WIDE, PART), jnp.float32)] * 2
        + [pltpu.SemaphoreType.DMA],
        compiler_params=roomy(32),
        name="pack_rows",
    )(place, raw_turned)


def lay_late(rows, which):
    return pl.pallas_call(
        functools.partial(late_kernel, which),
        in_specs=whole(1),
        out_specs=whole(1)[0],
        out_shape=late_shape(which),
        compiler_params=roomy(20),
        name="lay_late",
        cost_estimate=light,
    )(rows)


def merge_kernel(place_ref, raw_ref, own_ref, take_ref, out_ref, rows_ref, even_ref, odd_ref):
    turned_scatter(place_ref, raw_ref, rows_ref, even_ref, odd_ref)

    def one_slot(slot, carry):
        start = pl.multiple_of(slot * WIRES, 8)
        for piece in range(3):
            rows = pl.ds(start + piece * EARLY_ROWS, EARLY_ROWS)
            take = take_ref[piece * EARLY_ROWS : (piece + 1) * EARLY_ROWS, :] > 0.5
            value = jnp.where(take, rows_ref[rows, 0:EARLY], own_ref[rows, 0:EARLY])
            out_ref[slot, :, piece * EARLY : (piece + 1) * EARLY] = value
        out_ref[slot, :, 3 * EARLY : PART] = jnp.zeros((EARLY_ROWS, PART - 3 * EARLY), jnp.float32)
        return carry

    lax.fori_loop(0, SLABS, one_slot, 0)


def merge_rows(place, raw_turned, own, take):
    chan_count = raw_turned.shape[1]
    return pl.pallas_call(
        merge_kernel,
        in_specs=[pl.BlockSpec(memory_space=pltpu.SMEM)] + whole(3),
        out_specs=whole(1)[0],
        out_shape=jax.ShapeDtypeStruct((SLABS, EARLY_ROWS, PART), jnp.float32),
        scratch_shapes=[pltpu.VMEM((chan_count, PART), jnp.float32)] + [pltpu.VMEM((WIDE, PART), jnp.float32)] * 2,
        compiler_params=roomy(40),
        name="merge_rows",
    )(place, raw_turned, own, take)


def across(left, right):
    return lax.dot_general(left, right, (((1,), (1,)), ((), ())), preferred_element_type=jnp.float32)


def group_kernel(raw_ref, group_ref, good_ref, out_ref):
    group_count = out_ref.shape[0]
    names = lax.broadcasted_iota(jnp.int32, (group_count, WIDE), 0)

    def some(step, total):
        part = pl.ds(pl.multiple_of(step * WIDE, WIDE), WIDE)
        member = jnp.where(names == group_ref[:, part], good_ref[:, part], 0.0).astype(jnp.bfloat16)
        high, low = split(raw_ref[:, part])
        return total + (across(member, high) + across(member, low))

    out_ref[...] = lax.fori_loop(0, raw_ref.shape[1] // WIDE, some, jnp.zeros(out_ref.shape, jnp.float32))


def sum_groups(raw_turned, local_group, good_mask):
    group_count = raw_turned.shape[1] // GROUP
    return pl.pallas_call(
        group_kernel,
        in_specs=whole(3),
        out_specs=whole(1)[0],
        out_shape=jax.ShapeDtypeStruct((group_count, SLAB), jnp.float32),
        compiler_params=roomy(24),
        name="sum_groups",
        cost_estimate=light,
    )(raw_turned, local_group[None, :], good_mask[None, :])


def facts_kernel(place_ref, facts_ref, out_ref):
    names = lax.broadcasted_iota(jnp.int32, (32, WIDE), 0)
    tops = lax.broadcasted_iota(jnp.int32, (16, WIDE), 0)

    def some(step, total):
        part = pl.ds(pl.multiple_of(step * WIDE, WIDE), WIDE)
        place = place_ref[:, part]
        top = tops == place >> 5
        picked = [jnp.where(top, facts_ref[fact : fact + 1, part], 0.0) for fact in range(facts_ref.shape[0])]
        member = (names == place & 31).astype(jnp.float32).astype(jnp.bfloat16)
        return total + across(jnp.concatenate(picked, axis=0).astype(jnp.bfloat16), member)

    out_ref[...] = lax.fori_loop(0, place_ref.shape[1] // WIDE, some, jnp.zeros(out_ref.shape, jnp.float32))


def pick_facts(place, facts):
    count = facts.shape[0]
    picked = pl.pallas_call(
        facts_kernel,
        in_specs=whole(2),
        out_specs=whole(1)[0],
        out_shape=jax.ShapeDtypeStruct((count * 16, 32), jnp.float32),
        compiler_params=roomy(16),
        name="pick_facts",
        cost_estimate=light,
    )(place[None, :], facts)
    return picked.reshape(count, 16 * 32)[:, :WIRES]


def add(first, second):
    return (first[0] + second[0], first[1] + second[1])


def sub(first, second):
    return (first[0] - second[0], first[1] - second[1])


def turn(value, sign):
    if sign < 0:
        return (value[1], -value[0])
    return (-value[1], value[0])


def scaled(value, angle):
    real, imag = math.cos(angle), math.sin(angle)
    if abs(angle) < 1e-12:
        return value
    return (value[0] * real - value[1] * imag, value[0] * imag + value[1] * real)


def four_point(items, sign):
    even_sum, even_diff = add(items[0], items[2]), sub(items[0], items[2])
    odd_sum, odd_diff = add(items[1], items[3]), turn(sub(items[1], items[3]), sign)
    return [add(even_sum, odd_sum), add(even_diff, odd_diff), sub(even_sum, odd_sum), sub(even_diff, odd_diff)]


def eighth(value, count, sign):
    root = math.sqrt(0.5)
    if count == 0:
        return value
    if count == 2:
        return turn(value, sign)
    real, imag = value
    if count == 1:
        return ((real - sign * imag) * root, (imag + sign * real) * root)
    return ((-real - sign * imag) * root, (sign * real - imag) * root)


def eight_point(items, sign):
    even = four_point(items[0::2], sign)
    odd = four_point(items[1::2], sign)
    odd = [eighth(value, count, sign) for count, value in enumerate(odd)]
    return [add(even[k], odd[k]) for k in range(4)] + [sub(even[k], odd[k]) for k in range(4)]


def slab_points(load, store, middle_ref, sign):
    for low in range(8):
        outs = four_point([load(8 * high + low) for high in range(4)], sign)
        for k, value in enumerate(outs):
            value = scaled(value, sign * 2.0 * math.pi * low * k / 32)
            middle_ref[8 * k + low, 0] = value[0]
            middle_ref[8 * k + low, 1] = value[1]
    for k in range(4):
        outs = eight_point([(middle_ref[8 * k + low, 0], middle_ref[8 * k + low, 1]) for low in range(8)], sign)
        for big, value in enumerate(outs):
            store(k + 4 * big, value)


def tail_kernel(
    early,
    own0,
    own1,
    got0,
    got1,
    take_ref,
    good_ref,
    common_ref,
    member_ref,
    high_ref,
    low_ref,
    filter_hbm,
    twist_ref,
    tick_high_ref,
    tick_low_ref,
    untick_high_ref,
    untick_low_ref,
    back_high_ref,
    back_low_ref,
    out_ref,
    rows_ref,
    plane_ref,
    both_ref,
    covar_ref,
    power_ref,
    middle_ref,
    filter_ref,
    filter_done,
):
    fetch = pltpu.make_async_copy(filter_hbm, filter_ref, filter_done)
    fetch.start()
    both_ref[...] = jnp.zeros_like(both_ref)
    covar_ref[...] = jnp.zeros_like(covar_ref)
    power_ref[...] = jnp.zeros_like(power_ref)

    def spread_common(pair):
        for slab in range(2):
            both_ref[:, slab * PART : slab * PART + SLAB] = common_ref[2 * pair + slab]
        high, low = split(both_ref[...])
        return dot(member_ref[...], high) + dot(member_ref[...], low)

    def spread_power(power):
        high, rest = split(power)
        middle = (power - high.astype(jnp.float32) - rest.astype(jnp.float32)).astype(jnp.bfloat16)
        return dot(member_ref[...], high) + (dot(member_ref[...], rest) + dot(member_ref[...], middle))

    def assemble(pair, carry):
        for half in range(2):
            slab = 2 * pair + half
            base = half * PART
            for piece in range(3):
                rows = slice(piece * EARLY_ROWS, (piece + 1) * EARLY_ROWS)
                value = early[slab]
                if piece:
                    value = pltpu.roll(value, PART - piece * EARLY, 1)
                rows_ref[pair, rows, base : base + PART] = value
            for which, (own, got) in enumerate(((own0, got0), (own1, got1))):
                sent = SENT[which]
                for piece in range(2):
                    part = slice(piece * LATE, (piece + 1) * LATE)
                    at = LATE_BASE[which] + piece * LATE_ROWS[which]
                    take = take_ref[at : at + sent, :] > 0.5
                    lanes = slice(base + EARLY, base + SLAB)
                    rows_ref[pair, at : at + sent, lanes] = jnp.where(take, got[slab, :, part], own[slab, 0:sent, part])
                    if sent < LATE_ROWS[which]:
                        rest = slice(at + sent, at + LATE_ROWS[which])
                        rows_ref[pair, rest, lanes] = own[slab, sent : LATE_ROWS[which], part]
        spread = spread_common(pair)
        covar_ref[...] += rows_ref[pair] * spread
        power_ref[...] += both_ref[...] * both_ref[...]
        return carry

    lax.fori_loop(0, SLABS // 2, assemble, 0)
    covar = jnp.sum(covar_ref[...], axis=1, keepdims=True) / TICKS
    power = jnp.sum(power_ref[...], axis=1, keepdims=True) / TICKS
    power = spread_power(jnp.broadcast_to(power, (power.shape[0], PART)))[:, 0:1]
    weight = covar / (power + epsilon_power)

    def to_wires(pair, carry):
        cleaned = good_ref[...] * (rows_ref[pair] - weight * spread_common(pair))
        row_high, row_low = split(cleaned)
        result = three_dot(high_ref[...], low_ref[...], row_high, row_low)
        for slab in range(2):
            for part in range(2):
                plane_ref[2 * pair + slab, part] = result[
                    part * HALF : (part + 1) * HALF, slab * PART : (slab + 1) * PART
                ]
        return carry

    for pair in range(SLABS // 2):
        to_wires(pair, 0)

    def slabs_over(index, carry, sign):
        rows = pl.ds(pl.multiple_of(index * 8, 8), 8)

        def load(item):
            real, imag = plane_ref[item, 0, rows, :], plane_ref[item, 1, rows, :]
            if sign < 0:
                return (real, imag)
            cosine, sine = twist_ref[item, 0], twist_ref[item, 1]
            return (real * cosine - imag * sine, real * sine + imag * cosine)

        def store(item, value):
            real, imag = value
            if sign < 0:
                cosine, sine = twist_ref[item, 0], twist_ref[item, 1]
                real, imag = real * cosine + imag * sine, imag * cosine - real * sine
            plane_ref[item, 0, rows, :] = real
            plane_ref[item, 1, rows, :] = imag

        slab_points(load, store, middle_ref, sign)
        return carry

    lax.fori_loop(0, HALF // 8, functools.partial(slabs_over, sign=-1), 0)

    def filtered(item, carry):
        data_high, data_low = split(jnp.concatenate([plane_ref[item, 0], plane_ref[item, 1]], axis=1))
        spectrum = three_dot(data_high, data_low, tick_high_ref[...], tick_low_ref[...])
        real, imag = spectrum[:, :PART], spectrum[:, PART:]
        filter_real, filter_imag = filter_ref[item, :, :PART], filter_ref[item, :, PART:]
        mixed = jnp.concatenate(
            [real * filter_real - imag * filter_imag, real * filter_imag + imag * filter_real], axis=1
        )
        mixed_high, mixed_low = split(mixed)
        result = three_dot(mixed_high, mixed_low, untick_high_ref[...], untick_low_ref[...])
        plane_ref[item, 0] = result[:, :PART]
        plane_ref[item, 1] = result[:, PART:]
        return carry

    fetch.wait()
    lax.fori_loop(0, SLABS, filtered, 0, unroll=8)
    lax.fori_loop(0, HALF // 8, functools.partial(slabs_over, sign=1), 0)
    for pair in range(SLABS // 2):
        both = jnp.concatenate(
            [plane_ref[2 * pair + slab].reshape(2 * HALF, PART) for slab in range(2)], axis=1
        )
        data_high, data_low = split(both)
        result = three_dot(back_high_ref[...], back_low_ref[...], data_high, data_low)
        for slab in range(2):
            at = (2 * pair + slab) * SLAB
            out_ref[:, at : at + SLAB] = result[:, slab * PART : slab * PART + SLAB]


def tail(early, own, got, take, good, commons, member, high, low, filters):
    back_high, back_low = two_halves(wire_tables()[1])
    tick, untick, twist = tick_tables()
    tables = (twist, *two_halves(tick), *two_halves(untick), back_high, back_low)
    operands = (early, *own, *got, take, good, commons, member, high, low, filters, *tables)
    return pl.pallas_call(
        tail_kernel,
        in_specs=whole(11) + [pl.BlockSpec(memory_space=pl.ANY)] + whole(len(operands) - 12),
        out_specs=whole(1)[0],
        out_shape=jax.ShapeDtypeStruct((WIRES, TICKS), jnp.float32),
        scratch_shapes=[
            pltpu.VMEM((SLABS // 2, WIRES, HALF), jnp.float32),
            pltpu.VMEM((SLABS, 2, HALF, PART), jnp.float32),
            pltpu.VMEM((commons.shape[1], HALF), jnp.float32),
            pltpu.VMEM((WIRES, HALF), jnp.float32),
            pltpu.VMEM((commons.shape[1], HALF), jnp.float32),
            pltpu.VMEM((SLABS, 2, 8, PART), jnp.float32),
            pltpu.VMEM((SLABS, HALF, HALF), jnp.float32),
            pltpu.SemaphoreType.DMA,
        ],
        compiler_params=roomy(60),
        name="deconvolve",
    )(*operands)


def make_filter(wire_kernel, time_kernel):
    forward, _ = wire_tables()
    wire_resp = jnp.dot(forward.astype(np.float32), wire_kernel, precision=highest).reshape(2, 1, HALF, 1)
    first = np.arange(SLABS)
    angle = 2.0 * np.pi * (np.outer(first, first) % SLABS) / SLABS
    slabs = time_kernel.reshape(SLABS, SLAB)
    real = jnp.dot(np.cos(angle).astype(np.float32), slabs, precision=highest)
    imag = jnp.dot(-np.sin(angle).astype(np.float32), slabs, precision=highest)
    twist = 2.0 * np.pi * np.outer(first, np.arange(SLAB)) / TICKS
    cosine, sine = np.cos(twist).astype(np.float32), np.sin(twist).astype(np.float32)
    real, imag = real * cosine + imag * sine, imag * cosine - real * sine
    inner = np.arange(SLAB)
    angle = 2.0 * np.pi * (np.outer(inner, inner) % SLAB) / SLAB
    cosine, sine = np.cos(angle).astype(np.float32), np.sin(angle).astype(np.float32)
    both = jnp.dot(
        jnp.concatenate([real, imag], axis=1),
        np.block([[cosine, -sine], [sine, cosine]]).astype(np.float32),
        precision=highest,
    )
    time_resp = jnp.pad(both.reshape(SLABS, 2, SLAB), ((0, 0), (0, 0), (0, PART - SLAB)))
    time_real, time_imag = time_resp[:, 0][:, None, :], time_resp[:, 1][:, None, :]
    real = wire_resp[0] * time_real - wire_resp[1] * time_imag
    imag = wire_resp[0] * time_imag + wire_resp[1] * time_real
    denominator = real * real + imag * imag + regular_term
    return jnp.concatenate([real / denominator, -imag / denominator], axis=2)


def picked_tables(wires):
    wire_high, wire_low = two_halves(wire_tables()[0])
    picked = (jnp.arange(WIRES, dtype=jnp.int32)[:, None] == wires[None, :]).astype(jnp.bfloat16)
    return dot(jnp.asarray(wire_high), picked).astype(jnp.bfloat16), dot(jnp.asarray(wire_low), picked).astype(
        jnp.bfloat16
    )


def shards(raw, bad, group_id, chan_plane, chan_wire, plane_offset, wire_kernel, time_kernel):
    chan_count = raw.shape[0]
    group_count = chan_count // GROUP
    apa_index = lax.axis_index("apa")
    tick_index = lax.axis_index("tick")
    parity = apa_index % 2
    swap = [(i, i ^ 1) for i in range(lax.axis_size("apa"))]
    raw_turned = raw.T
    early_got = lax.ppermute(raw_turned[:EARLY], "apa", swap)
    local_group = group_id - apa_index * group_count
    good_mask = 1.0 - bad.astype(jnp.float32)
    pair_base = (apa_index // 2 * 2 * SLABS).astype(jnp.int32)
    place, cross_count = rank_rows(chan_plane, pair_base, (1 - parity).astype(jnp.int32))
    place_got = lax.ppermute(place, "apa", swap)
    late0, rows = pack_rows(place, raw_turned)
    late0, later_place, later_raw = lax.optimization_barrier((late0, place, raw_turned))
    common = sum_groups(later_raw, local_group, good_mask)
    late1 = lay_late(rows, 1)

    def over_ticks(value):
        return lax.all_to_all(value, "tick", split_axis=0, concat_axis=0, tiled=True)

    own0 = over_ticks(late0)
    common_got = lax.ppermute(common, "apa", swap)
    first = jnp.where(parity == 0, common, common_got)
    second = jnp.where(parity == 0, common_got, common)
    commons = lax.all_gather(jnp.concatenate([first, second], axis=0), "tick")
    facts = jnp.stack([chan_wire >> 5, chan_wire & 31, local_group, bad, chan_plane - pair_base])
    facts = pick_facts(later_place - tick_index * WIRES, facts.astype(jnp.float32)).astype(jnp.int32)
    row_offset = jnp.take(plane_offset, facts[4] + pair_base)
    row_wire = (facts[0] * 32 + facts[1] + row_offset) % WIRES
    facts = jnp.stack([row_wire, facts[2] + parity * group_count, facts[3]])
    take = jnp.asarray(row_order()) < cross_count
    facts = jnp.where(take[None, :], lax.ppermute(facts, "apa", swap), facts)
    row_take = take.astype(jnp.float32)[:, None]
    row_good = 1.0 - facts[2].astype(jnp.float32)[:, None]
    member = (facts[1][:, None] == jnp.arange(2 * group_count, dtype=jnp.int32)[None, :]).astype(jnp.bfloat16)
    high, low = picked_tables(facts[0])
    filters = make_filter(wire_kernel, time_kernel)
    own0, late1, early_got = lax.optimization_barrier((own0, late1, early_got))
    own1 = over_ticks(late1)
    got0 = lax.ppermute(own0[:, : SENT[0]], "apa", swap)
    early = merge_rows(place_got, early_got, rows, row_take)
    early, got0 = lax.optimization_barrier((early, got0))
    early = over_ticks(early)
    got1 = lax.ppermute(own1[:, : SENT[1]], "apa", swap)
    return tail(early, (own0, own1), (got0, got1), row_take, row_good, commons, member, high, low, filters)[None]


def solution(mesh):
    placed = (P("apa", "tick"), P("apa"), P("apa"), P("apa"), P("apa"), P(), P(), P())
    return jax.shard_map(
        shards,
        mesh=mesh,
        in_specs=placed,
        out_specs=P(("apa", "tick"), None, None),
        check_vma=False,
    )
```

```python
import functools
import math

import jax
import jax.numpy as jnp
import ml_dtypes
import numpy as np
from jax import lax
from jax.experimental import pallas as pl
from jax.experimental.pallas import tpu as pltpu
from jax.sharding import PartitionSpec as P

TICKS = 3200
GROUP = 128
WIRES = 480
SLABS = 32
SLAB = 100
PART = 128
HALF = 256
EARLY = 40
LATE = 60
EARLY_ROWS = 160
LATE_ROWS = (96, 144)
LATE_BASE = (0, 192)
BLOCK = 256
WIDE = 512
SENT = (96, 120)

highest = lax.Precision.HIGHEST
epsilon_power = 1e-06
regular_term = 0.25
mega = 1024 * 1024


light = pl.CostEstimate(flops=1, bytes_accessed=1, transcendentals=0)


def roomy(size):
    return pltpu.CompilerParams(vmem_limit_bytes=size * mega)


def two_halves(table):
    high = table.astype(ml_dtypes.bfloat16)
    low = (table - high.astype(np.float64)).astype(ml_dtypes.bfloat16)
    return high, low


def split(value):
    high = value.astype(jnp.bfloat16)
    low = (value - high.astype(jnp.float32)).astype(jnp.bfloat16)
    return high, low


def dot(left, right):
    return jnp.dot(left, right, preferred_element_type=jnp.float32)


def three_dot(left_high, left_low, right_high, right_low):
    return dot(left_high, right_high) + (dot(left_high, right_low) + dot(left_low, right_high))


def wire_tables():
    spread = np.outer(np.arange(WIRES // 2 + 1), np.arange(WIRES)) % WIRES
    angle = 2.0 * np.pi * spread / WIRES
    forward = np.zeros((2, HALF, WIRES))
    forward[0, : WIRES // 2 + 1] = np.cos(angle)
    forward[1, : WIRES // 2 + 1] = -np.sin(angle)
    weight = np.full((WIRES // 2 + 1, 1), 2.0)
    weight[0] = weight[-1] = 1.0
    weight /= WIRES * TICKS
    backward = np.zeros((2, HALF, WIRES))
    backward[0, : WIRES // 2 + 1] = weight * np.cos(angle)
    backward[1, : WIRES // 2 + 1] = -weight * np.sin(angle)
    return forward.reshape(2 * HALF, WIRES), backward.reshape(2 * HALF, WIRES).T.copy()


def tick_tables():
    angle = 2.0 * np.pi * (np.outer(np.arange(SLAB), np.arange(SLAB)) % SLAB) / SLAB
    table = np.zeros((2, PART, 2, PART))
    table[0, :SLAB, 0, :SLAB] = table[1, :SLAB, 1, :SLAB] = np.cos(angle)
    table[0, :SLAB, 1, :SLAB] = -np.sin(angle)
    table[1, :SLAB, 0, :SLAB] = np.sin(angle)
    table = table.reshape(HALF, HALF)
    twist = 2.0 * np.pi * np.outer(np.arange(SLABS), np.arange(PART)) / TICKS
    return table, table.T.copy(), np.stack([np.cos(twist), np.sin(twist)], axis=1).astype(np.float32)[:, :, None, :]


def row_order():
    row = np.arange(WIRES)
    piece = (row >= 336).astype(np.int32)
    place = row - 192 - 144 * piece
    late = np.where(place < 114, 192 + 114 * piece + place, 420 + 30 * piece + place - 114)
    return np.where(row < 192, row, late).astype(np.int32)


def rank_kernel(plane_ref, base_ref, cross_ref, place_ref, count_ref):
    tri_row = lax.broadcasted_iota(jnp.int32, (BLOCK, BLOCK), 0)
    tri_col = lax.broadcasted_iota(jnp.int32, (BLOCK, BLOCK), 1)
    earlier = (tri_row < tri_col).astype(jnp.float32).astype(jnp.bfloat16)
    names = lax.broadcasted_iota(jnp.int32, (2 * SLABS, BLOCK), 0)
    pair_base = base_ref[0]
    cross_side = cross_ref[0]
    chan_count = plane_ref.shape[1]
    local = plane_ref[...] - pair_base
    is_cross = (local // SLABS == cross_side).astype(jnp.float32)
    cross_count = jnp.sum(is_cross, axis=1, keepdims=True) * (1.0 / SLABS)
    before = jnp.zeros((2 * SLABS, 1), jnp.float32)
    for block in range(chan_count // BLOCK):
        part = slice(block * BLOCK, (block + 1) * BLOCK)
        member = (names == local[:, part]).astype(jnp.float32)
        prefix = dot(member.astype(jnp.bfloat16), earlier) + before
        rank = jnp.sum(member * prefix, axis=0, keepdims=True)
        before = before + jnp.sum(member, axis=1, keepdims=True)
        order = (rank + (1.0 - is_cross[:, part]) * cross_count).astype(jnp.int32)
        near_row = order + jnp.where(order >= 306, 30, 0)
        far_row = order - 114 + jnp.where(order >= 450, 114, 0)
        row = jnp.where(order < 192, order, jnp.where(order < 420, near_row, far_row))
        place_ref[:, part] = (local[:, part] % SLABS) * WIRES + row
    count_ref[...] = jnp.broadcast_to(cross_count.astype(jnp.int32), count_ref.shape)


def rank_rows(chan_plane, pair_base, cross_side):
    chan_count = chan_plane.shape[0]
    scalar = pl.BlockSpec(memory_space=pltpu.SMEM)
    whole = pl.BlockSpec(memory_space=pltpu.VMEM)
    place, count = pl.pallas_call(
        rank_kernel,
        in_specs=[whole, scalar, scalar],
        out_specs=[whole, whole],
        out_shape=[
            jax.ShapeDtypeStruct((1, chan_count), jnp.int32),
            jax.ShapeDtypeStruct((8, 128), jnp.int32),
        ],
        compiler_params=roomy(16),
        name="rank_rows",
    )(chan_plane[None, :], pair_base[None], cross_side[None])
    return place[0], count[0, 0]


def whole(count):
    return [pl.BlockSpec(memory_space=pltpu.VMEM)] * count


def turned_scatter(place_ref, raw_ref, rows_ref, even_ref, odd_ref):
    ticks, chan_count = raw_ref.shape
    steps = chan_count // WIDE

    def turn_block(step, to_ref):
        at = pl.multiple_of(step * WIDE, WIDE)
        to_ref[:, 0:ticks] = raw_ref[:, pl.ds(at, WIDE)].T

    def move(step, from_ref):
        first = step * WIDE
        for row in range(WIDE):
            rows_ref[pl.ds(place_ref[first + row], 1), :] = from_ref[pl.ds(row, 1), :]

    turn_block(0, even_ref)

    def both(half, carry):
        turn_block(2 * half + 1, odd_ref)
        move(2 * half, even_ref)
        turn_block(jnp.minimum(2 * half + 2, steps - 2), even_ref)
        move(2 * half + 1, odd_ref)
        return carry

    lax.fori_loop(0, steps // 2, both, 0)


def late_kernel(which, rows_ref, out_ref, low=0, high=SLABS):
    size = LATE_ROWS[which]

    def one_slot(slot, carry):
        start = pl.multiple_of(slot * WIRES, 8)
        for piece in range(2):
            at = start + LATE_BASE[which] + piece * size
            out_ref[slot, :, piece * LATE : (piece + 1) * LATE] = rows_ref[pl.ds(at, size), EARLY:SLAB]
        return carry

    lax.fori_loop(low, high, one_slot, 0)


def late_shape(which):
    return jax.ShapeDtypeStruct((SLABS, LATE_ROWS[which], PART), jnp.float32)


def pack_kernel(place_ref, raw_ref, late_out, rows_out, rows_ref, late_ref, even_ref, odd_ref, rows_done, late_done):
    turned_scatter(place_ref, raw_ref, rows_ref, even_ref, odd_ref)
    keep = pltpu.make_async_copy(rows_ref, rows_out, rows_done)
    keep.start()
    late_kernel(0, rows_ref, late_ref)
    send = pltpu.make_async_copy(late_ref, late_out, late_done)
    send.start()
    keep.wait()
    send.wait()


def pack_rows(place, raw_turned):
    chan_count = raw_turned.shape[1]
    return pl.pallas_call(
        pack_kernel,
        in_specs=[pl.BlockSpec(memory_space=pltpu.SMEM)] + whole(1),
        out_specs=[pl.BlockSpec(memory_space=pltpu.HBM)] * 2,
        out_shape=[late_shape(0), jax.ShapeDtypeStruct((chan_count, PART), jnp.float32)],
        scratch_shapes=[
            pltpu.VMEM((chan_count, PART), jnp.float32),
            pltpu.VMEM((SLABS, LATE_ROWS[0], PART), jnp.float32),
        ]
        + [pltpu.VMEM((WIDE, PART), jnp.float32)] * 2
        + [pltpu.SemaphoreType.DMA] * 2,
        compiler_params=roomy(60),
        name="pack_rows",
    )(place, raw_turned)


def fetched_late_kernel(which, rows_hbm, out_ref, rows_ref, done_ref):
    quarter = rows_ref.shape[0] // 4
    copies = [
        pltpu.make_async_copy(
            rows_hbm.at[pl.ds(part * quarter, quarter)], rows_ref.at[pl.ds(part * quarter, quarter)], done_ref.at[part]
        )
        for part in range(4)
    ]
    for copy in copies:
        copy.start()
    for part, copy in enumerate(copies):
        copy.wait()
        late_kernel(which, rows_ref, out_ref, part * SLABS // 4, (part + 1) * SLABS // 4)


def lay_late(rows, which):
    return pl.pallas_call(
        functools.partial(fetched_late_kernel, which),
        in_specs=[pl.BlockSpec(memory_space=pltpu.HBM)],
        out_specs=whole(1)[0],
        out_shape=late_shape(which),
        scratch_shapes=[pltpu.VMEM(rows.shape, jnp.float32), pltpu.SemaphoreType.DMA((4,))],
        compiler_params=roomy(60),
        name="lay_late",
        cost_estimate=light,
    )(rows)


def merge_kernel(place_ref, raw_ref, own_hbm, take_ref, out_ref, rows_ref, even_ref, odd_ref, own_ref, own_done):
    fetch = pltpu.make_async_copy(own_hbm, own_ref, own_done)
    fetch.start()
    turned_scatter(place_ref, raw_ref, rows_ref, even_ref, odd_ref)
    fetch.wait()

    def one_slot(slot, carry):
        start = pl.multiple_of(slot * WIRES, 8)
        for piece in range(3):
            rows = pl.ds(start + piece * EARLY_ROWS, EARLY_ROWS)
            take = take_ref[piece * EARLY_ROWS : (piece + 1) * EARLY_ROWS, :] > 0.5
            value = jnp.where(take, rows_ref[rows, 0:EARLY], own_ref[rows, 0:EARLY])
            out_ref[slot, :, piece * EARLY : (piece + 1) * EARLY] = value
        out_ref[slot, :, 3 * EARLY : PART] = jnp.zeros((EARLY_ROWS, PART - 3 * EARLY), jnp.float32)
        return carry

    lax.fori_loop(0, SLABS, one_slot, 0)


def merge_rows(place, raw_turned, own, take):
    chan_count = raw_turned.shape[1]
    return pl.pallas_call(
        merge_kernel,
        in_specs=[pl.BlockSpec(memory_space=pltpu.SMEM)] + whole(1) + [pl.BlockSpec(memory_space=pltpu.HBM)] + whole(1),
        out_specs=whole(1)[0],
        out_shape=jax.ShapeDtypeStruct((SLABS, EARLY_ROWS, PART), jnp.float32),
        scratch_shapes=[pltpu.VMEM((chan_count, PART), jnp.float32)]
        + [pltpu.VMEM((WIDE, PART), jnp.float32)] * 2
        + [pltpu.VMEM((chan_count, PART), jnp.float32), pltpu.SemaphoreType.DMA],
        compiler_params=roomy(60),
        name="merge_rows",
    )(place, raw_turned, own, take)


def across(left, right):
    return lax.dot_general(left, right, (((1,), (1,)), ((), ())), preferred_element_type=jnp.float32)


def group_kernel(raw_ref, group_ref, good_ref, out_ref):
    group_count = out_ref.shape[0]
    names = lax.broadcasted_iota(jnp.int32, (group_count, WIDE), 0)

    def some(step, total):
        part = pl.ds(pl.multiple_of(step * WIDE, WIDE), WIDE)
        member = jnp.where(names == group_ref[:, part], good_ref[:, part], 0.0).astype(jnp.bfloat16)
        high, low = split(raw_ref[:, part])
        return total + (across(member, high) + across(member, low))

    out_ref[...] = lax.fori_loop(0, raw_ref.shape[1] // WIDE, some, jnp.zeros(out_ref.shape, jnp.float32))


def sum_groups(raw_turned, local_group, good_mask):
    group_count = raw_turned.shape[1] // GROUP
    return pl.pallas_call(
        group_kernel,
        in_specs=whole(3),
        out_specs=whole(1)[0],
        out_shape=jax.ShapeDtypeStruct((group_count, SLAB), jnp.float32),
        compiler_params=roomy(24),
        name="sum_groups",
        cost_estimate=light,
    )(raw_turned, local_group[None, :], good_mask[None, :])


def facts_kernel(place_ref, facts_ref, out_ref):
    names = lax.broadcasted_iota(jnp.int32, (32, WIDE), 0)
    tops = lax.broadcasted_iota(jnp.int32, (16, WIDE), 0)

    def some(step, total):
        part = pl.ds(pl.multiple_of(step * WIDE, WIDE), WIDE)
        place = place_ref[:, part]
        top = tops == place >> 5
        picked = [jnp.where(top, facts_ref[fact : fact + 1, part], 0.0) for fact in range(facts_ref.shape[0])]
        member = (names == place & 31).astype(jnp.float32).astype(jnp.bfloat16)
        return total + across(jnp.concatenate(picked, axis=0).astype(jnp.bfloat16), member)

    out_ref[...] = lax.fori_loop(0, place_ref.shape[1] // WIDE, some, jnp.zeros(out_ref.shape, jnp.float32))


def pick_facts(place, facts):
    count = facts.shape[0]
    picked = pl.pallas_call(
        facts_kernel,
        in_specs=whole(2),
        out_specs=whole(1)[0],
        out_shape=jax.ShapeDtypeStruct((count * 16, 32), jnp.float32),
        compiler_params=roomy(16),
        name="pick_facts",
        cost_estimate=light,
    )(place[None, :], facts)
    return picked.reshape(count, 16 * 32)[:, :WIRES]


def add(first, second):
    return (first[0] + second[0], first[1] + second[1])


def sub(first, second):
    return (first[0] - second[0], first[1] - second[1])


def turn(value, sign):
    if sign < 0:
        return (value[1], -value[0])
    return (-value[1], value[0])


def scaled(value, angle):
    real, imag = math.cos(angle), math.sin(angle)
    if abs(angle) < 1e-12:
        return value
    return (value[0] * real - value[1] * imag, value[0] * imag + value[1] * real)


def four_point(items, sign):
    even_sum, even_diff = add(items[0], items[2]), sub(items[0], items[2])
    odd_sum, odd_diff = add(items[1], items[3]), turn(sub(items[1], items[3]), sign)
    return [add(even_sum, odd_sum), add(even_diff, odd_diff), sub(even_sum, odd_sum), sub(even_diff, odd_diff)]


def eighth(value, count, sign):
    root = math.sqrt(0.5)
    if count == 0:
        return value
    if count == 2:
        return turn(value, sign)
    real, imag = value
    if count == 1:
        return ((real - sign * imag) * root, (imag + sign * real) * root)
    return ((-real - sign * imag) * root, (sign * real - imag) * root)


def eight_point(items, sign):
    even = four_point(items[0::2], sign)
    odd = four_point(items[1::2], sign)
    odd = [eighth(value, count, sign) for count, value in enumerate(odd)]
    return [add(even[k], odd[k]) for k in range(4)] + [sub(even[k], odd[k]) for k in range(4)]


def slab_points(load, store, middle_ref, sign):
    for low in range(8):
        outs = four_point([load(8 * high + low) for high in range(4)], sign)
        for k, value in enumerate(outs):
            value = scaled(value, sign * 2.0 * math.pi * low * k / 32)
            middle_ref[8 * k + low, 0] = value[0]
            middle_ref[8 * k + low, 1] = value[1]
    for k in range(4):
        outs = eight_point([(middle_ref[8 * k + low, 0], middle_ref[8 * k + low, 1]) for low in range(8)], sign)
        for big, value in enumerate(outs):
            store(k + 4 * big, value)


def tail_kernel(
    early,
    own0,
    own1,
    got0,
    got1,
    take_ref,
    good_ref,
    common_ref,
    member_ref,
    high_ref,
    low_ref,
    filter_hbm,
    twist_ref,
    tick_high_ref,
    tick_low_ref,
    untick_high_ref,
    untick_low_ref,
    back_high_ref,
    back_low_ref,
    out_ref,
    rows_ref,
    plane_ref,
    both_ref,
    covar_ref,
    power_ref,
    middle_ref,
    filter_ref,
    filter_done,
):
    fetch = pltpu.make_async_copy(filter_hbm, filter_ref, filter_done)
    fetch.start()
    both_ref[...] = jnp.zeros_like(both_ref)
    covar_ref[...] = jnp.zeros_like(covar_ref)
    power_ref[...] = jnp.zeros_like(power_ref)

    def spread_common(pair):
        for slab in range(2):
            both_ref[:, slab * PART : slab * PART + SLAB] = common_ref[2 * pair + slab]
        high, low = split(both_ref[...])
        return dot(member_ref[...], high) + dot(member_ref[...], low)

    def spread_power(power):
        high, rest = split(power)
        middle = (power - high.astype(jnp.float32) - rest.astype(jnp.float32)).astype(jnp.bfloat16)
        return dot(member_ref[...], high) + (dot(member_ref[...], rest) + dot(member_ref[...], middle))

    def assemble(pair, carry):
        for half in range(2):
            slab = 2 * pair + half
            base = half * PART
            for piece in range(3):
                rows = slice(piece * EARLY_ROWS, (piece + 1) * EARLY_ROWS)
                value = early[slab]
                if piece:
                    value = pltpu.roll(value, PART - piece * EARLY, 1)
                rows_ref[pair, rows, base : base + PART] = value
            for which, (own, got) in enumerate(((own0, got0), (own1, got1))):
                sent = SENT[which]
                for piece in range(2):
                    part = slice(piece * LATE, (piece + 1) * LATE)
                    at = LATE_BASE[which] + piece * LATE_ROWS[which]
                    take = take_ref[at : at + sent, :] > 0.5
                    lanes = slice(base + EARLY, base + SLAB)
                    rows_ref[pair, at : at + sent, lanes] = jnp.where(take, got[slab, :, part], own[slab, 0:sent, part])
                    if sent < LATE_ROWS[which]:
                        rest = slice(at + sent, at + LATE_ROWS[which])
                        rows_ref[pair, rest, lanes] = own[slab, sent : LATE_ROWS[which], part]
        spread = spread_common(pair)
        covar_ref[...] += rows_ref[pair] * spread
        power_ref[...] += both_ref[...] * both_ref[...]
        return carry

    lax.fori_loop(0, SLABS // 2, assemble, 0)
    covar = jnp.sum(covar_ref[...], axis=1, keepdims=True) / TICKS
    power = jnp.sum(power_ref[...], axis=1, keepdims=True) / TICKS
    power = spread_power(jnp.broadcast_to(power, (power.shape[0], PART)))[:, 0:1]
    weight = covar / (power + epsilon_power)

    def to_wires(pair, carry):
        cleaned = good_ref[...] * (rows_ref[pair] - weight * spread_common(pair))
        row_high, row_low = split(cleaned)
        result = three_dot(high_ref[...], low_ref[...], row_high, row_low)
        for slab in range(2):
            for part in range(2):
                plane_ref[2 * pair + slab, part] = result[
                    part * HALF : (part + 1) * HALF, slab * PART : (slab + 1) * PART
                ]
        return carry

    for pair in range(SLABS // 2):
        to_wires(pair, 0)

    def slabs_over(index, carry, sign):
        rows = pl.ds(pl.multiple_of(index * 8, 8), 8)

        def load(item):
            real, imag = plane_ref[item, 0, rows, :], plane_ref[item, 1, rows, :]
            if sign < 0:
                return (real, imag)
            cosine, sine = twist_ref[item, 0], twist_ref[item, 1]
            return (real * cosine - imag * sine, real * sine + imag * cosine)

        def store(item, value):
            real, imag = value
            if sign < 0:
                cosine, sine = twist_ref[item, 0], twist_ref[item, 1]
                real, imag = real * cosine + imag * sine, imag * cosine - real * sine
            plane_ref[item, 0, rows, :] = real
            plane_ref[item, 1, rows, :] = imag

        slab_points(load, store, middle_ref, sign)
        return carry

    lax.fori_loop(0, HALF // 8, functools.partial(slabs_over, sign=-1), 0)

    def filtered(item, carry):
        data_high, data_low = split(jnp.concatenate([plane_ref[item, 0], plane_ref[item, 1]], axis=1))
        spectrum = three_dot(data_high, data_low, tick_high_ref[...], tick_low_ref[...])
        real, imag = spectrum[:, :PART], spectrum[:, PART:]
        filter_real, filter_imag = filter_ref[item, :, :PART], filter_ref[item, :, PART:]
        mixed = jnp.concatenate(
            [real * filter_real - imag * filter_imag, real * filter_imag + imag * filter_real], axis=1
        )
        mixed_high, mixed_low = split(mixed)
        result = three_dot(mixed_high, mixed_low, untick_high_ref[...], untick_low_ref[...])
        plane_ref[item, 0] = result[:, :PART]
        plane_ref[item, 1] = result[:, PART:]
        return carry

    fetch.wait()
    lax.fori_loop(0, SLABS, filtered, 0, unroll=8)
    lax.fori_loop(0, HALF // 8, functools.partial(slabs_over, sign=1), 0)
    for pair in range(SLABS // 2):
        both = jnp.concatenate(
            [plane_ref[2 * pair + slab].reshape(2 * HALF, PART) for slab in range(2)], axis=1
        )
        data_high, data_low = split(both)
        result = three_dot(back_high_ref[...], back_low_ref[...], data_high, data_low)
        for slab in range(2):
            at = (2 * pair + slab) * SLAB
            out_ref[:, at : at + SLAB] = result[:, slab * PART : slab * PART + SLAB]


def tail(early, own, got, take, good, commons, member, high, low, filters):
    back_high, back_low = two_halves(wire_tables()[1])
    tick, untick, twist = tick_tables()
    tables = (twist, *two_halves(tick), *two_halves(untick), back_high, back_low)
    operands = (early, *own, *got, take, good, commons, member, high, low, filters, *tables)
    return pl.pallas_call(
        tail_kernel,
        in_specs=whole(11) + [pl.BlockSpec(memory_space=pl.ANY)] + whole(len(operands) - 12),
        out_specs=whole(1)[0],
        out_shape=jax.ShapeDtypeStruct((WIRES, TICKS), jnp.float32),
        scratch_shapes=[
            pltpu.VMEM((SLABS // 2, WIRES, HALF), jnp.float32),
            pltpu.VMEM((SLABS, 2, HALF, PART), jnp.float32),
            pltpu.VMEM((commons.shape[1], HALF), jnp.float32),
            pltpu.VMEM((WIRES, HALF), jnp.float32),
            pltpu.VMEM((commons.shape[1], HALF), jnp.float32),
            pltpu.VMEM((SLABS, 2, 8, PART), jnp.float32),
            pltpu.VMEM((SLABS, HALF, HALF), jnp.float32),
            pltpu.SemaphoreType.DMA,
        ],
        compiler_params=roomy(60),
        name="deconvolve",
    )(*operands)


def make_filter(wire_kernel, time_kernel):
    forward, _ = wire_tables()
    wire_resp = jnp.dot(forward.astype(np.float32), wire_kernel, precision=highest).reshape(2, 1, HALF, 1)
    first = np.arange(SLABS)
    angle = 2.0 * np.pi * (np.outer(first, first) % SLABS) / SLABS
    slabs = time_kernel.reshape(SLABS, SLAB)
    real = jnp.dot(np.cos(angle).astype(np.float32), slabs, precision=highest)
    imag = jnp.dot(-np.sin(angle).astype(np.float32), slabs, precision=highest)
    twist = 2.0 * np.pi * np.outer(first, np.arange(SLAB)) / TICKS
    cosine, sine = np.cos(twist).astype(np.float32), np.sin(twist).astype(np.float32)
    real, imag = real * cosine + imag * sine, imag * cosine - real * sine
    inner = np.arange(SLAB)
    angle = 2.0 * np.pi * (np.outer(inner, inner) % SLAB) / SLAB
    cosine, sine = np.cos(angle).astype(np.float32), np.sin(angle).astype(np.float32)
    both = jnp.dot(
        jnp.concatenate([real, imag], axis=1),
        np.block([[cosine, -sine], [sine, cosine]]).astype(np.float32),
        precision=highest,
    )
    time_resp = jnp.pad(both.reshape(SLABS, 2, SLAB), ((0, 0), (0, 0), (0, PART - SLAB)))
    time_real, time_imag = time_resp[:, 0][:, None, :], time_resp[:, 1][:, None, :]
    real = wire_resp[0] * time_real - wire_resp[1] * time_imag
    imag = wire_resp[0] * time_imag + wire_resp[1] * time_real
    denominator = real * real + imag * imag + regular_term
    return jnp.concatenate([real / denominator, -imag / denominator], axis=2)


def picked_tables(wires):
    wire_high, wire_low = two_halves(wire_tables()[0])
    picked = (jnp.arange(WIRES, dtype=jnp.int32)[:, None] == wires[None, :]).astype(jnp.bfloat16)
    return dot(jnp.asarray(wire_high), picked).astype(jnp.bfloat16), dot(jnp.asarray(wire_low), picked).astype(
        jnp.bfloat16
    )


def shards(raw, bad, group_id, chan_plane, chan_wire, plane_offset, wire_kernel, time_kernel):
    chan_count = raw.shape[0]
    group_count = chan_count // GROUP
    apa_index = lax.axis_index("apa")
    tick_index = lax.axis_index("tick")
    parity = apa_index % 2
    swap = [(i, i ^ 1) for i in range(lax.axis_size("apa"))]
    raw_turned = raw.T
    early_got = lax.ppermute(raw_turned[:EARLY], "apa", swap)
    local_group = group_id - apa_index * group_count
    good_mask = 1.0 - bad.astype(jnp.float32)
    pair_base = (apa_index // 2 * 2 * SLABS).astype(jnp.int32)
    place, cross_count = rank_rows(chan_plane, pair_base, (1 - parity).astype(jnp.int32))
    place_got = lax.ppermute(place, "apa", swap)
    late0, rows = pack_rows(place, raw_turned)
    late0, later_place, later_raw = lax.optimization_barrier((late0, place, raw_turned))
    common = sum_groups(later_raw, local_group, good_mask)
    late1 = lay_late(rows, 1)

    def over_ticks(value):
        return lax.all_to_all(value, "tick", split_axis=0, concat_axis=0, tiled=True)

    own0 = over_ticks(late0)
    common_got = lax.ppermute(common, "apa", swap)
    facts = jnp.stack([chan_wire >> 5, chan_wire & 31, local_group, bad, chan_plane - pair_base])
    facts = pick_facts(later_place - tick_index * WIRES, facts.astype(jnp.float32)).astype(jnp.int32)
    own0, late1, early_got, common_got = lax.optimization_barrier((own0, late1, early_got, common_got))
    first = jnp.where(parity == 0, common, common_got)
    second = jnp.where(parity == 0, common_got, common)
    commons = lax.all_gather(jnp.concatenate([first, second], axis=0), "tick")
    own1 = over_ticks(late1)
    got0 = lax.ppermute(own0[:, : SENT[0]], "apa", swap)
    take = jnp.asarray(row_order()) < cross_count
    row_take = take.astype(jnp.float32)[:, None]
    early = merge_rows(place_got, early_got, rows, row_take)
    early, got0, facts = lax.optimization_barrier((early, got0, facts))
    early = over_ticks(early)
    got1 = lax.ppermute(own1[:, : SENT[1]], "apa", swap)
    row_offset = jnp.take(plane_offset, facts[4] + pair_base)
    row_wire = (facts[0] * 32 + facts[1] + row_offset) % WIRES
    facts = jnp.stack([row_wire, facts[2] + parity * group_count, facts[3]])
    facts = jnp.where(take[None, :], lax.ppermute(facts, "apa", swap), facts)
    row_good = 1.0 - facts[2].astype(jnp.float32)[:, None]
    member = (facts[1][:, None] == jnp.arange(2 * group_count, dtype=jnp.int32)[None, :]).astype(jnp.bfloat16)
    high, low = picked_tables(facts[0])
    filters = make_filter(wire_kernel, time_kernel)
    return tail(early, (own0, own1), (got0, got1), row_take, row_good, commons, member, high, low, filters)[None]


def solution(mesh):
    placed = (P("apa", "tick"), P("apa"), P("apa"), P("apa"), P("apa"), P(), P(), P())
    return jax.shard_map(
        shards,
        mesh=mesh,
        in_specs=placed,
        out_specs=P(("apa", "tick"), None, None),
        check_vma=False,
    )
```

```python
import functools
import math

import jax
import jax.numpy as jnp
import ml_dtypes
import numpy as np
from jax import lax
from jax.experimental import pallas as pl
from jax.experimental.pallas import tpu as pltpu
from jax.sharding import PartitionSpec as P

TICKS = 3200
GROUP = 128
WIRES = 480
SLABS = 32
SLAB = 100
PART = 128
HALF = 256
EARLY = 40
LATE = 60
EARLY_ROWS = 160
LATE_ROWS = (96, 144)
LATE_BASE = (0, 192)
BLOCK = 256
WIDE = 512
OUT_PART = 640
SENT = (96, 120)

highest = lax.Precision.HIGHEST
epsilon_power = 1e-06
regular_term = 0.25
mega = 1024 * 1024


light = pl.CostEstimate(flops=1, bytes_accessed=1, transcendentals=0)


def roomy(size):
    return pltpu.CompilerParams(vmem_limit_bytes=size * mega)


def two_halves(table):
    high = table.astype(ml_dtypes.bfloat16)
    low = (table - high.astype(np.float64)).astype(ml_dtypes.bfloat16)
    return high, low


def split(value):
    high = value.astype(jnp.bfloat16)
    low = (value - high.astype(jnp.float32)).astype(jnp.bfloat16)
    return high, low


def dot(left, right):
    return jnp.dot(left, right, preferred_element_type=jnp.float32)


def three_dot(left_high, left_low, right_high, right_low):
    return dot(left_high, right_high) + (dot(left_high, right_low) + dot(left_low, right_high))


def wire_tables():
    spread = np.outer(np.arange(WIRES // 2 + 1), np.arange(WIRES)) % WIRES
    angle = 2.0 * np.pi * spread / WIRES
    forward = np.zeros((2, HALF, WIRES))
    forward[0, : WIRES // 2 + 1] = np.cos(angle)
    forward[1, : WIRES // 2 + 1] = -np.sin(angle)
    weight = np.full((WIRES // 2 + 1, 1), 2.0)
    weight[0] = weight[-1] = 1.0
    weight /= WIRES * TICKS
    backward = np.zeros((2, HALF, WIRES))
    backward[0, : WIRES // 2 + 1] = weight * np.cos(angle)
    backward[1, : WIRES // 2 + 1] = -weight * np.sin(angle)
    return forward.reshape(2 * HALF, WIRES), backward.reshape(2 * HALF, WIRES).T.copy()


def tick_tables():
    angle = 2.0 * np.pi * (np.outer(np.arange(SLAB), np.arange(SLAB)) % SLAB) / SLAB
    table = np.zeros((2, PART, 2, PART))
    table[0, :SLAB, 0, :SLAB] = table[1, :SLAB, 1, :SLAB] = np.cos(angle)
    table[0, :SLAB, 1, :SLAB] = -np.sin(angle)
    table[1, :SLAB, 0, :SLAB] = np.sin(angle)
    table = table.reshape(HALF, HALF)
    twist = 2.0 * np.pi * np.outer(np.arange(SLABS), np.arange(PART)) / TICKS
    return table, table.T.copy(), np.stack([np.cos(twist), np.sin(twist)], axis=1).astype(np.float32)[:, :, None, :]


def row_order():
    row = np.arange(WIRES)
    piece = (row >= 336).astype(np.int32)
    place = row - 192 - 144 * piece
    late = np.where(place < 114, 192 + 114 * piece + place, 420 + 30 * piece + place - 114)
    return np.where(row < 192, row, late).astype(np.int32)


def rank_kernel(plane_ref, base_ref, cross_ref, place_ref, count_ref):
    tri_row = lax.broadcasted_iota(jnp.int32, (BLOCK, BLOCK), 0)
    tri_col = lax.broadcasted_iota(jnp.int32, (BLOCK, BLOCK), 1)
    earlier = (tri_row < tri_col).astype(jnp.float32).astype(jnp.bfloat16)
    names = lax.broadcasted_iota(jnp.int32, (2 * SLABS, BLOCK), 0)
    pair_base = base_ref[0]
    cross_side = cross_ref[0]
    chan_count = plane_ref.shape[1]
    local = plane_ref[...] - pair_base
    is_cross = (local // SLABS == cross_side).astype(jnp.float32)
    cross_count = jnp.sum(is_cross, axis=1, keepdims=True) * (1.0 / SLABS)
    before = jnp.zeros((2 * SLABS, 1), jnp.float32)
    for block in range(chan_count // BLOCK):
        part = slice(block * BLOCK, (block + 1) * BLOCK)
        member = (names == local[:, part]).astype(jnp.float32)
        prefix = dot(member.astype(jnp.bfloat16), earlier) + before
        rank = jnp.sum(member * prefix, axis=0, keepdims=True)
        before = before + jnp.sum(member, axis=1, keepdims=True)
        order = (rank + (1.0 - is_cross[:, part]) * cross_count).astype(jnp.int32)
        near_row = order + jnp.where(order >= 306, 30, 0)
        far_row = order - 114 + jnp.where(order >= 450, 114, 0)
        row = jnp.where(order < 192, order, jnp.where(order < 420, near_row, far_row))
        place_ref[:, part] = (local[:, part] % SLABS) * WIRES + row
    count_ref[...] = jnp.broadcast_to(cross_count.astype(jnp.int32), count_ref.shape)


def rank_rows(chan_plane, pair_base, cross_side):
    chan_count = chan_plane.shape[0]
    scalar = pl.BlockSpec(memory_space=pltpu.SMEM)
    whole = pl.BlockSpec(memory_space=pltpu.VMEM)
    place, count = pl.pallas_call(
        rank_kernel,
        in_specs=[whole, scalar, scalar],
        out_specs=[whole, whole],
        out_shape=[
            jax.ShapeDtypeStruct((1, chan_count), jnp.int32),
            jax.ShapeDtypeStruct((8, 128), jnp.int32),
        ],
        compiler_params=roomy(16),
        name="rank_rows",
    )(chan_plane[None, :], pair_base[None], cross_side[None])
    return place[0], count[0, 0]


def whole(count):
    return [pl.BlockSpec(memory_space=pltpu.VMEM)] * count


def turned_scatter(place_ref, raw_ref, rows_ref, even_ref, odd_ref):
    ticks, chan_count = raw_ref.shape
    steps = chan_count // WIDE

    def turn_block(step, to_ref):
        at = pl.multiple_of(step * WIDE, WIDE)
        to_ref[:, 0:ticks] = raw_ref[:, pl.ds(at, WIDE)].T

    def move(step, from_ref):
        first = step * WIDE
        for row in range(WIDE):
            rows_ref[pl.ds(place_ref[first + row], 1), :] = from_ref[pl.ds(row, 1), :]

    turn_block(0, even_ref)

    def both(half, carry):
        turn_block(2 * half + 1, odd_ref)
        move(2 * half, even_ref)
        turn_block(jnp.minimum(2 * half + 2, steps - 2), even_ref)
        move(2 * half + 1, odd_ref)
        return carry

    lax.fori_loop(0, steps // 2, both, 0)


def late_kernel(which, rows_ref, out_ref, low=0, high=SLABS):
    size = LATE_ROWS[which]

    def one_slot(slot, carry):
        start = pl.multiple_of(slot * WIRES, 8)
        for piece in range(2):
            at = start + LATE_BASE[which] + piece * size
            out_ref[slot, :, piece * LATE : (piece + 1) * LATE] = rows_ref[pl.ds(at, size), EARLY:SLAB]
        return carry

    lax.fori_loop(low, high, one_slot, 0)


def late_shape(which):
    return jax.ShapeDtypeStruct((SLABS, LATE_ROWS[which], PART), jnp.float32)


def pack_kernel(place_ref, raw_ref, late_out, rows_out, rows_ref, late_ref, even_ref, odd_ref, rows_done, late_done):
    turned_scatter(place_ref, raw_ref, rows_ref, even_ref, odd_ref)
    keep = pltpu.make_async_copy(rows_ref, rows_out, rows_done)
    keep.start()
    late_kernel(0, rows_ref, late_ref)
    send = pltpu.make_async_copy(late_ref, late_out, late_done)
    send.start()
    keep.wait()
    send.wait()


def pack_rows(place, raw_turned):
    chan_count = raw_turned.shape[1]
    return pl.pallas_call(
        pack_kernel,
        in_specs=[pl.BlockSpec(memory_space=pltpu.SMEM)] + whole(1),
        out_specs=[pl.BlockSpec(memory_space=pltpu.HBM)] * 2,
        out_shape=[late_shape(0), jax.ShapeDtypeStruct((chan_count, PART), jnp.float32)],
        scratch_shapes=[
            pltpu.VMEM((chan_count, PART), jnp.float32),
            pltpu.VMEM((SLABS, LATE_ROWS[0], PART), jnp.float32),
        ]
        + [pltpu.VMEM((WIDE, PART), jnp.float32)] * 2
        + [pltpu.SemaphoreType.DMA] * 2,
        compiler_params=roomy(60),
        name="pack_rows",
    )(place, raw_turned)


def fetched_late_kernel(which, rows_hbm, out_ref, rows_ref, done_ref):
    quarter = rows_ref.shape[0] // 4
    copies = [
        pltpu.make_async_copy(
            rows_hbm.at[pl.ds(part * quarter, quarter)], rows_ref.at[pl.ds(part * quarter, quarter)], done_ref.at[part]
        )
        for part in range(4)
    ]
    for copy in copies:
        copy.start()
    for part, copy in enumerate(copies):
        copy.wait()
        late_kernel(which, rows_ref, out_ref, part * SLABS // 4, (part + 1) * SLABS // 4)


def lay_late(rows, which):
    return pl.pallas_call(
        functools.partial(fetched_late_kernel, which),
        in_specs=[pl.BlockSpec(memory_space=pltpu.HBM)],
        out_specs=whole(1)[0],
        out_shape=late_shape(which),
        scratch_shapes=[pltpu.VMEM(rows.shape, jnp.float32), pltpu.SemaphoreType.DMA((4,))],
        compiler_params=roomy(60),
        name="lay_late",
        cost_estimate=light,
    )(rows)


def merge_kernel(place_ref, raw_ref, own_hbm, take_ref, out_ref, rows_ref, even_ref, odd_ref, own_ref, own_done):
    fetch = pltpu.make_async_copy(own_hbm, own_ref, own_done)
    fetch.start()
    turned_scatter(place_ref, raw_ref, rows_ref, even_ref, odd_ref)
    fetch.wait()

    def one_slot(slot, carry):
        start = pl.multiple_of(slot * WIRES, 8)
        for piece in range(3):
            rows = pl.ds(start + piece * EARLY_ROWS, EARLY_ROWS)
            take = take_ref[piece * EARLY_ROWS : (piece + 1) * EARLY_ROWS, :] > 0.5
            value = jnp.where(take, rows_ref[rows, 0:EARLY], own_ref[rows, 0:EARLY])
            out_ref[slot, :, piece * EARLY : (piece + 1) * EARLY] = value
        out_ref[slot, :, 3 * EARLY : PART] = jnp.zeros((EARLY_ROWS, PART - 3 * EARLY), jnp.float32)
        return carry

    lax.fori_loop(0, SLABS, one_slot, 0)


def merge_rows(place, raw_turned, own, take):
    chan_count = raw_turned.shape[1]
    return pl.pallas_call(
        merge_kernel,
        in_specs=[pl.BlockSpec(memory_space=pltpu.SMEM)] + whole(1) + [pl.BlockSpec(memory_space=pltpu.HBM)] + whole(1),
        out_specs=whole(1)[0],
        out_shape=jax.ShapeDtypeStruct((SLABS, EARLY_ROWS, PART), jnp.float32),
        scratch_shapes=[pltpu.VMEM((chan_count, PART), jnp.float32)]
        + [pltpu.VMEM((WIDE, PART), jnp.float32)] * 2
        + [pltpu.VMEM((chan_count, PART), jnp.float32), pltpu.SemaphoreType.DMA],
        compiler_params=roomy(60),
        name="merge_rows",
    )(place, raw_turned, own, take)


def across(left, right):
    return lax.dot_general(left, right, (((1,), (1,)), ((), ())), preferred_element_type=jnp.float32)


def group_kernel(raw_ref, group_ref, good_ref, out_ref):
    group_count = out_ref.shape[0]
    names = lax.broadcasted_iota(jnp.int32, (group_count, WIDE), 0)

    def some(step, total):
        part = pl.ds(pl.multiple_of(step * WIDE, WIDE), WIDE)
        member = jnp.where(names == group_ref[:, part], good_ref[:, part], 0.0).astype(jnp.bfloat16)
        high, low = split(raw_ref[:, part])
        return total + (across(member, high) + across(member, low))

    zero = jnp.zeros((group_count, SLAB), jnp.float32)
    out_ref[...] = jnp.zeros_like(out_ref)
    out_ref[:, 0:SLAB] = lax.fori_loop(0, raw_ref.shape[1] // WIDE, some, zero)


def sum_groups(raw_turned, local_group, good_mask):
    group_count = raw_turned.shape[1] // GROUP
    return pl.pallas_call(
        group_kernel,
        in_specs=whole(3),
        out_specs=whole(1)[0],
        out_shape=jax.ShapeDtypeStruct((group_count, PART), jnp.float32),
        compiler_params=roomy(24),
        name="sum_groups",
        cost_estimate=light,
    )(raw_turned, local_group[None, :], good_mask[None, :])


def facts_kernel(place_ref, facts_ref, out_ref):
    names = lax.broadcasted_iota(jnp.int32, (32, WIDE), 0)
    tops = lax.broadcasted_iota(jnp.int32, (16, WIDE), 0)

    def some(step, total):
        part = pl.ds(pl.multiple_of(step * WIDE, WIDE), WIDE)
        place = place_ref[:, part]
        top = tops == place >> 5
        picked = [jnp.where(top, facts_ref[fact : fact + 1, part], 0.0) for fact in range(facts_ref.shape[0])]
        member = (names == place & 31).astype(jnp.float32).astype(jnp.bfloat16)
        return total + across(jnp.concatenate(picked, axis=0).astype(jnp.bfloat16), member)

    out_ref[...] = lax.fori_loop(0, place_ref.shape[1] // WIDE, some, jnp.zeros(out_ref.shape, jnp.float32))


def pick_facts(place, facts):
    count = facts.shape[0]
    picked = pl.pallas_call(
        facts_kernel,
        in_specs=whole(2),
        out_specs=whole(1)[0],
        out_shape=jax.ShapeDtypeStruct((count * 16, 32), jnp.float32),
        compiler_params=roomy(16),
        name="pick_facts",
        cost_estimate=light,
    )(place[None, :], facts)
    return picked.reshape(count, 16 * 32)[:, :WIRES]


def add(first, second):
    return (first[0] + second[0], first[1] + second[1])


def sub(first, second):
    return (first[0] - second[0], first[1] - second[1])


def turn(value, sign):
    if sign < 0:
        return (value[1], -value[0])
    return (-value[1], value[0])


def scaled(value, angle):
    real, imag = math.cos(angle), math.sin(angle)
    if abs(angle) < 1e-12:
        return value
    return (value[0] * real - value[1] * imag, value[0] * imag + value[1] * real)


def four_point(items, sign):
    even_sum, even_diff = add(items[0], items[2]), sub(items[0], items[2])
    odd_sum, odd_diff = add(items[1], items[3]), turn(sub(items[1], items[3]), sign)
    return [add(even_sum, odd_sum), add(even_diff, odd_diff), sub(even_sum, odd_sum), sub(even_diff, odd_diff)]


def eighth(value, count, sign):
    root = math.sqrt(0.5)
    if count == 0:
        return value
    if count == 2:
        return turn(value, sign)
    real, imag = value
    if count == 1:
        return ((real - sign * imag) * root, (imag + sign * real) * root)
    return ((-real - sign * imag) * root, (sign * real - imag) * root)


def eight_point(items, sign):
    even = four_point(items[0::2], sign)
    odd = four_point(items[1::2], sign)
    odd = [eighth(value, count, sign) for count, value in enumerate(odd)]
    return [add(even[k], odd[k]) for k in range(4)] + [sub(even[k], odd[k]) for k in range(4)]


def slab_points(load, store, middle_ref, sign):
    for low in range(8):
        outs = four_point([load(8 * high + low) for high in range(4)], sign)
        for k, value in enumerate(outs):
            value = scaled(value, sign * 2.0 * math.pi * low * k / 32)
            middle_ref[8 * k + low, 0] = value[0]
            middle_ref[8 * k + low, 1] = value[1]
    for k in range(4):
        outs = eight_point([(middle_ref[8 * k + low, 0], middle_ref[8 * k + low, 1]) for low in range(8)], sign)
        for big, value in enumerate(outs):
            store(k + 4 * big, value)


def tail_kernel(*refs):
    sources, refs = refs[:6], refs[6:]
    take_ref, good_ref, member_ref, high_ref, low_ref, real_hbm, imag_hbm, twist_ref = refs[:8]
    tick_high_ref, tick_low_ref, untick_high_ref, untick_low_ref, back_high_ref, back_low_ref = refs[8:14]
    out_hbm, held, refs = refs[14], refs[15:21], refs[21:]
    rows_ref, plane_ref, covar_ref, power_ref, middle_ref, real_ref, imag_ref, out_ref = refs[:8]
    fetched, filter_done, out_done = refs[8:]
    early, own0, own1, got0, got1, common_ref = held
    quarters = []
    for quarter in range(4):
        part = pl.ds(quarter * SLABS // 4, SLABS // 4)
        quarters.append(
            [
                pltpu.make_async_copy(source.at[part], target.at[part], fetched.at[index, quarter])
                for index, (source, target) in enumerate(zip(sources, held))
            ]
        )
    for copies in quarters:
        for copy in copies:
            copy.start()
    filter_copies = [
        pltpu.make_async_copy(real_hbm, real_ref, filter_done.at[0]),
        pltpu.make_async_copy(imag_hbm, imag_ref, filter_done.at[1]),
    ]
    for copy in filter_copies:
        copy.start()
    covar_ref[...] = jnp.zeros_like(covar_ref)
    power_ref[...] = jnp.zeros_like(power_ref)

    def both_commons(pair):
        return jnp.concatenate([common_ref[2 * pair], common_ref[2 * pair + 1]], axis=1)

    def spread_common(commons):
        high, low = split(commons)
        return dot(member_ref[...], high) + dot(member_ref[...], low)

    def spread_power(power):
        high, rest = split(power)
        middle = (power - high.astype(jnp.float32) - rest.astype(jnp.float32)).astype(jnp.bfloat16)
        return dot(member_ref[...], high) + (dot(member_ref[...], rest) + dot(member_ref[...], middle))

    def assemble(pair, carry):
        for half in range(2):
            slab = 2 * pair + half
            base = half * PART
            for piece in range(3):
                rows = slice(piece * EARLY_ROWS, (piece + 1) * EARLY_ROWS)
                value = early[slab]
                if piece:
                    value = pltpu.roll(value, PART - piece * EARLY, 1)
                rows_ref[pair, rows, base : base + PART] = value
            for which, (own, got) in enumerate(((own0, got0), (own1, got1))):
                sent = SENT[which]
                for piece in range(2):
                    part = slice(piece * LATE, (piece + 1) * LATE)
                    at = LATE_BASE[which] + piece * LATE_ROWS[which]
                    take = take_ref[at : at + sent, :] > 0.5
                    lanes = slice(base + EARLY, base + SLAB)
                    rows_ref[pair, at : at + sent, lanes] = jnp.where(take, got[slab, :, part], own[slab, 0:sent, part])
                    if sent < LATE_ROWS[which]:
                        rest = slice(at + sent, at + LATE_ROWS[which])
                        rows_ref[pair, rest, lanes] = own[slab, sent : LATE_ROWS[which], part]
        commons = both_commons(pair)
        covar_ref[...] += rows_ref[pair] * spread_common(commons)
        power_ref[...] += commons * commons
        return carry

    for quarter in range(4):
        for copy in quarters[quarter]:
            copy.wait()
        lax.fori_loop(quarter * SLABS // 8, (quarter + 1) * SLABS // 8, assemble, 0)
    covar = jnp.sum(covar_ref[...], axis=1, keepdims=True) / TICKS
    power = jnp.sum(power_ref[...], axis=1, keepdims=True) / TICKS
    power = spread_power(jnp.broadcast_to(power, (power.shape[0], PART)))[:, 0:1]
    weight = covar / (power + epsilon_power)

    def to_wires(pair, carry):
        cleaned = good_ref[...] * (rows_ref[pair] - weight * spread_common(both_commons(pair)))
        row_high, row_low = split(cleaned)
        result = three_dot(high_ref[...], low_ref[...], row_high, row_low)
        for slab in range(2):
            for part in range(2):
                plane_ref[2 * pair + slab, part] = result[
                    part * HALF : (part + 1) * HALF, slab * PART : (slab + 1) * PART
                ]
        return carry

    for pair in range(SLABS // 2):
        to_wires(pair, 0)

    def slabs_over(index, carry, sign):
        rows = pl.ds(pl.multiple_of(index * 8, 8), 8)

        def load(item):
            real, imag = plane_ref[item, 0, rows, :], plane_ref[item, 1, rows, :]
            if sign < 0:
                return (real, imag)
            cosine, sine = twist_ref[item, 0], twist_ref[item, 1]
            return (real * cosine - imag * sine, real * sine + imag * cosine)

        def store(item, value):
            real, imag = value
            if sign < 0:
                cosine, sine = twist_ref[item, 0], twist_ref[item, 1]
                real, imag = real * cosine + imag * sine, imag * cosine - real * sine
            plane_ref[item, 0, rows, :] = real
            plane_ref[item, 1, rows, :] = imag

        slab_points(load, store, middle_ref, sign)
        return carry

    lax.fori_loop(0, HALF // 8, functools.partial(slabs_over, sign=-1), 0)

    def filtered(item, carry):
        data_high, data_low = split(jnp.concatenate([plane_ref[item, 0], plane_ref[item, 1]], axis=1))
        spectrum = three_dot(data_high, data_low, tick_high_ref[...], tick_low_ref[...])
        real, imag = spectrum[:, :PART], spectrum[:, PART:]
        filter_real, filter_imag = real_ref[item], imag_ref[item]
        mixed = jnp.concatenate(
            [real * filter_real - imag * filter_imag, real * filter_imag + imag * filter_real], axis=1
        )
        mixed_high, mixed_low = split(mixed)
        result = three_dot(mixed_high, mixed_low, untick_high_ref[...], untick_low_ref[...])
        plane_ref[item, 0] = result[:, :PART]
        plane_ref[item, 1] = result[:, PART:]
        return carry

    for copy in filter_copies:
        copy.wait()
    lax.fori_loop(0, SLABS, filtered, 0, unroll=8)
    lax.fori_loop(0, HALF // 8, functools.partial(slabs_over, sign=1), 0)
    out_copies = []
    for pair in range(SLABS // 2):
        both = jnp.concatenate(
            [plane_ref[2 * pair + slab].reshape(2 * HALF, PART) for slab in range(2)], axis=1
        )
        data_high, data_low = split(both)
        result = three_dot(back_high_ref[...], back_low_ref[...], data_high, data_low)
        for slab in range(2):
            at = (2 * pair + slab) * SLAB
            out_ref[:, at : at + SLAB] = result[:, slab * PART : slab * PART + SLAB]
        while len(out_copies) < 5 and (len(out_copies) + 1) * OUT_PART <= (pair + 1) * 2 * SLAB:
            part = pl.ds(len(out_copies) * OUT_PART, OUT_PART)
            out_copies.append(pltpu.make_async_copy(out_ref.at[:, part], out_hbm.at[:, part], out_done.at[len(out_copies)]))
            out_copies[-1].start()
    for copy in out_copies:
        copy.wait()


def tail(early, own, got, take, good, commons, member, high, low, filters):
    back_high, back_low = two_halves(wire_tables()[1])
    tick, untick, twist = tick_tables()
    tables = (twist, *two_halves(tick), *two_halves(untick), back_high, back_low)
    moved = (early, *own, *got, commons)
    operands = (*moved, take, good, member, high, low, *filters, *tables)
    far = [pl.BlockSpec(memory_space=pltpu.HBM)]
    return pl.pallas_call(
        tail_kernel,
        in_specs=far * 6 + whole(5) + far * 2 + whole(len(tables)),
        out_specs=far[0],
        out_shape=jax.ShapeDtypeStruct((WIRES, TICKS), jnp.float32),
        scratch_shapes=[pltpu.VMEM(value.shape, jnp.float32) for value in moved]
        + [
            pltpu.VMEM((SLABS // 2, WIRES, HALF), jnp.float32),
            pltpu.VMEM((SLABS, 2, HALF, PART), jnp.float32),
            pltpu.VMEM((WIRES, HALF), jnp.float32),
            pltpu.VMEM((commons.shape[1], HALF), jnp.float32),
            pltpu.VMEM((SLABS, 2, 8, PART), jnp.float32),
            pltpu.VMEM((SLABS, HALF, PART), jnp.float32),
            pltpu.VMEM((SLABS, HALF, PART), jnp.float32),
            pltpu.VMEM((WIRES, TICKS), jnp.float32),
            pltpu.SemaphoreType.DMA((6, 4)),
            pltpu.SemaphoreType.DMA((2,)),
            pltpu.SemaphoreType.DMA((5,)),
        ],
        compiler_params=roomy(60),
        name="deconvolve",
    )(*operands)


def make_filter(wire_kernel, time_kernel):
    forward, _ = wire_tables()
    wire_resp = jnp.dot(forward.astype(np.float32), wire_kernel, precision=highest).reshape(2, 1, HALF, 1)
    first = np.arange(SLABS)
    angle = 2.0 * np.pi * (np.outer(first, first) % SLABS) / SLABS
    slabs = time_kernel.reshape(SLABS, SLAB)
    real = jnp.dot(np.cos(angle).astype(np.float32), slabs, precision=highest)
    imag = jnp.dot(-np.sin(angle).astype(np.float32), slabs, precision=highest)
    twist = 2.0 * np.pi * np.outer(first, np.arange(SLAB)) / TICKS
    cosine, sine = np.cos(twist).astype(np.float32), np.sin(twist).astype(np.float32)
    real, imag = real * cosine + imag * sine, imag * cosine - real * sine
    inner = np.arange(SLAB)
    angle = 2.0 * np.pi * (np.outer(inner, inner) % SLAB) / SLAB
    cosine, sine = np.cos(angle).astype(np.float32), np.sin(angle).astype(np.float32)
    both = jnp.dot(
        jnp.concatenate([real, imag], axis=1),
        np.block([[cosine, -sine], [sine, cosine]]).astype(np.float32),
        precision=highest,
    )
    time_resp = jnp.pad(both.reshape(SLABS, 2, SLAB), ((0, 0), (0, 0), (0, PART - SLAB)))
    time_real, time_imag = time_resp[:, 0][:, None, :], time_resp[:, 1][:, None, :]
    real = wire_resp[0] * time_real - wire_resp[1] * time_imag
    imag = wire_resp[0] * time_imag + wire_resp[1] * time_real
    denominator = real * real + imag * imag + regular_term
    return real / denominator, -imag / denominator


def picked_tables(wires):
    wire_high, wire_low = two_halves(wire_tables()[0])
    picked = (jnp.arange(WIRES, dtype=jnp.int32)[:, None] == wires[None, :]).astype(jnp.bfloat16)
    return dot(jnp.asarray(wire_high), picked).astype(jnp.bfloat16), dot(jnp.asarray(wire_low), picked).astype(
        jnp.bfloat16
    )


def shards(raw, bad, group_id, chan_plane, chan_wire, plane_offset, wire_kernel, time_kernel):
    chan_count = raw.shape[0]
    group_count = chan_count // GROUP
    apa_index = lax.axis_index("apa")
    tick_index = lax.axis_index("tick")
    parity = apa_index % 2
    swap = [(i, i ^ 1) for i in range(lax.axis_size("apa"))]
    raw_turned = raw.T
    early_got = lax.ppermute(raw_turned[:EARLY], "apa", swap)
    local_group = group_id - apa_index * group_count
    good_mask = 1.0 - bad.astype(jnp.float32)
    pair_base = (apa_index // 2 * 2 * SLABS).astype(jnp.int32)
    place, cross_count = rank_rows(chan_plane, pair_base, (1 - parity).astype(jnp.int32))
    place_got = lax.ppermute(place, "apa", swap)
    late0, rows = pack_rows(place, raw_turned)
    late0, later_place, later_raw = lax.optimization_barrier((late0, place, raw_turned))
    common = sum_groups(later_raw, local_group, good_mask)
    late1 = lay_late(rows, 1)

    def over_ticks(value):
        return lax.all_to_all(value, "tick", split_axis=0, concat_axis=0, tiled=True)

    own0 = over_ticks(late0)
    common_got = lax.ppermute(common, "apa", swap)
    facts = jnp.stack([chan_wire >> 5, chan_wire & 31, local_group, bad, chan_plane - pair_base])
    facts = pick_facts(later_place - tick_index * WIRES, facts.astype(jnp.float32)).astype(jnp.int32)
    own0, late1, early_got, common_got, facts = lax.optimization_barrier((own0, late1, early_got, common_got, facts))
    first = jnp.where(parity == 0, common, common_got)
    second = jnp.where(parity == 0, common_got, common)
    commons = lax.all_gather(jnp.concatenate([first, second], axis=0), "tick")
    own1 = over_ticks(late1)
    got0 = lax.ppermute(own0[:, : SENT[0]], "apa", swap)
    take = jnp.asarray(row_order()) < cross_count
    row_take = take.astype(jnp.float32)[:, None]
    early = merge_rows(place_got, early_got, rows, row_take)
    facts_got = lax.ppermute(facts, "apa", swap)
    early, got0, facts, facts_got, late_sent = lax.optimization_barrier(
        (early, got0, facts, facts_got, own1[:, : SENT[1]])
    )
    got1 = lax.ppermute(late_sent, "apa", swap)
    early = over_ticks(early)
    row_side = jnp.where(take, 1 - parity, parity)
    facts = jnp.where(take[None, :], facts_got, facts)
    row_offset = jnp.take(plane_offset, facts[4] + pair_base)
    row_wire = (facts[0] * 32 + facts[1] + row_offset) % WIRES
    row_group = facts[2] + row_side * group_count
    row_good = 1.0 - facts[3].astype(jnp.float32)[:, None]
    member = (row_group[:, None] == jnp.arange(2 * group_count, dtype=jnp.int32)[None, :]).astype(jnp.bfloat16)
    high, low = picked_tables(row_wire)
    filters = make_filter(wire_kernel, time_kernel)
    return tail(early, (own0, own1), (got0, got1), row_take, row_good, commons, member, high, low, filters)[None]


def solution(mesh):
    placed = (P("apa", "tick"), P("apa"), P("apa"), P("apa"), P("apa"), P(), P(), P())
    return jax.shard_map(
        shards,
        mesh=mesh,
        in_specs=placed,
        out_specs=P(("apa", "tick"), None, None),
        check_vma=False,
    )
```

```python
import functools
import math

import jax
import jax.numpy as jnp
import ml_dtypes
import numpy as np
from jax import lax
from jax.experimental import pallas as pl
from jax.experimental.pallas import tpu as pltpu
from jax.sharding import PartitionSpec as P

TICKS = 3200
GROUP = 128
WIRES = 480
SLABS = 32
SLAB = 100
PART = 128
HALF = 256
EARLY = 40
LATE = 60
EARLY_ROWS = 160
LATE_ROWS = (96, 144)
LATE_BASE = (0, 192)
BLOCK = 256
WIDE = 512
OUT_PART = 640
SENT = (96, 120)

highest = lax.Precision.HIGHEST
epsilon_power = 1e-06
regular_term = 0.25
mega = 1024 * 1024


light = pl.CostEstimate(flops=1, bytes_accessed=1, transcendentals=0)


def roomy(size):
    return pltpu.CompilerParams(vmem_limit_bytes=size * mega)


def two_halves(table):
    high = table.astype(ml_dtypes.bfloat16)
    low = (table - high.astype(np.float64)).astype(ml_dtypes.bfloat16)
    return high, low


def split(value):
    high = value.astype(jnp.bfloat16)
    low = (value - high.astype(jnp.float32)).astype(jnp.bfloat16)
    return high, low


def dot(left, right):
    return jnp.dot(left, right, preferred_element_type=jnp.float32)


def three_dot(left_high, left_low, right_high, right_low):
    return dot(left_high, right_high) + (dot(left_high, right_low) + dot(left_low, right_high))


def wire_tables():
    spread = np.outer(np.arange(WIRES // 2 + 1), np.arange(WIRES)) % WIRES
    angle = 2.0 * np.pi * spread / WIRES
    forward = np.zeros((2, HALF, WIRES))
    forward[0, : WIRES // 2 + 1] = np.cos(angle)
    forward[1, : WIRES // 2 + 1] = -np.sin(angle)
    weight = np.full((WIRES // 2 + 1, 1), 2.0)
    weight[0] = weight[-1] = 1.0
    weight /= WIRES * TICKS
    backward = np.zeros((2, HALF, WIRES))
    backward[0, : WIRES // 2 + 1] = weight * np.cos(angle)
    backward[1, : WIRES // 2 + 1] = -weight * np.sin(angle)
    return forward.reshape(2 * HALF, WIRES), backward.reshape(2 * HALF, WIRES).T.copy()


def tick_tables():
    angle = 2.0 * np.pi * (np.outer(np.arange(SLAB), np.arange(SLAB)) % SLAB) / SLAB
    table = np.zeros((2, PART, 2, PART))
    table[0, :SLAB, 0, :SLAB] = table[1, :SLAB, 1, :SLAB] = np.cos(angle)
    table[0, :SLAB, 1, :SLAB] = -np.sin(angle)
    table[1, :SLAB, 0, :SLAB] = np.sin(angle)
    table = table.reshape(HALF, HALF)
    twist = 2.0 * np.pi * np.outer(np.arange(SLABS), np.arange(PART)) / TICKS
    return table, table.T.copy(), np.stack([np.cos(twist), np.sin(twist)], axis=1).astype(np.float32)[:, :, None, :]


def row_order():
    row = np.arange(WIRES)
    piece = (row >= 336).astype(np.int32)
    place = row - 192 - 144 * piece
    late = np.where(place < 114, 192 + 114 * piece + place, 420 + 30 * piece + place - 114)
    return np.where(row < 192, row, late).astype(np.int32)


def rank_kernel(plane_ref, base_ref, cross_ref, raw_hbm, place_ref, count_ref, early_hbm, early_done):
    send = pltpu.make_async_copy(raw_hbm.at[pl.ds(0, EARLY)], early_hbm, early_done)
    send.start()
    tri_row = lax.broadcasted_iota(jnp.int32, (BLOCK, BLOCK), 0)
    tri_col = lax.broadcasted_iota(jnp.int32, (BLOCK, BLOCK), 1)
    earlier = (tri_row < tri_col).astype(jnp.float32).astype(jnp.bfloat16)
    names = lax.broadcasted_iota(jnp.int32, (2 * SLABS, BLOCK), 0)
    pair_base = base_ref[0]
    cross_side = cross_ref[0]
    chan_count = plane_ref.shape[1]
    local = plane_ref[...] - pair_base
    is_cross = (local // SLABS == cross_side).astype(jnp.float32)
    cross_count = jnp.sum(is_cross, axis=1, keepdims=True) * (1.0 / SLABS)
    before = jnp.zeros((2 * SLABS, 1), jnp.float32)
    for block in range(chan_count // BLOCK):
        part = slice(block * BLOCK, (block + 1) * BLOCK)
        member = (names == local[:, part]).astype(jnp.float32)
        prefix = dot(member.astype(jnp.bfloat16), earlier) + before
        rank = jnp.sum(member * prefix, axis=0, keepdims=True)
        before = before + jnp.sum(member, axis=1, keepdims=True)
        order = (rank + (1.0 - is_cross[:, part]) * cross_count).astype(jnp.int32)
        near_row = order + jnp.where(order >= 306, 30, 0)
        far_row = order - 114 + jnp.where(order >= 450, 114, 0)
        row = jnp.where(order < 192, order, jnp.where(order < 420, near_row, far_row))
        place_ref[:, part] = (local[:, part] % SLABS) * WIRES + row
    count_ref[...] = jnp.broadcast_to(cross_count.astype(jnp.int32), count_ref.shape)
    send.wait()


def rank_rows(chan_plane, pair_base, cross_side, raw_turned):
    chan_count = chan_plane.shape[0]
    scalar = pl.BlockSpec(memory_space=pltpu.SMEM)
    far = pl.BlockSpec(memory_space=pltpu.HBM)
    place, count, early = pl.pallas_call(
        rank_kernel,
        in_specs=whole(1) + [scalar, scalar, far],
        out_specs=whole(2) + [far],
        out_shape=[
            jax.ShapeDtypeStruct((1, chan_count), jnp.int32),
            jax.ShapeDtypeStruct((8, 128), jnp.int32),
            jax.ShapeDtypeStruct((EARLY, chan_count), jnp.float32),
        ],
        scratch_shapes=[pltpu.SemaphoreType.DMA],
        compiler_params=roomy(60),
        name="rank_rows",
    )(chan_plane[None, :], pair_base[None], cross_side[None], raw_turned)
    return place[0], count[0, 0], early


def whole(count):
    return [pl.BlockSpec(memory_space=pltpu.VMEM)] * count


def turned_scatter(place_ref, raw_ref, rows_ref, even_ref, odd_ref):
    ticks, chan_count = raw_ref.shape
    steps = chan_count // WIDE

    def turn_block(step, to_ref):
        at = pl.multiple_of(step * WIDE, WIDE)
        to_ref[:, 0:ticks] = raw_ref[:, pl.ds(at, WIDE)].T

    def move(step, from_ref):
        first = step * WIDE
        for row in range(WIDE):
            rows_ref[pl.ds(place_ref[first + row], 1), :] = from_ref[pl.ds(row, 1), :]

    turn_block(0, even_ref)

    def both(half, carry):
        turn_block(2 * half + 1, odd_ref)
        move(2 * half, even_ref)
        turn_block(jnp.minimum(2 * half + 2, steps - 2), even_ref)
        move(2 * half + 1, odd_ref)
        return carry

    lax.fori_loop(0, steps // 2, both, 0)


def late_kernel(which, rows_ref, out_ref, low=0, high=SLABS):
    size = LATE_ROWS[which]

    def one_slot(slot, carry):
        start = pl.multiple_of(slot * WIRES, 8)
        for piece in range(2):
            at = start + LATE_BASE[which] + piece * size
            out_ref[slot, :, piece * LATE : (piece + 1) * LATE] = rows_ref[pl.ds(at, size), EARLY:SLAB]
        return carry

    lax.fori_loop(low, high, one_slot, 0)


def late_shape(which):
    return jax.ShapeDtypeStruct((SLABS, LATE_ROWS[which], PART), jnp.float32)


def pack_kernel(place_ref, raw_ref, late_out, rows_out, rows_ref, late_ref, even_ref, odd_ref, rows_done, late_done):
    turned_scatter(place_ref, raw_ref, rows_ref, even_ref, odd_ref)
    keep = pltpu.make_async_copy(rows_ref, rows_out, rows_done)
    keep.start()
    late_kernel(0, rows_ref, late_ref)
    send = pltpu.make_async_copy(late_ref, late_out, late_done)
    send.start()
    keep.wait()
    send.wait()


def pack_rows(place, raw_turned):
    chan_count = raw_turned.shape[1]
    return pl.pallas_call(
        pack_kernel,
        in_specs=[pl.BlockSpec(memory_space=pltpu.SMEM)] + whole(1),
        out_specs=[pl.BlockSpec(memory_space=pltpu.HBM)] * 2,
        out_shape=[late_shape(0), jax.ShapeDtypeStruct((chan_count, PART), jnp.float32)],
        scratch_shapes=[
            pltpu.VMEM((chan_count, PART), jnp.float32),
            pltpu.VMEM((SLABS, LATE_ROWS[0], PART), jnp.float32),
        ]
        + [pltpu.VMEM((WIDE, PART), jnp.float32)] * 2
        + [pltpu.SemaphoreType.DMA] * 2,
        compiler_params=roomy(60),
        name="pack_rows",
    )(place, raw_turned)


def fetched_late_kernel(which, rows_hbm, out_ref, rows_ref, done_ref):
    quarter = rows_ref.shape[0] // 4
    copies = [
        pltpu.make_async_copy(
            rows_hbm.at[pl.ds(part * quarter, quarter)], rows_ref.at[pl.ds(part * quarter, quarter)], done_ref.at[part]
        )
        for part in range(4)
    ]
    for copy in copies:
        copy.start()
    for part, copy in enumerate(copies):
        copy.wait()
        late_kernel(which, rows_ref, out_ref, part * SLABS // 4, (part + 1) * SLABS // 4)


def lay_late(rows, which):
    return pl.pallas_call(
        functools.partial(fetched_late_kernel, which),
        in_specs=[pl.BlockSpec(memory_space=pltpu.HBM)],
        out_specs=whole(1)[0],
        out_shape=late_shape(which),
        scratch_shapes=[pltpu.VMEM(rows.shape, jnp.float32), pltpu.SemaphoreType.DMA((4,))],
        compiler_params=roomy(60),
        name="lay_late",
        cost_estimate=light,
    )(rows)


def merge_kernel(place_ref, raw_ref, own_hbm, take_ref, out_ref, rows_ref, even_ref, odd_ref, own_ref, own_done):
    fetch = pltpu.make_async_copy(own_hbm, own_ref, own_done)
    fetch.start()
    turned_scatter(place_ref, raw_ref, rows_ref, even_ref, odd_ref)
    fetch.wait()

    def one_slot(slot, carry):
        start = pl.multiple_of(slot * WIRES, 8)
        for piece in range(3):
            rows = pl.ds(start + piece * EARLY_ROWS, EARLY_ROWS)
            take = take_ref[piece * EARLY_ROWS : (piece + 1) * EARLY_ROWS, :] > 0.5
            value = jnp.where(take, rows_ref[rows, 0:EARLY], own_ref[rows, 0:EARLY])
            out_ref[slot, :, piece * EARLY : (piece + 1) * EARLY] = value
        out_ref[slot, :, 3 * EARLY : PART] = jnp.zeros((EARLY_ROWS, PART - 3 * EARLY), jnp.float32)
        return carry

    lax.fori_loop(0, SLABS, one_slot, 0)


def merge_rows(place, raw_turned, own, take):
    chan_count = raw_turned.shape[1]
    return pl.pallas_call(
        merge_kernel,
        in_specs=[pl.BlockSpec(memory_space=pltpu.SMEM)] + whole(1) + [pl.BlockSpec(memory_space=pltpu.HBM)] + whole(1),
        out_specs=whole(1)[0],
        out_shape=jax.ShapeDtypeStruct((SLABS, EARLY_ROWS, PART), jnp.float32),
        scratch_shapes=[pltpu.VMEM((chan_count, PART), jnp.float32)]
        + [pltpu.VMEM((WIDE, PART), jnp.float32)] * 2
        + [pltpu.VMEM((chan_count, PART), jnp.float32), pltpu.SemaphoreType.DMA],
        compiler_params=roomy(60),
        name="merge_rows",
    )(place, raw_turned, own, take)


def across(left, right):
    return lax.dot_general(left, right, (((1,), (1,)), ((), ())), preferred_element_type=jnp.float32)


def group_kernel(raw_ref, group_ref, good_ref, out_ref):
    group_count = out_ref.shape[0]
    names = lax.broadcasted_iota(jnp.int32, (group_count, WIDE), 0)

    def some(step, total):
        part = pl.ds(pl.multiple_of(step * WIDE, WIDE), WIDE)
        member = jnp.where(names == group_ref[:, part], good_ref[:, part], 0.0).astype(jnp.bfloat16)
        high, low = split(raw_ref[:, part])
        return total + (across(member, high) + across(member, low))

    zero = jnp.zeros((group_count, SLAB), jnp.float32)
    out_ref[...] = jnp.zeros_like(out_ref)
    out_ref[:, 0:SLAB] = lax.fori_loop(0, raw_ref.shape[1] // WIDE, some, zero)


def sum_groups(raw_turned, local_group, good_mask):
    group_count = raw_turned.shape[1] // GROUP
    return pl.pallas_call(
        group_kernel,
        in_specs=whole(3),
        out_specs=whole(1)[0],
        out_shape=jax.ShapeDtypeStruct((group_count, PART), jnp.float32),
        compiler_params=roomy(24),
        name="sum_groups",
        cost_estimate=light,
    )(raw_turned, local_group[None, :], good_mask[None, :])


def facts_kernel(place_ref, facts_ref, out_ref):
    names = lax.broadcasted_iota(jnp.int32, (32, WIDE), 0)
    tops = lax.broadcasted_iota(jnp.int32, (16, WIDE), 0)

    def some(step, total):
        part = pl.ds(pl.multiple_of(step * WIDE, WIDE), WIDE)
        place = place_ref[:, part]
        top = tops == place >> 5
        picked = [jnp.where(top, facts_ref[fact : fact + 1, part], 0.0) for fact in range(facts_ref.shape[0])]
        member = (names == place & 31).astype(jnp.float32).astype(jnp.bfloat16)
        return total + across(jnp.concatenate(picked, axis=0).astype(jnp.bfloat16), member)

    out_ref[...] = lax.fori_loop(0, place_ref.shape[1] // WIDE, some, jnp.zeros(out_ref.shape, jnp.float32))


def pick_facts(place, facts):
    count = facts.shape[0]
    picked = pl.pallas_call(
        facts_kernel,
        in_specs=whole(2),
        out_specs=whole(1)[0],
        out_shape=jax.ShapeDtypeStruct((count * 16, 32), jnp.float32),
        compiler_params=roomy(16),
        name="pick_facts",
        cost_estimate=light,
    )(place[None, :], facts)
    return picked.reshape(count, 16 * 32)[:, :WIRES]


def add(first, second):
    return (first[0] + second[0], first[1] + second[1])


def sub(first, second):
    return (first[0] - second[0], first[1] - second[1])


def turn(value, sign):
    if sign < 0:
        return (value[1], -value[0])
    return (-value[1], value[0])


def scaled(value, angle):
    real, imag = math.cos(angle), math.sin(angle)
    if abs(angle) < 1e-12:
        return value
    return (value[0] * real - value[1] * imag, value[0] * imag + value[1] * real)


def four_point(items, sign):
    even_sum, even_diff = add(items[0], items[2]), sub(items[0], items[2])
    odd_sum, odd_diff = add(items[1], items[3]), turn(sub(items[1], items[3]), sign)
    return [add(even_sum, odd_sum), add(even_diff, odd_diff), sub(even_sum, odd_sum), sub(even_diff, odd_diff)]


def eighth(value, count, sign):
    root = math.sqrt(0.5)
    if count == 0:
        return value
    if count == 2:
        return turn(value, sign)
    real, imag = value
    if count == 1:
        return ((real - sign * imag) * root, (imag + sign * real) * root)
    return ((-real - sign * imag) * root, (sign * real - imag) * root)


def eight_point(items, sign):
    even = four_point(items[0::2], sign)
    odd = four_point(items[1::2], sign)
    odd = [eighth(value, count, sign) for count, value in enumerate(odd)]
    return [add(even[k], odd[k]) for k in range(4)] + [sub(even[k], odd[k]) for k in range(4)]


def slab_points(load, store, middle_ref, sign):
    for low in range(8):
        outs = four_point([load(8 * high + low) for high in range(4)], sign)
        for k, value in enumerate(outs):
            value = scaled(value, sign * 2.0 * math.pi * low * k / 32)
            middle_ref[8 * k + low, 0] = value[0]
            middle_ref[8 * k + low, 1] = value[1]
    for k in range(4):
        outs = eight_point([(middle_ref[8 * k + low, 0], middle_ref[8 * k + low, 1]) for low in range(8)], sign)
        for big, value in enumerate(outs):
            store(k + 4 * big, value)


def tail_kernel(*refs):
    sources, got1, refs = refs[:5], refs[5], refs[6:]
    take_ref, good_ref, member_ref, high_ref, low_ref, real_hbm, imag_hbm, twist_ref = refs[:8]
    tick_high_ref, tick_low_ref, untick_high_ref, untick_low_ref, back_high_ref, back_low_ref = refs[8:14]
    out_hbm, held, refs = refs[14], refs[15:20], refs[20:]
    rows_ref, plane_ref, covar_ref, power_ref, middle_ref, real_ref, imag_ref, out_ref = refs[:8]
    fetched, filter_done, out_done = refs[8:]
    early, own0, own1, got0, common_ref = held
    quarters = []
    for quarter in range(4):
        part = pl.ds(quarter * SLABS // 4, SLABS // 4)
        quarters.append(
            [
                pltpu.make_async_copy(source.at[part], target.at[part], fetched.at[index, quarter])
                for index, (source, target) in enumerate(zip(sources, held))
            ]
        )
    for copies in quarters:
        for copy in copies:
            copy.start()
    filter_copies = [
        pltpu.make_async_copy(real_hbm, real_ref, filter_done.at[0]),
        pltpu.make_async_copy(imag_hbm, imag_ref, filter_done.at[1]),
    ]
    for copy in filter_copies:
        copy.start()
    covar_ref[...] = jnp.zeros_like(covar_ref)
    power_ref[...] = jnp.zeros_like(power_ref)

    def both_commons(pair):
        return jnp.concatenate([common_ref[2 * pair], common_ref[2 * pair + 1]], axis=1)

    def spread_common(commons):
        high, low = split(commons)
        return dot(member_ref[...], high) + dot(member_ref[...], low)

    def spread_power(power):
        high, rest = split(power)
        middle = (power - high.astype(jnp.float32) - rest.astype(jnp.float32)).astype(jnp.bfloat16)
        return dot(member_ref[...], high) + (dot(member_ref[...], rest) + dot(member_ref[...], middle))

    def assemble(pair, carry):
        for half in range(2):
            slab = 2 * pair + half
            base = half * PART
            for piece in range(3):
                rows = slice(piece * EARLY_ROWS, (piece + 1) * EARLY_ROWS)
                value = early[slab]
                if piece:
                    value = pltpu.roll(value, PART - piece * EARLY, 1)
                rows_ref[pair, rows, base : base + PART] = value
            for which, (own, got) in enumerate(((own0, got0), (own1, got1))):
                sent = SENT[which]
                for piece in range(2):
                    part = slice(piece * LATE, (piece + 1) * LATE)
                    at = LATE_BASE[which] + piece * LATE_ROWS[which]
                    take = take_ref[at : at + sent, :] > 0.5
                    lanes = slice(base + EARLY, base + SLAB)
                    rows_ref[pair, at : at + sent, lanes] = jnp.where(take, got[slab, :, part], own[slab, 0:sent, part])
                    if sent < LATE_ROWS[which]:
                        rest = slice(at + sent, at + LATE_ROWS[which])
                        rows_ref[pair, rest, lanes] = own[slab, sent : LATE_ROWS[which], part]
        commons = both_commons(pair)
        covar_ref[...] += rows_ref[pair] * spread_common(commons)
        power_ref[...] += commons * commons
        return carry

    for quarter in range(4):
        for copy in quarters[quarter]:
            copy.wait()
        lax.fori_loop(quarter * SLABS // 8, (quarter + 1) * SLABS // 8, assemble, 0)
    covar = jnp.sum(covar_ref[...], axis=1, keepdims=True) / TICKS
    power = jnp.sum(power_ref[...], axis=1, keepdims=True) / TICKS
    power = spread_power(jnp.broadcast_to(power, (power.shape[0], PART)))[:, 0:1]
    weight = covar / (power + epsilon_power)

    def to_wires(pair, carry):
        cleaned = good_ref[...] * (rows_ref[pair] - weight * spread_common(both_commons(pair)))
        row_high, row_low = split(cleaned)
        result = three_dot(high_ref[...], low_ref[...], row_high, row_low)
        for slab in range(2):
            for part in range(2):
                plane_ref[2 * pair + slab, part] = result[
                    part * HALF : (part + 1) * HALF, slab * PART : (slab + 1) * PART
                ]
        return carry

    for pair in range(SLABS // 2):
        to_wires(pair, 0)

    def slabs_over(index, carry, sign):
        rows = pl.ds(pl.multiple_of(index * 8, 8), 8)

        def load(item):
            real, imag = plane_ref[item, 0, rows, :], plane_ref[item, 1, rows, :]
            if sign < 0:
                return (real, imag)
            cosine, sine = twist_ref[item, 0], twist_ref[item, 1]
            return (real * cosine - imag * sine, real * sine + imag * cosine)

        def store(item, value):
            real, imag = value
            if sign < 0:
                cosine, sine = twist_ref[item, 0], twist_ref[item, 1]
                real, imag = real * cosine + imag * sine, imag * cosine - real * sine
            plane_ref[item, 0, rows, :] = real
            plane_ref[item, 1, rows, :] = imag

        slab_points(load, store, middle_ref, sign)
        return carry

    lax.fori_loop(0, HALF // 8, functools.partial(slabs_over, sign=-1), 0, unroll=2)

    def filtered(item, carry):
        data_high, data_low = split(jnp.concatenate([plane_ref[item, 0], plane_ref[item, 1]], axis=1))
        spectrum = three_dot(data_high, data_low, tick_high_ref[...], tick_low_ref[...])
        real, imag = spectrum[:, :PART], spectrum[:, PART:]
        filter_real, filter_imag = real_ref[item], imag_ref[item]
        mixed = jnp.concatenate(
            [real * filter_real - imag * filter_imag, real * filter_imag + imag * filter_real], axis=1
        )
        mixed_high, mixed_low = split(mixed)
        result = three_dot(mixed_high, mixed_low, untick_high_ref[...], untick_low_ref[...])
        plane_ref[item, 0] = result[:, :PART]
        plane_ref[item, 1] = result[:, PART:]
        return carry

    for copy in filter_copies:
        copy.wait()
    lax.fori_loop(0, SLABS, filtered, 0, unroll=16)
    lax.fori_loop(0, HALF // 8, functools.partial(slabs_over, sign=1), 0, unroll=2)
    out_copies = []
    for pair in range(SLABS // 2):
        both = jnp.concatenate(
            [plane_ref[2 * pair + slab].reshape(2 * HALF, PART) for slab in range(2)], axis=1
        )
        data_high, data_low = split(both)
        result = three_dot(back_high_ref[...], back_low_ref[...], data_high, data_low)
        for slab in range(2):
            at = (2 * pair + slab) * SLAB
            out_ref[:, at : at + SLAB] = result[:, slab * PART : slab * PART + SLAB]
        while len(out_copies) < 5 and (len(out_copies) + 1) * OUT_PART <= (pair + 1) * 2 * SLAB:
            part = pl.ds(len(out_copies) * OUT_PART, OUT_PART)
            out_copies.append(pltpu.make_async_copy(out_ref.at[:, part], out_hbm.at[:, part], out_done.at[len(out_copies)]))
            out_copies[-1].start()
    for copy in out_copies:
        copy.wait()


def tail(early, own, got, take, good, commons, member, high, low, filters):
    back_high, back_low = two_halves(wire_tables()[1])
    tick, untick, twist = tick_tables()
    tables = (twist, *two_halves(tick), *two_halves(untick), back_high, back_low)
    moved = (early, *own, got[0], commons)
    operands = (*moved, got[1], take, good, member, high, low, *filters, *tables)
    far = [pl.BlockSpec(memory_space=pltpu.HBM)]
    return pl.pallas_call(
        tail_kernel,
        in_specs=far * 5 + whole(6) + far * 2 + whole(len(tables)),
        out_specs=far[0],
        out_shape=jax.ShapeDtypeStruct((WIRES, TICKS), jnp.float32),
        scratch_shapes=[pltpu.VMEM(value.shape, jnp.float32) for value in moved]
        + [
            pltpu.VMEM((SLABS // 2, WIRES, HALF), jnp.float32),
            pltpu.VMEM((SLABS, 2, HALF, PART), jnp.float32),
            pltpu.VMEM((WIRES, HALF), jnp.float32),
            pltpu.VMEM((commons.shape[1], HALF), jnp.float32),
            pltpu.VMEM((SLABS, 2, 8, PART), jnp.float32),
            pltpu.VMEM((SLABS, HALF, PART), jnp.float32),
            pltpu.VMEM((SLABS, HALF, PART), jnp.float32),
            pltpu.VMEM((WIRES, TICKS), jnp.float32),
            pltpu.SemaphoreType.DMA((5, 4)),
            pltpu.SemaphoreType.DMA((2,)),
            pltpu.SemaphoreType.DMA((5,)),
        ],
        compiler_params=roomy(48),
        name="deconvolve",
    )(*operands)


def make_filter(wire_kernel, time_kernel):
    forward, _ = wire_tables()
    wire_resp = jnp.dot(forward.astype(np.float32), wire_kernel, precision=highest).reshape(2, 1, HALF, 1)
    first = np.arange(SLABS)
    angle = 2.0 * np.pi * (np.outer(first, first) % SLABS) / SLABS
    slabs = time_kernel.reshape(SLABS, SLAB)
    real = jnp.dot(np.cos(angle).astype(np.float32), slabs, precision=highest)
    imag = jnp.dot(-np.sin(angle).astype(np.float32), slabs, precision=highest)
    twist = 2.0 * np.pi * np.outer(first, np.arange(SLAB)) / TICKS
    cosine, sine = np.cos(twist).astype(np.float32), np.sin(twist).astype(np.float32)
    real, imag = real * cosine + imag * sine, imag * cosine - real * sine
    inner = np.arange(SLAB)
    angle = 2.0 * np.pi * (np.outer(inner, inner) % SLAB) / SLAB
    cosine, sine = np.cos(angle).astype(np.float32), np.sin(angle).astype(np.float32)
    both = jnp.dot(
        jnp.concatenate([real, imag], axis=1),
        np.block([[cosine, -sine], [sine, cosine]]).astype(np.float32),
        precision=highest,
    )
    time_resp = jnp.pad(both.reshape(SLABS, 2, SLAB), ((0, 0), (0, 0), (0, PART - SLAB)))
    time_real, time_imag = time_resp[:, 0][:, None, :], time_resp[:, 1][:, None, :]
    real = wire_resp[0] * time_real - wire_resp[1] * time_imag
    imag = wire_resp[0] * time_imag + wire_resp[1] * time_real
    denominator = real * real + imag * imag + regular_term
    return real / denominator, -imag / denominator


def picked_tables(wires):
    wire_high, wire_low = two_halves(wire_tables()[0])
    picked = (jnp.arange(WIRES, dtype=jnp.int32)[:, None] == wires[None, :]).astype(jnp.bfloat16)
    return dot(jnp.asarray(wire_high), picked).astype(jnp.bfloat16), dot(jnp.asarray(wire_low), picked).astype(
        jnp.bfloat16
    )


def shards(raw, bad, group_id, chan_plane, chan_wire, plane_offset, wire_kernel, time_kernel):
    chan_count = raw.shape[0]
    group_count = chan_count // GROUP
    apa_index = lax.axis_index("apa")
    tick_index = lax.axis_index("tick")
    parity = apa_index % 2
    swap = [(i, i ^ 1) for i in range(lax.axis_size("apa"))]
    raw_turned = raw.T
    local_group = group_id - apa_index * group_count
    good_mask = 1.0 - bad.astype(jnp.float32)
    pair_base = (apa_index // 2 * 2 * SLABS).astype(jnp.int32)
    place, cross_count, early_sent = rank_rows(chan_plane, pair_base, (1 - parity).astype(jnp.int32), raw_turned)
    early_got = lax.ppermute(early_sent, "apa", swap)
    place_got = lax.ppermute(place, "apa", swap)
    late0, rows = pack_rows(place, raw_turned)
    late0, later_place, later_raw = lax.optimization_barrier((late0, place, raw_turned))
    common = sum_groups(later_raw, local_group, good_mask)
    late1 = lay_late(rows, 1)

    def over_ticks(value):
        return lax.all_to_all(value, "tick", split_axis=0, concat_axis=0, tiled=True)

    own0 = over_ticks(late0)
    common_got = lax.ppermute(common, "apa", swap)
    facts = jnp.stack([chan_wire >> 5, chan_wire & 31, local_group, bad, chan_plane - pair_base])
    facts = pick_facts(later_place - tick_index * WIRES, facts.astype(jnp.float32)).astype(jnp.int32)
    own0, late1, early_got, common_got, facts = lax.optimization_barrier((own0, late1, early_got, common_got, facts))
    first = jnp.where(parity == 0, common, common_got)
    second = jnp.where(parity == 0, common_got, common)
    commons = lax.all_gather(jnp.concatenate([first, second], axis=0), "tick")
    own1 = over_ticks(late1)
    got0 = lax.ppermute(own0[:, : SENT[0]], "apa", swap)
    take = jnp.asarray(row_order()) < cross_count
    row_take = take.astype(jnp.float32)[:, None]
    early = merge_rows(place_got, early_got, rows, row_take)
    facts_got = lax.ppermute(facts, "apa", swap)
    early, got0, facts, facts_got, late_sent = lax.optimization_barrier(
        (early, got0, facts, facts_got, own1[:, : SENT[1]])
    )
    got1 = lax.ppermute(late_sent, "apa", swap)
    early = over_ticks(early)
    row_side = jnp.where(take, 1 - parity, parity)
    facts = jnp.where(take[None, :], facts_got, facts)
    row_offset = jnp.take(plane_offset, facts[4] + pair_base)
    row_wire = (facts[0] * 32 + facts[1] + row_offset) % WIRES
    row_group = facts[2] + row_side * group_count
    row_good = 1.0 - facts[3].astype(jnp.float32)[:, None]
    member = (row_group[:, None] == jnp.arange(2 * group_count, dtype=jnp.int32)[None, :]).astype(jnp.bfloat16)
    high, low = picked_tables(row_wire)
    filters = make_filter(wire_kernel, time_kernel)
    return tail(early, (own0, own1), (got0, got1), row_take, row_good, commons, member, high, low, filters)[None]


def solution(mesh):
    placed = (P("apa", "tick"), P("apa"), P("apa"), P("apa"), P("apa"), P(), P(), P())
    return jax.shard_map(
        shards,
        mesh=mesh,
        in_specs=placed,
        out_specs=P(("apa", "tick"), None, None),
        check_vma=False,
    )
```

```python
import functools
import math

import jax
import jax.numpy as jnp
import ml_dtypes
import numpy as np
from jax import lax
from jax.experimental import pallas as pl
from jax.experimental.pallas import tpu as pltpu
from jax.sharding import PartitionSpec as P

TICKS = 3200
GROUP = 128
WIRES = 480
SLABS = 32
SLAB = 100
PART = 128
HALF = 256
EARLY = 40
LATE = 60
EARLY_ROWS = 160
LATE_ROWS = (96, 144)
LATE_BASE = (0, 192)
BLOCK = 256
WIDE = 512
OUT_PART = 640
SENT = (96, 120)

highest = lax.Precision.HIGHEST
epsilon_power = 1e-06
regular_term = 0.25
mega = 1024 * 1024


light = pl.CostEstimate(flops=1, bytes_accessed=1, transcendentals=0)


def roomy(size):
    return pltpu.CompilerParams(vmem_limit_bytes=size * mega)


def two_halves(table):
    high = table.astype(ml_dtypes.bfloat16)
    low = (table - high.astype(np.float64)).astype(ml_dtypes.bfloat16)
    return high, low


def split(value):
    high = value.astype(jnp.bfloat16)
    low = (value - high.astype(jnp.float32)).astype(jnp.bfloat16)
    return high, low


def dot(left, right):
    return jnp.dot(left, right, preferred_element_type=jnp.float32)


def three_dot(left_high, left_low, right_high, right_low):
    return dot(left_high, right_high) + (dot(left_high, right_low) + dot(left_low, right_high))


def wire_tables():
    spread = np.outer(np.arange(WIRES // 2 + 1), np.arange(WIRES)) % WIRES
    angle = 2.0 * np.pi * spread / WIRES
    forward = np.zeros((2, HALF, WIRES))
    forward[0, : WIRES // 2 + 1] = np.cos(angle)
    forward[1, : WIRES // 2 + 1] = -np.sin(angle)
    weight = np.full((WIRES // 2 + 1, 1), 2.0)
    weight[0] = weight[-1] = 1.0
    weight /= WIRES * TICKS
    backward = np.zeros((2, HALF, WIRES))
    backward[0, : WIRES // 2 + 1] = weight * np.cos(angle)
    backward[1, : WIRES // 2 + 1] = -weight * np.sin(angle)
    return forward.reshape(2 * HALF, WIRES), backward.reshape(2 * HALF, WIRES).T.copy()


def tick_tables():
    angle = 2.0 * np.pi * (np.outer(np.arange(SLAB), np.arange(SLAB)) % SLAB) / SLAB
    table = np.zeros((2, PART, 2, PART))
    table[0, :SLAB, 0, :SLAB] = table[1, :SLAB, 1, :SLAB] = np.cos(angle)
    table[0, :SLAB, 1, :SLAB] = -np.sin(angle)
    table[1, :SLAB, 0, :SLAB] = np.sin(angle)
    table = table.reshape(HALF, HALF)
    twist = 2.0 * np.pi * np.outer(np.arange(SLABS), np.arange(PART)) / TICKS
    return table, table.T.copy(), np.stack([np.cos(twist), np.sin(twist)], axis=1).astype(np.float32)[:, :, None, :]


def row_order():
    row = np.arange(WIRES)
    piece = (row >= 336).astype(np.int32)
    place = row - 192 - 144 * piece
    late = np.where(place < 114, 192 + 114 * piece + place, 420 + 30 * piece + place - 114)
    return np.where(row < 192, row, late).astype(np.int32)


def rank_kernel(plane_ref, base_ref, cross_ref, raw_hbm, place_ref, count_ref, early_hbm, early_ref, early_done):
    fetch = pltpu.make_async_copy(raw_hbm.at[pl.ds(0, EARLY)], early_ref, early_done.at[0])
    fetch.start()
    tri_row = lax.broadcasted_iota(jnp.int32, (BLOCK, BLOCK), 0)
    tri_col = lax.broadcasted_iota(jnp.int32, (BLOCK, BLOCK), 1)
    fetch.wait()
    send = pltpu.make_async_copy(early_ref, early_hbm, early_done.at[1])
    send.start()
    earlier = (tri_row < tri_col).astype(jnp.float32).astype(jnp.bfloat16)
    names = lax.broadcasted_iota(jnp.int32, (2 * SLABS, BLOCK), 0)
    pair_base = base_ref[0]
    cross_side = cross_ref[0]
    chan_count = plane_ref.shape[1]
    local = plane_ref[...] - pair_base
    is_cross = (local // SLABS == cross_side).astype(jnp.float32)
    cross_count = jnp.sum(is_cross, axis=1, keepdims=True) * (1.0 / SLABS)
    before = jnp.zeros((2 * SLABS, 1), jnp.float32)
    for block in range(chan_count // BLOCK):
        part = slice(block * BLOCK, (block + 1) * BLOCK)
        member = (names == local[:, part]).astype(jnp.float32)
        prefix = dot(member.astype(jnp.bfloat16), earlier) + before
        rank = jnp.sum(member * prefix, axis=0, keepdims=True)
        before = before + jnp.sum(member, axis=1, keepdims=True)
        order = (rank + (1.0 - is_cross[:, part]) * cross_count).astype(jnp.int32)
        near_row = order + jnp.where(order >= 306, 30, 0)
        far_row = order - 114 + jnp.where(order >= 450, 114, 0)
        row = jnp.where(order < 192, order, jnp.where(order < 420, near_row, far_row))
        place_ref[:, part] = (local[:, part] % SLABS) * WIRES + row
    count_ref[...] = jnp.broadcast_to(cross_count.astype(jnp.int32), count_ref.shape)
    send.wait()


def rank_rows(chan_plane, pair_base, cross_side, raw_turned):
    chan_count = chan_plane.shape[0]
    scalar = pl.BlockSpec(memory_space=pltpu.SMEM)
    far = pl.BlockSpec(memory_space=pltpu.HBM)
    place, count, early = pl.pallas_call(
        rank_kernel,
        in_specs=whole(1) + [scalar, scalar, far],
        out_specs=whole(2) + [far],
        out_shape=[
            jax.ShapeDtypeStruct((1, chan_count), jnp.int32),
            jax.ShapeDtypeStruct((8, 128), jnp.int32),
            jax.ShapeDtypeStruct((EARLY, chan_count), jnp.float32),
        ],
        scratch_shapes=[pltpu.VMEM((EARLY, chan_count), jnp.float32), pltpu.SemaphoreType.DMA((2,))],
        compiler_params=roomy(60),
        name="rank_rows",
    )(chan_plane[None, :], pair_base[None], cross_side[None], raw_turned)
    return place[0], count[0, 0], early


def whole(count):
    return [pl.BlockSpec(memory_space=pltpu.VMEM)] * count


def turned_scatter(place_ref, raw_ref, rows_ref, even_ref, odd_ref):
    ticks, chan_count = raw_ref.shape
    steps = chan_count // WIDE

    def turn_block(step, to_ref):
        at = pl.multiple_of(step * WIDE, WIDE)
        to_ref[:, 0:ticks] = raw_ref[:, pl.ds(at, WIDE)].T

    def move(step, from_ref):
        first = step * WIDE
        for row in range(WIDE):
            rows_ref[pl.ds(place_ref[first + row], 1), :] = from_ref[pl.ds(row, 1), :]

    turn_block(0, even_ref)

    def both(half, carry):
        turn_block(2 * half + 1, odd_ref)
        move(2 * half, even_ref)
        turn_block(jnp.minimum(2 * half + 2, steps - 2), even_ref)
        move(2 * half + 1, odd_ref)
        return carry

    lax.fori_loop(0, steps // 2, both, 0)


def late_kernel(which, rows_ref, out_ref, low=0, high=SLABS):
    size = LATE_ROWS[which]

    def one_slot(slot, carry):
        start = pl.multiple_of(slot * WIRES, 8)
        for piece in range(2):
            at = start + LATE_BASE[which] + piece * size
            out_ref[slot, :, piece * LATE : (piece + 1) * LATE] = rows_ref[pl.ds(at, size), EARLY:SLAB]
        return carry

    lax.fori_loop(low, high, one_slot, 0)


def late_shape(which):
    return jax.ShapeDtypeStruct((SLABS, LATE_ROWS[which], PART), jnp.float32)


def pack_kernel(place_ref, raw_ref, late_out, rows_out, rows_ref, late_ref, even_ref, odd_ref, rows_done, late_done):
    turned_scatter(place_ref, raw_ref, rows_ref, even_ref, odd_ref)
    keep = pltpu.make_async_copy(rows_ref, rows_out, rows_done)
    keep.start()
    late_kernel(0, rows_ref, late_ref)
    send = pltpu.make_async_copy(late_ref, late_out, late_done)
    send.start()
    keep.wait()
    send.wait()


def pack_rows(place, raw_turned):
    chan_count = raw_turned.shape[1]
    return pl.pallas_call(
        pack_kernel,
        in_specs=[pl.BlockSpec(memory_space=pltpu.SMEM)] + whole(1),
        out_specs=[pl.BlockSpec(memory_space=pltpu.HBM)] * 2,
        out_shape=[late_shape(0), jax.ShapeDtypeStruct((chan_count, PART), jnp.float32)],
        scratch_shapes=[
            pltpu.VMEM((chan_count, PART), jnp.float32),
            pltpu.VMEM((SLABS, LATE_ROWS[0], PART), jnp.float32),
        ]
        + [pltpu.VMEM((WIDE, PART), jnp.float32)] * 2
        + [pltpu.SemaphoreType.DMA] * 2,
        compiler_params=roomy(60),
        name="pack_rows",
    )(place, raw_turned)


def fetched_late_kernel(which, rows_hbm, out_ref, rows_ref, done_ref):
    quarter = rows_ref.shape[0] // 4
    copies = [
        pltpu.make_async_copy(
            rows_hbm.at[pl.ds(part * quarter, quarter)], rows_ref.at[pl.ds(part * quarter, quarter)], done_ref.at[part]
        )
        for part in range(4)
    ]
    for copy in copies:
        copy.start()
    for part, copy in enumerate(copies):
        copy.wait()
        late_kernel(which, rows_ref, out_ref, part * SLABS // 4, (part + 1) * SLABS // 4)


def lay_late(rows, which):
    return pl.pallas_call(
        functools.partial(fetched_late_kernel, which),
        in_specs=[pl.BlockSpec(memory_space=pltpu.HBM)],
        out_specs=whole(1)[0],
        out_shape=late_shape(which),
        scratch_shapes=[pltpu.VMEM(rows.shape, jnp.float32), pltpu.SemaphoreType.DMA((4,))],
        compiler_params=roomy(60),
        name="lay_late",
        cost_estimate=light,
    )(rows)


def merge_kernel(place_ref, raw_ref, own_hbm, take_ref, out_ref, rows_ref, even_ref, odd_ref, own_ref, own_done):
    fetch = pltpu.make_async_copy(own_hbm, own_ref, own_done)
    fetch.start()
    turned_scatter(place_ref, raw_ref, rows_ref, even_ref, odd_ref)
    fetch.wait()

    def one_slot(slot, carry):
        start = pl.multiple_of(slot * WIRES, 8)
        for piece in range(3):
            rows = pl.ds(start + piece * EARLY_ROWS, EARLY_ROWS)
            take = take_ref[piece * EARLY_ROWS : (piece + 1) * EARLY_ROWS, :] > 0.5
            value = jnp.where(take, rows_ref[rows, 0:EARLY], own_ref[rows, 0:EARLY])
            out_ref[slot, :, piece * EARLY : (piece + 1) * EARLY] = value
        out_ref[slot, :, 3 * EARLY : PART] = jnp.zeros((EARLY_ROWS, PART - 3 * EARLY), jnp.float32)
        return carry

    lax.fori_loop(0, SLABS, one_slot, 0)


def merge_rows(place, raw_turned, own, take):
    chan_count = raw_turned.shape[1]
    return pl.pallas_call(
        merge_kernel,
        in_specs=[pl.BlockSpec(memory_space=pltpu.SMEM)] + whole(1) + [pl.BlockSpec(memory_space=pltpu.HBM)] + whole(1),
        out_specs=whole(1)[0],
        out_shape=jax.ShapeDtypeStruct((SLABS, EARLY_ROWS, PART), jnp.float32),
        scratch_shapes=[pltpu.VMEM((chan_count, PART), jnp.float32)]
        + [pltpu.VMEM((WIDE, PART), jnp.float32)] * 2
        + [pltpu.VMEM((chan_count, PART), jnp.float32), pltpu.SemaphoreType.DMA],
        compiler_params=roomy(60),
        name="merge_rows",
    )(place, raw_turned, own, take)


def across(left, right):
    return lax.dot_general(left, right, (((1,), (1,)), ((), ())), preferred_element_type=jnp.float32)


def group_kernel(raw_ref, group_ref, good_ref, out_ref):
    group_count = out_ref.shape[0]
    names = lax.broadcasted_iota(jnp.int32, (group_count, WIDE), 0)

    def some(step, total):
        part = pl.ds(pl.multiple_of(step * WIDE, WIDE), WIDE)
        member = jnp.where(names == group_ref[:, part], good_ref[:, part], 0.0).astype(jnp.bfloat16)
        high, low = split(raw_ref[:, part])
        return total + (across(member, high) + across(member, low))

    zero = jnp.zeros((group_count, SLAB), jnp.float32)
    out_ref[...] = jnp.zeros_like(out_ref)
    out_ref[:, 0:SLAB] = lax.fori_loop(0, raw_ref.shape[1] // WIDE, some, zero)


def sum_groups(raw_turned, local_group, good_mask):
    group_count = raw_turned.shape[1] // GROUP
    return pl.pallas_call(
        group_kernel,
        in_specs=whole(3),
        out_specs=whole(1)[0],
        out_shape=jax.ShapeDtypeStruct((group_count, PART), jnp.float32),
        compiler_params=roomy(24),
        name="sum_groups",
        cost_estimate=light,
    )(raw_turned, local_group[None, :], good_mask[None, :])


def facts_kernel(place_ref, facts_ref, out_ref):
    names = lax.broadcasted_iota(jnp.int32, (32, WIDE), 0)
    tops = lax.broadcasted_iota(jnp.int32, (16, WIDE), 0)

    def some(step, total):
        part = pl.ds(pl.multiple_of(step * WIDE, WIDE), WIDE)
        place = place_ref[:, part]
        top = tops == place >> 5
        picked = [jnp.where(top, facts_ref[fact : fact + 1, part], 0.0) for fact in range(facts_ref.shape[0])]
        member = (names == place & 31).astype(jnp.float32).astype(jnp.bfloat16)
        return total + across(jnp.concatenate(picked, axis=0).astype(jnp.bfloat16), member)

    out_ref[...] = lax.fori_loop(0, place_ref.shape[1] // WIDE, some, jnp.zeros(out_ref.shape, jnp.float32))


def pick_facts(place, facts):
    count = facts.shape[0]
    picked = pl.pallas_call(
        facts_kernel,
        in_specs=whole(2),
        out_specs=whole(1)[0],
        out_shape=jax.ShapeDtypeStruct((count * 16, 32), jnp.float32),
        compiler_params=roomy(16),
        name="pick_facts",
        cost_estimate=light,
    )(place[None, :], facts)
    return picked.reshape(count, 16 * 32)[:, :WIRES]


def add(first, second):
    return (first[0] + second[0], first[1] + second[1])


def sub(first, second):
    return (first[0] - second[0], first[1] - second[1])


def turn(value, sign):
    if sign < 0:
        return (value[1], -value[0])
    return (-value[1], value[0])


def scaled(value, angle):
    real, imag = math.cos(angle), math.sin(angle)
    if abs(angle) < 1e-12:
        return value
    return (value[0] * real - value[1] * imag, value[0] * imag + value[1] * real)


def four_point(items, sign):
    even_sum, even_diff = add(items[0], items[2]), sub(items[0], items[2])
    odd_sum, odd_diff = add(items[1], items[3]), turn(sub(items[1], items[3]), sign)
    return [add(even_sum, odd_sum), add(even_diff, odd_diff), sub(even_sum, odd_sum), sub(even_diff, odd_diff)]


def eighth(value, count, sign):
    root = math.sqrt(0.5)
    if count == 0:
        return value
    if count == 2:
        return turn(value, sign)
    real, imag = value
    if count == 1:
        return ((real - sign * imag) * root, (imag + sign * real) * root)
    return ((-real - sign * imag) * root, (sign * real - imag) * root)


def eight_point(items, sign):
    even = four_point(items[0::2], sign)
    odd = four_point(items[1::2], sign)
    odd = [eighth(value, count, sign) for count, value in enumerate(odd)]
    return [add(even[k], odd[k]) for k in range(4)] + [sub(even[k], odd[k]) for k in range(4)]


def slab_points(load, store, middle_ref, sign):
    for low in range(8):
        outs = four_point([load(8 * high + low) for high in range(4)], sign)
        for k, value in enumerate(outs):
            value = scaled(value, sign * 2.0 * math.pi * low * k / 32)
            middle_ref[8 * k + low, 0] = value[0]
            middle_ref[8 * k + low, 1] = value[1]
    for k in range(4):
        outs = eight_point([(middle_ref[8 * k + low, 0], middle_ref[8 * k + low, 1]) for low in range(8)], sign)
        for big, value in enumerate(outs):
            store(k + 4 * big, value)


def tail_kernel(*refs):
    sources, refs = refs[:6], refs[6:]
    take_ref, good_ref, member_ref, high_ref, low_ref, real_hbm, imag_hbm, twist_ref = refs[:8]
    tick_high_ref, tick_low_ref, untick_high_ref, untick_low_ref, back_high_ref, back_low_ref = refs[8:14]
    out_hbm, held, refs = refs[14], refs[15:21], refs[21:]
    rows_ref, plane_ref, covar_ref, power_ref, middle_ref, real_ref, imag_ref, out_ref = refs[:8]
    fetched, filter_done, out_done = refs[8:]
    early, own0, own1, got0, got1, common_ref = held
    quarters = []
    for quarter in range(4):
        part = pl.ds(quarter * SLABS // 4, SLABS // 4)
        quarters.append(
            [
                pltpu.make_async_copy(source.at[part], target.at[part], fetched.at[index, quarter])
                for index, (source, target) in enumerate(zip(sources, held))
            ]
        )
    for copies in quarters:
        for copy in copies:
            copy.start()
    filter_copies = [
        pltpu.make_async_copy(real_hbm, real_ref, filter_done.at[0]),
        pltpu.make_async_copy(imag_hbm, imag_ref, filter_done.at[1]),
    ]
    for copy in filter_copies:
        copy.start()
    covar_ref[...] = jnp.zeros_like(covar_ref)
    power_ref[...] = jnp.zeros_like(power_ref)

    def both_commons(pair):
        return jnp.concatenate([common_ref[2 * pair], common_ref[2 * pair + 1]], axis=1)

    def spread_common(commons):
        high, low = split(commons)
        return dot(member_ref[...], high) + dot(member_ref[...], low)

    def spread_power(power):
        high, rest = split(power)
        middle = (power - high.astype(jnp.float32) - rest.astype(jnp.float32)).astype(jnp.bfloat16)
        return dot(member_ref[...], high) + (dot(member_ref[...], rest) + dot(member_ref[...], middle))

    def assemble(pair, carry):
        for half in range(2):
            slab = 2 * pair + half
            base = half * PART
            for piece in range(3):
                rows = slice(piece * EARLY_ROWS, (piece + 1) * EARLY_ROWS)
                value = early[slab]
                if piece:
                    value = pltpu.roll(value, PART - piece * EARLY, 1)
                rows_ref[pair, rows, base : base + PART] = value
            for which, (own, got) in enumerate(((own0, got0), (own1, got1))):
                sent = SENT[which]
                for piece in range(2):
                    part = slice(piece * LATE, (piece + 1) * LATE)
                    at = LATE_BASE[which] + piece * LATE_ROWS[which]
                    take = take_ref[at : at + sent, :] > 0.5
                    lanes = slice(base + EARLY, base + SLAB)
                    rows_ref[pair, at : at + sent, lanes] = jnp.where(take, got[slab, :, part], own[slab, 0:sent, part])
                    if sent < LATE_ROWS[which]:
                        rest = slice(at + sent, at + LATE_ROWS[which])
                        rows_ref[pair, rest, lanes] = own[slab, sent : LATE_ROWS[which], part]
        commons = both_commons(pair)
        covar_ref[...] += rows_ref[pair] * spread_common(commons)
        power_ref[...] += commons * commons
        return carry

    for quarter in range(4):
        for copy in quarters[quarter]:
            copy.wait()
        lax.fori_loop(quarter * SLABS // 8, (quarter + 1) * SLABS // 8, assemble, 0)
    covar = jnp.sum(covar_ref[...], axis=1, keepdims=True) / TICKS
    power = jnp.sum(power_ref[...], axis=1, keepdims=True) / TICKS
    power = spread_power(jnp.broadcast_to(power, (power.shape[0], PART)))[:, 0:1]
    weight = covar / (power + epsilon_power)

    def to_wires(pair, carry):
        cleaned = good_ref[...] * (rows_ref[pair] - weight * spread_common(both_commons(pair)))
        row_high, row_low = split(cleaned)
        result = three_dot(high_ref[...], low_ref[...], row_high, row_low)
        for slab in range(2):
            for part in range(2):
                plane_ref[2 * pair + slab, part] = result[
                    part * HALF : (part + 1) * HALF, slab * PART : (slab + 1) * PART
                ]
        return carry

    for pair in range(SLABS // 2):
        to_wires(pair, 0)

    def slabs_over(index, carry, sign):
        rows = pl.ds(pl.multiple_of(index * 8, 8), 8)

        def load(item):
            real, imag = plane_ref[item, 0, rows, :], plane_ref[item, 1, rows, :]
            if sign < 0:
                return (real, imag)
            cosine, sine = twist_ref[item, 0], twist_ref[item, 1]
            return (real * cosine - imag * sine, real * sine + imag * cosine)

        def store(item, value):
            real, imag = value
            if sign < 0:
                cosine, sine = twist_ref[item, 0], twist_ref[item, 1]
                real, imag = real * cosine + imag * sine, imag * cosine - real * sine
            plane_ref[item, 0, rows, :] = real
            plane_ref[item, 1, rows, :] = imag

        slab_points(load, store, middle_ref, sign)
        return carry

    lax.fori_loop(0, HALF // 8, functools.partial(slabs_over, sign=-1), 0, unroll=2)

    def filtered(item, carry):
        data_high, data_low = split(jnp.concatenate([plane_ref[item, 0], plane_ref[item, 1]], axis=1))
        spectrum = three_dot(data_high, data_low, tick_high_ref[...], tick_low_ref[...])
        real, imag = spectrum[:, :PART], spectrum[:, PART:]
        filter_real, filter_imag = real_ref[item], imag_ref[item]
        mixed = jnp.concatenate(
            [real * filter_real - imag * filter_imag, real * filter_imag + imag * filter_real], axis=1
        )
        mixed_high, mixed_low = split(mixed)
        result = three_dot(mixed_high, mixed_low, untick_high_ref[...], untick_low_ref[...])
        plane_ref[item, 0] = result[:, :PART]
        plane_ref[item, 1] = result[:, PART:]
        return carry

    for copy in filter_copies:
        copy.wait()
    lax.fori_loop(0, SLABS, filtered, 0, unroll=16)
    lax.fori_loop(0, HALF // 8, functools.partial(slabs_over, sign=1), 0, unroll=2)
    out_copies = []
    for pair in range(SLABS // 2):
        both = jnp.concatenate(
            [plane_ref[2 * pair + slab].reshape(2 * HALF, PART) for slab in range(2)], axis=1
        )
        data_high, data_low = split(both)
        result = three_dot(back_high_ref[...], back_low_ref[...], data_high, data_low)
        for slab in range(2):
            at = (2 * pair + slab) * SLAB
            out_ref[:, at : at + SLAB] = result[:, slab * PART : slab * PART + SLAB]
        while len(out_copies) < 5 and (len(out_copies) + 1) * OUT_PART <= (pair + 1) * 2 * SLAB:
            part = pl.ds(len(out_copies) * OUT_PART, OUT_PART)
            out_copies.append(pltpu.make_async_copy(out_ref.at[:, part], out_hbm.at[:, part], out_done.at[len(out_copies)]))
            out_copies[-1].start()
    for copy in out_copies:
        copy.wait()


def tail(early, own, got, take, good, commons, member, high, low, filters):
    back_high, back_low = two_halves(wire_tables()[1])
    tick, untick, twist = tick_tables()
    tables = (twist, *two_halves(tick), *two_halves(untick), back_high, back_low)
    moved = (early, *own, *got, commons)
    operands = (*moved, take, good, member, high, low, *filters, *tables)
    far = [pl.BlockSpec(memory_space=pltpu.HBM)]
    return pl.pallas_call(
        tail_kernel,
        in_specs=far * 6 + whole(5) + far * 2 + whole(len(tables)),
        out_specs=far[0],
        out_shape=jax.ShapeDtypeStruct((WIRES, TICKS), jnp.float32),
        scratch_shapes=[pltpu.VMEM(value.shape, jnp.float32) for value in moved]
        + [
            pltpu.VMEM((SLABS // 2, WIRES, HALF), jnp.float32),
            pltpu.VMEM((SLABS, 2, HALF, PART), jnp.float32),
            pltpu.VMEM((WIRES, HALF), jnp.float32),
            pltpu.VMEM((commons.shape[1], HALF), jnp.float32),
            pltpu.VMEM((SLABS, 2, 8, PART), jnp.float32),
            pltpu.VMEM((SLABS, HALF, PART), jnp.float32),
            pltpu.VMEM((SLABS, HALF, PART), jnp.float32),
            pltpu.VMEM((WIRES, TICKS), jnp.float32),
            pltpu.SemaphoreType.DMA((6, 4)),
            pltpu.SemaphoreType.DMA((2,)),
            pltpu.SemaphoreType.DMA((5,)),
        ],
        compiler_params=roomy(60),
        name="deconvolve",
    )(*operands)


def make_filter(wire_kernel, time_kernel):
    forward, _ = wire_tables()
    wire_resp = jnp.dot(forward.astype(np.float32), wire_kernel, precision=highest).reshape(2, 1, HALF, 1)
    first = np.arange(SLABS)
    angle = 2.0 * np.pi * (np.outer(first, first) % SLABS) / SLABS
    slabs = time_kernel.reshape(SLABS, SLAB)
    real = jnp.dot(np.cos(angle).astype(np.float32), slabs, precision=highest)
    imag = jnp.dot(-np.sin(angle).astype(np.float32), slabs, precision=highest)
    twist = 2.0 * np.pi * np.outer(first, np.arange(SLAB)) / TICKS
    cosine, sine = np.cos(twist).astype(np.float32), np.sin(twist).astype(np.float32)
    real, imag = real * cosine + imag * sine, imag * cosine - real * sine
    inner = np.arange(SLAB)
    angle = 2.0 * np.pi * (np.outer(inner, inner) % SLAB) / SLAB
    cosine, sine = np.cos(angle).astype(np.float32), np.sin(angle).astype(np.float32)
    both = jnp.dot(
        jnp.concatenate([real, imag], axis=1),
        np.block([[cosine, -sine], [sine, cosine]]).astype(np.float32),
        precision=highest,
    )
    time_resp = jnp.pad(both.reshape(SLABS, 2, SLAB), ((0, 0), (0, 0), (0, PART - SLAB)))
    time_real, time_imag = time_resp[:, 0][:, None, :], time_resp[:, 1][:, None, :]
    real = wire_resp[0] * time_real - wire_resp[1] * time_imag
    imag = wire_resp[0] * time_imag + wire_resp[1] * time_real
    denominator = real * real + imag * imag + regular_term
    return real / denominator, -imag / denominator


def picked_tables(wires):
    wire_high, wire_low = two_halves(wire_tables()[0])
    picked = (jnp.arange(WIRES, dtype=jnp.int32)[:, None] == wires[None, :]).astype(jnp.bfloat16)
    return dot(jnp.asarray(wire_high), picked).astype(jnp.bfloat16), dot(jnp.asarray(wire_low), picked).astype(
        jnp.bfloat16
    )


def shards(raw, bad, group_id, chan_plane, chan_wire, plane_offset, wire_kernel, time_kernel):
    chan_count = raw.shape[0]
    group_count = chan_count // GROUP
    apa_index = lax.axis_index("apa")
    tick_index = lax.axis_index("tick")
    parity = apa_index % 2
    swap = [(i, i ^ 1) for i in range(lax.axis_size("apa"))]
    raw_turned = raw.T
    local_group = group_id - apa_index * group_count
    good_mask = 1.0 - bad.astype(jnp.float32)
    pair_base = (apa_index // 2 * 2 * SLABS).astype(jnp.int32)
    place, cross_count, early_sent = rank_rows(chan_plane, pair_base, (1 - parity).astype(jnp.int32), raw_turned)
    early_got = lax.ppermute(early_sent, "apa", swap)
    place_got = lax.ppermute(place, "apa", swap)
    late0, rows = pack_rows(place, raw_turned)
    late0, later_place, later_raw = lax.optimization_barrier((late0, place, raw_turned))
    common = sum_groups(later_raw, local_group, good_mask)
    late1 = lay_late(rows, 1)

    def over_ticks(value):
        return lax.all_to_all(value, "tick", split_axis=0, concat_axis=0, tiled=True)

    own0 = over_ticks(late0)
    common_got = lax.ppermute(common, "apa", swap)
    facts = jnp.stack([chan_wire >> 5, chan_wire & 31, local_group, bad, chan_plane - pair_base])
    facts = pick_facts(later_place - tick_index * WIRES, facts.astype(jnp.float32)).astype(jnp.int32)
    own0, late1, early_got, common_got, facts = lax.optimization_barrier((own0, late1, early_got, common_got, facts))
    first = jnp.where(parity == 0, common, common_got)
    second = jnp.where(parity == 0, common_got, common)
    commons = lax.all_gather(jnp.concatenate([first, second], axis=0), "tick")
    own1 = over_ticks(late1)
    got0 = lax.ppermute(own0[:, : SENT[0]], "apa", swap)
    take = jnp.asarray(row_order()) < cross_count
    row_take = take.astype(jnp.float32)[:, None]
    early = merge_rows(place_got, early_got, rows, row_take)
    facts_got = lax.ppermute(facts, "apa", swap)
    early, got0, facts, facts_got, late_sent = lax.optimization_barrier(
        (early, got0, facts, facts_got, own1[:, : SENT[1]])
    )
    got1 = lax.ppermute(late_sent, "apa", swap)
    early = over_ticks(early)
    row_side = jnp.where(take, 1 - parity, parity)
    facts = jnp.where(take[None, :], facts_got, facts)
    row_offset = jnp.take(plane_offset, facts[4] + pair_base)
    row_wire = (facts[0] * 32 + facts[1] + row_offset) % WIRES
    row_group = facts[2] + row_side * group_count
    row_good = 1.0 - facts[3].astype(jnp.float32)[:, None]
    member = (row_group[:, None] == jnp.arange(2 * group_count, dtype=jnp.int32)[None, :]).astype(jnp.bfloat16)
    high, low = picked_tables(row_wire)
    filters = make_filter(wire_kernel, time_kernel)
    return tail(early, (own0, own1), (got0, got1), row_take, row_good, commons, member, high, low, filters)[None]


def solution(mesh):
    placed = (P("apa", "tick"), P("apa"), P("apa"), P("apa"), P("apa"), P(), P(), P())
    return jax.shard_map(
        shards,
        mesh=mesh,
        in_specs=placed,
        out_specs=P(("apa", "tick"), None, None),
        check_vma=False,
    )
```

```python
import functools
import math

import jax
import jax.numpy as jnp
import ml_dtypes
import numpy as np
from jax import lax
from jax.experimental import pallas as pl
from jax.experimental.pallas import tpu as pltpu
from jax.sharding import PartitionSpec as P

TICKS = 3200
GROUP = 128
WIRES = 480
SLABS = 32
SLAB = 100
PART = 128
HALF = 256
EARLY = 40
LATE = 60
EARLY_ROWS = 160
LATE_ROWS = (96, 144)
LATE_BASE = (0, 192)
BLOCK = 256
WIDE = 512
OUT_PART = 640
SENT = (96, 120)

highest = lax.Precision.HIGHEST
epsilon_power = 1e-06
regular_term = 0.25
mega = 1024 * 1024


light = pl.CostEstimate(flops=1, bytes_accessed=1, transcendentals=0)


def roomy(size):
    return pltpu.CompilerParams(vmem_limit_bytes=size * mega)


def two_halves(table):
    high = table.astype(ml_dtypes.bfloat16)
    low = (table - high.astype(np.float64)).astype(ml_dtypes.bfloat16)
    return high, low


def split(value):
    high = value.astype(jnp.bfloat16)
    low = (value - high.astype(jnp.float32)).astype(jnp.bfloat16)
    return high, low


def dot(left, right):
    return jnp.dot(left, right, preferred_element_type=jnp.float32)


def three_dot(left_high, left_low, right_high, right_low):
    return dot(left_high, right_high) + (dot(left_high, right_low) + dot(left_low, right_high))


def wire_tables():
    spread = np.outer(np.arange(WIRES // 2 + 1), np.arange(WIRES)) % WIRES
    angle = 2.0 * np.pi * spread / WIRES
    forward = np.zeros((2, HALF, WIRES))
    forward[0, : WIRES // 2 + 1] = np.cos(angle)
    forward[1, : WIRES // 2 + 1] = -np.sin(angle)
    weight = np.full((WIRES // 2 + 1, 1), 2.0)
    weight[0] = weight[-1] = 1.0
    weight /= WIRES * TICKS
    backward = np.zeros((2, HALF, WIRES))
    backward[0, : WIRES // 2 + 1] = weight * np.cos(angle)
    backward[1, : WIRES // 2 + 1] = -weight * np.sin(angle)
    return forward.reshape(2 * HALF, WIRES), backward.reshape(2 * HALF, WIRES).T.copy()


def tick_tables():
    angle = 2.0 * np.pi * (np.outer(np.arange(SLAB), np.arange(SLAB)) % SLAB) / SLAB
    table = np.zeros((2, PART, 2, PART))
    table[0, :SLAB, 0, :SLAB] = table[1, :SLAB, 1, :SLAB] = np.cos(angle)
    table[0, :SLAB, 1, :SLAB] = -np.sin(angle)
    table[1, :SLAB, 0, :SLAB] = np.sin(angle)
    table = table.reshape(HALF, HALF)
    twist = 2.0 * np.pi * np.outer(np.arange(SLABS), np.arange(PART)) / TICKS
    return table, table.T.copy(), np.stack([np.cos(twist), np.sin(twist)], axis=1).astype(np.float32)[:, :, None, :]


def row_order():
    row = np.arange(WIRES)
    piece = (row >= 336).astype(np.int32)
    place = row - 192 - 144 * piece
    late = np.where(place < 114, 192 + 114 * piece + place, 420 + 30 * piece + place - 114)
    return np.where(row < 192, row, late).astype(np.int32)


def early_kernel(raw_hbm, early_hbm, early_ref, fetched, sent):
    fetches, sends = [], []
    for piece in range(EARLY // 8):
        part = pl.ds(piece * 8, 8)
        fetches.append(pltpu.make_async_copy(raw_hbm.at[part], early_ref.at[part], fetched.at[piece]))
        sends.append(pltpu.make_async_copy(early_ref.at[part], early_hbm.at[part], sent.at[piece]))
    for fetch in fetches:
        fetch.start()
    for fetch, send in zip(fetches, sends):
        fetch.wait()
        send.start()
    for send in sends:
        send.wait()


def early_ticks(raw_turned):
    chan_count = raw_turned.shape[1]
    far = pl.BlockSpec(memory_space=pltpu.HBM)
    return pl.pallas_call(
        early_kernel,
        in_specs=[far],
        out_specs=far,
        out_shape=jax.ShapeDtypeStruct((EARLY, chan_count), jnp.float32),
        scratch_shapes=[
            pltpu.VMEM((EARLY, chan_count), jnp.float32),
            pltpu.SemaphoreType.DMA((EARLY // 8,)),
            pltpu.SemaphoreType.DMA((EARLY // 8,)),
        ],
        compiler_params=roomy(60),
        name="early_ticks",
    )(raw_turned)


def rank_kernel(plane_ref, base_ref, cross_ref, place_ref, count_ref):
    tri_row = lax.broadcasted_iota(jnp.int32, (BLOCK, BLOCK), 0)
    tri_col = lax.broadcasted_iota(jnp.int32, (BLOCK, BLOCK), 1)
    earlier = (tri_row < tri_col).astype(jnp.float32).astype(jnp.bfloat16)
    names = lax.broadcasted_iota(jnp.int32, (2 * SLABS, BLOCK), 0)
    pair_base = base_ref[0]
    cross_side = cross_ref[0]
    chan_count = plane_ref.shape[1]
    local = plane_ref[...] - pair_base
    is_cross = (local // SLABS == cross_side).astype(jnp.float32)
    cross_count = jnp.sum(is_cross, axis=1, keepdims=True) * (1.0 / SLABS)
    before = jnp.zeros((2 * SLABS, 1), jnp.float32)
    for block in range(chan_count // BLOCK):
        part = slice(block * BLOCK, (block + 1) * BLOCK)
        member = (names == local[:, part]).astype(jnp.float32)
        prefix = dot(member.astype(jnp.bfloat16), earlier) + before
        rank = jnp.sum(member * prefix, axis=0, keepdims=True)
        before = before + jnp.sum(member, axis=1, keepdims=True)
        order = (rank + (1.0 - is_cross[:, part]) * cross_count).astype(jnp.int32)
        near_row = order + jnp.where(order >= 306, 30, 0)
        far_row = order - 114 + jnp.where(order >= 450, 114, 0)
        row = jnp.where(order < 192, order, jnp.where(order < 420, near_row, far_row))
        place_ref[:, part] = (local[:, part] % SLABS) * WIRES + row
    count_ref[...] = jnp.broadcast_to(cross_count.astype(jnp.int32), count_ref.shape)


def rank_rows(chan_plane, pair_base, cross_side):
    chan_count = chan_plane.shape[0]
    scalar = pl.BlockSpec(memory_space=pltpu.SMEM)
    place, count = pl.pallas_call(
        rank_kernel,
        in_specs=whole(1) + [scalar, scalar],
        out_specs=whole(2),
        out_shape=[
            jax.ShapeDtypeStruct((1, chan_count), jnp.int32),
            jax.ShapeDtypeStruct((8, 128), jnp.int32),
        ],
        compiler_params=roomy(16),
        name="rank_rows",
    )(chan_plane[None, :], pair_base[None], cross_side[None])
    return place[0], count[0, 0]


def whole(count):
    return [pl.BlockSpec(memory_space=pltpu.VMEM)] * count


def turned_scatter(place_ref, raw_ref, rows_ref, even_ref, odd_ref):
    ticks, chan_count = raw_ref.shape
    steps = chan_count // WIDE

    def turn_block(step, to_ref):
        at = pl.multiple_of(step * WIDE, WIDE)
        to_ref[:, 0:ticks] = raw_ref[:, pl.ds(at, WIDE)].T

    def move(step, from_ref):
        first = step * WIDE
        for row in range(WIDE):
            rows_ref[pl.ds(place_ref[first + row], 1), :] = from_ref[pl.ds(row, 1), :]

    turn_block(0, even_ref)

    def both(half, carry):
        turn_block(2 * half + 1, odd_ref)
        move(2 * half, even_ref)
        turn_block(jnp.minimum(2 * half + 2, steps - 2), even_ref)
        move(2 * half + 1, odd_ref)
        return carry

    lax.fori_loop(0, steps // 2, both, 0)


def late_kernel(which, rows_ref, out_ref, low=0, high=SLABS):
    size = LATE_ROWS[which]

    def one_slot(slot, carry):
        start = pl.multiple_of(slot * WIRES, 8)
        for piece in range(2):
            at = start + LATE_BASE[which] + piece * size
            out_ref[slot, :, piece * LATE : (piece + 1) * LATE] = rows_ref[pl.ds(at, size), EARLY:SLAB]
        return carry

    lax.fori_loop(low, high, one_slot, 0)


def late_shape(which):
    return jax.ShapeDtypeStruct((SLABS, LATE_ROWS[which], PART), jnp.float32)


def pack_kernel(place_ref, raw_ref, late_out, rows_out, rows_ref, late_ref, even_ref, odd_ref, rows_done, late_done):
    turned_scatter(place_ref, raw_ref, rows_ref, even_ref, odd_ref)
    keep = pltpu.make_async_copy(rows_ref, rows_out, rows_done)
    keep.start()
    late_kernel(0, rows_ref, late_ref)
    send = pltpu.make_async_copy(late_ref, late_out, late_done)
    send.start()
    keep.wait()
    send.wait()


def pack_rows(place, raw_turned):
    chan_count = raw_turned.shape[1]
    return pl.pallas_call(
        pack_kernel,
        in_specs=[pl.BlockSpec(memory_space=pltpu.SMEM)] + whole(1),
        out_specs=[pl.BlockSpec(memory_space=pltpu.HBM)] * 2,
        out_shape=[late_shape(0), jax.ShapeDtypeStruct((chan_count, PART), jnp.float32)],
        scratch_shapes=[
            pltpu.VMEM((chan_count, PART), jnp.float32),
            pltpu.VMEM((SLABS, LATE_ROWS[0], PART), jnp.float32),
        ]
        + [pltpu.VMEM((WIDE, PART), jnp.float32)] * 2
        + [pltpu.SemaphoreType.DMA] * 2,
        compiler_params=roomy(60),
        name="pack_rows",
    )(place, raw_turned)


def fetched_late_kernel(which, rows_hbm, out_ref, rows_ref, done_ref):
    quarter = rows_ref.shape[0] // 4
    copies = [
        pltpu.make_async_copy(
            rows_hbm.at[pl.ds(part * quarter, quarter)], rows_ref.at[pl.ds(part * quarter, quarter)], done_ref.at[part]
        )
        for part in range(4)
    ]
    for copy in copies:
        copy.start()
    for part, copy in enumerate(copies):
        copy.wait()
        late_kernel(which, rows_ref, out_ref, part * SLABS // 4, (part + 1) * SLABS // 4)


def lay_late(rows, which):
    return pl.pallas_call(
        functools.partial(fetched_late_kernel, which),
        in_specs=[pl.BlockSpec(memory_space=pltpu.HBM)],
        out_specs=whole(1)[0],
        out_shape=late_shape(which),
        scratch_shapes=[pltpu.VMEM(rows.shape, jnp.float32), pltpu.SemaphoreType.DMA((4,))],
        compiler_params=roomy(60),
        name="lay_late",
        cost_estimate=light,
    )(rows)


def merge_kernel(place_ref, raw_ref, own_hbm, take_ref, out_ref, rows_ref, even_ref, odd_ref, own_ref, own_done):
    fetch = pltpu.make_async_copy(own_hbm, own_ref, own_done)
    fetch.start()
    turned_scatter(place_ref, raw_ref, rows_ref, even_ref, odd_ref)
    fetch.wait()

    def one_slot(slot, carry):
        start = pl.multiple_of(slot * WIRES, 8)
        for piece in range(3):
            rows = pl.ds(start + piece * EARLY_ROWS, EARLY_ROWS)
            take = take_ref[piece * EARLY_ROWS : (piece + 1) * EARLY_ROWS, :] > 0.5
            value = jnp.where(take, rows_ref[rows, 0:EARLY], own_ref[rows, 0:EARLY])
            out_ref[slot, :, piece * EARLY : (piece + 1) * EARLY] = value
        out_ref[slot, :, 3 * EARLY : PART] = jnp.zeros((EARLY_ROWS, PART - 3 * EARLY), jnp.float32)
        return carry

    lax.fori_loop(0, SLABS, one_slot, 0)


def merge_rows(place, raw_turned, own, take):
    chan_count = raw_turned.shape[1]
    return pl.pallas_call(
        merge_kernel,
        in_specs=[pl.BlockSpec(memory_space=pltpu.SMEM)] + whole(1) + [pl.BlockSpec(memory_space=pltpu.HBM)] + whole(1),
        out_specs=whole(1)[0],
        out_shape=jax.ShapeDtypeStruct((SLABS, EARLY_ROWS, PART), jnp.float32),
        scratch_shapes=[pltpu.VMEM((chan_count, PART), jnp.float32)]
        + [pltpu.VMEM((WIDE, PART), jnp.float32)] * 2
        + [pltpu.VMEM((chan_count, PART), jnp.float32), pltpu.SemaphoreType.DMA],
        compiler_params=roomy(60),
        name="merge_rows",
    )(place, raw_turned, own, take)


def across(left, right):
    return lax.dot_general(left, right, (((1,), (1,)), ((), ())), preferred_element_type=jnp.float32)


def group_kernel(raw_ref, group_ref, good_ref, out_ref):
    group_count = out_ref.shape[0]
    names = lax.broadcasted_iota(jnp.int32, (group_count, WIDE), 0)

    def some(step, total):
        part = pl.ds(pl.multiple_of(step * WIDE, WIDE), WIDE)
        member = jnp.where(names == group_ref[:, part], good_ref[:, part], 0.0).astype(jnp.bfloat16)
        high, low = split(raw_ref[:, part])
        return total + (across(member, high) + across(member, low))

    zero = jnp.zeros((group_count, SLAB), jnp.float32)
    out_ref[...] = jnp.zeros_like(out_ref)
    out_ref[:, 0:SLAB] = lax.fori_loop(0, raw_ref.shape[1] // WIDE, some, zero)


def sum_groups(raw_turned, local_group, good_mask):
    group_count = raw_turned.shape[1] // GROUP
    return pl.pallas_call(
        group_kernel,
        in_specs=whole(3),
        out_specs=whole(1)[0],
        out_shape=jax.ShapeDtypeStruct((group_count, PART), jnp.float32),
        compiler_params=roomy(24),
        name="sum_groups",
        cost_estimate=light,
    )(raw_turned, local_group[None, :], good_mask[None, :])


def facts_kernel(place_ref, facts_ref, out_ref):
    names = lax.broadcasted_iota(jnp.int32, (32, WIDE), 0)
    tops = lax.broadcasted_iota(jnp.int32, (16, WIDE), 0)

    def some(step, total):
        part = pl.ds(pl.multiple_of(step * WIDE, WIDE), WIDE)
        place = place_ref[:, part]
        top = tops == place >> 5
        picked = [jnp.where(top, facts_ref[fact : fact + 1, part], 0.0) for fact in range(facts_ref.shape[0])]
        member = (names == place & 31).astype(jnp.float32).astype(jnp.bfloat16)
        return total + across(jnp.concatenate(picked, axis=0).astype(jnp.bfloat16), member)

    out_ref[...] = lax.fori_loop(0, place_ref.shape[1] // WIDE, some, jnp.zeros(out_ref.shape, jnp.float32))


def pick_facts(place, facts):
    count = facts.shape[0]
    picked = pl.pallas_call(
        facts_kernel,
        in_specs=whole(2),
        out_specs=whole(1)[0],
        out_shape=jax.ShapeDtypeStruct((count * 16, 32), jnp.float32),
        compiler_params=roomy(16),
        name="pick_facts",
        cost_estimate=light,
    )(place[None, :], facts)
    return picked.reshape(count, 16 * 32)[:, :WIRES]


def add(first, second):
    return (first[0] + second[0], first[1] + second[1])


def sub(first, second):
    return (first[0] - second[0], first[1] - second[1])


def turn(value, sign):
    if sign < 0:
        return (value[1], -value[0])
    return (-value[1], value[0])


def scaled(value, angle):
    real, imag = math.cos(angle), math.sin(angle)
    if abs(angle) < 1e-12:
        return value
    return (value[0] * real - value[1] * imag, value[0] * imag + value[1] * real)


def four_point(items, sign):
    even_sum, even_diff = add(items[0], items[2]), sub(items[0], items[2])
    odd_sum, odd_diff = add(items[1], items[3]), turn(sub(items[1], items[3]), sign)
    return [add(even_sum, odd_sum), add(even_diff, odd_diff), sub(even_sum, odd_sum), sub(even_diff, odd_diff)]


def eighth(value, count, sign):
    root = math.sqrt(0.5)
    if count == 0:
        return value
    if count == 2:
        return turn(value, sign)
    real, imag = value
    if count == 1:
        return ((real - sign * imag) * root, (imag + sign * real) * root)
    return ((-real - sign * imag) * root, (sign * real - imag) * root)


def eight_point(items, sign):
    even = four_point(items[0::2], sign)
    odd = four_point(items[1::2], sign)
    odd = [eighth(value, count, sign) for count, value in enumerate(odd)]
    return [add(even[k], odd[k]) for k in range(4)] + [sub(even[k], odd[k]) for k in range(4)]


def slab_points(load, store, middle_ref, sign):
    for low in range(8):
        outs = four_point([load(8 * high + low) for high in range(4)], sign)
        for k, value in enumerate(outs):
            value = scaled(value, sign * 2.0 * math.pi * low * k / 32)
            middle_ref[8 * k + low, 0] = value[0]
            middle_ref[8 * k + low, 1] = value[1]
    for k in range(4):
        outs = eight_point([(middle_ref[8 * k + low, 0], middle_ref[8 * k + low, 1]) for low in range(8)], sign)
        for big, value in enumerate(outs):
            store(k + 4 * big, value)


def tail_kernel(*refs):
    sources, refs = refs[:6], refs[6:]
    take_ref, good_ref, member_ref, high_ref, low_ref, real_hbm, imag_hbm, twist_ref = refs[:8]
    tick_high_ref, tick_low_ref, untick_high_ref, untick_low_ref, back_high_ref, back_low_ref = refs[8:14]
    out_hbm, held, refs = refs[14], refs[15:21], refs[21:]
    rows_ref, plane_ref, covar_ref, power_ref, middle_ref, real_ref, imag_ref, out_ref = refs[:8]
    fetched, filter_done, out_done = refs[8:]
    early, own0, own1, got0, got1, common_ref = held
    quarters = []
    for quarter in range(4):
        part = pl.ds(quarter * SLABS // 4, SLABS // 4)
        quarters.append(
            [
                pltpu.make_async_copy(source.at[part], target.at[part], fetched.at[index, quarter])
                for index, (source, target) in enumerate(zip(sources, held))
            ]
        )
    for copies in quarters:
        for copy in copies:
            copy.start()
    filter_copies = [
        pltpu.make_async_copy(real_hbm, real_ref, filter_done.at[0]),
        pltpu.make_async_copy(imag_hbm, imag_ref, filter_done.at[1]),
    ]
    for copy in filter_copies:
        copy.start()
    covar_ref[...] = jnp.zeros_like(covar_ref)
    power_ref[...] = jnp.zeros_like(power_ref)

    def both_commons(pair):
        return jnp.concatenate([common_ref[2 * pair], common_ref[2 * pair + 1]], axis=1)

    def spread_common(commons):
        high, low = split(commons)
        return dot(member_ref[...], high) + dot(member_ref[...], low)

    def spread_power(power):
        high, rest = split(power)
        middle = (power - high.astype(jnp.float32) - rest.astype(jnp.float32)).astype(jnp.bfloat16)
        return dot(member_ref[...], high) + (dot(member_ref[...], rest) + dot(member_ref[...], middle))

    def assemble(pair, carry):
        for half in range(2):
            slab = 2 * pair + half
            base = half * PART
            for piece in range(3):
                rows = slice(piece * EARLY_ROWS, (piece + 1) * EARLY_ROWS)
                value = early[slab]
                if piece:
                    value = pltpu.roll(value, PART - piece * EARLY, 1)
                rows_ref[pair, rows, base : base + PART] = value
            for which, (own, got) in enumerate(((own0, got0), (own1, got1))):
                sent = SENT[which]
                for piece in range(2):
                    part = slice(piece * LATE, (piece + 1) * LATE)
                    at = LATE_BASE[which] + piece * LATE_ROWS[which]
                    take = take_ref[at : at + sent, :] > 0.5
                    lanes = slice(base + EARLY, base + SLAB)
                    rows_ref[pair, at : at + sent, lanes] = jnp.where(take, got[slab, :, part], own[slab, 0:sent, part])
                    if sent < LATE_ROWS[which]:
                        rest = slice(at + sent, at + LATE_ROWS[which])
                        rows_ref[pair, rest, lanes] = own[slab, sent : LATE_ROWS[which], part]
        commons = both_commons(pair)
        covar_ref[...] += rows_ref[pair] * spread_common(commons)
        power_ref[...] += commons * commons
        return carry

    for quarter in range(4):
        for copy in quarters[quarter]:
            copy.wait()
        lax.fori_loop(quarter * SLABS // 8, (quarter + 1) * SLABS // 8, assemble, 0)
    covar = jnp.sum(covar_ref[...], axis=1, keepdims=True) / TICKS
    power = jnp.sum(power_ref[...], axis=1, keepdims=True) / TICKS
    power = spread_power(jnp.broadcast_to(power, (power.shape[0], PART)))[:, 0:1]
    weight = covar / (power + epsilon_power)

    def to_wires(pair, carry):
        cleaned = good_ref[...] * (rows_ref[pair] - weight * spread_common(both_commons(pair)))
        row_high, row_low = split(cleaned)
        result = three_dot(high_ref[...], low_ref[...], row_high, row_low)
        for slab in range(2):
            for part in range(2):
                plane_ref[2 * pair + slab, part] = result[
                    part * HALF : (part + 1) * HALF, slab * PART : (slab + 1) * PART
                ]
        return carry

    for pair in range(SLABS // 2):
        to_wires(pair, 0)

    def slabs_over(index, carry, sign):
        rows = pl.ds(pl.multiple_of(index * 8, 8), 8)

        def load(item):
            real, imag = plane_ref[item, 0, rows, :], plane_ref[item, 1, rows, :]
            if sign < 0:
                return (real, imag)
            cosine, sine = twist_ref[item, 0], twist_ref[item, 1]
            return (real * cosine - imag * sine, real * sine + imag * cosine)

        def store(item, value):
            real, imag = value
            if sign < 0:
                cosine, sine = twist_ref[item, 0], twist_ref[item, 1]
                real, imag = real * cosine + imag * sine, imag * cosine - real * sine
            plane_ref[item, 0, rows, :] = real
            plane_ref[item, 1, rows, :] = imag

        slab_points(load, store, middle_ref, sign)
        return carry

    lax.fori_loop(0, HALF // 8, functools.partial(slabs_over, sign=-1), 0, unroll=2)

    def filtered(item, carry):
        data_high, data_low = split(jnp.concatenate([plane_ref[item, 0], plane_ref[item, 1]], axis=1))
        spectrum = three_dot(data_high, data_low, tick_high_ref[...], tick_low_ref[...])
        real, imag = spectrum[:, :PART], spectrum[:, PART:]
        filter_real, filter_imag = real_ref[item], imag_ref[item]
        mixed = jnp.concatenate(
            [real * filter_real - imag * filter_imag, real * filter_imag + imag * filter_real], axis=1
        )
        mixed_high, mixed_low = split(mixed)
        result = three_dot(mixed_high, mixed_low, untick_high_ref[...], untick_low_ref[...])
        plane_ref[item, 0] = result[:, :PART]
        plane_ref[item, 1] = result[:, PART:]
        return carry

    for copy in filter_copies:
        copy.wait()
    lax.fori_loop(0, SLABS, filtered, 0, unroll=16)
    lax.fori_loop(0, HALF // 8, functools.partial(slabs_over, sign=1), 0, unroll=2)
    out_copies = []
    for pair in range(SLABS // 2):
        both = jnp.concatenate(
            [plane_ref[2 * pair + slab].reshape(2 * HALF, PART) for slab in range(2)], axis=1
        )
        data_high, data_low = split(both)
        result = three_dot(back_high_ref[...], back_low_ref[...], data_high, data_low)
        for slab in range(2):
            at = (2 * pair + slab) * SLAB
            out_ref[:, at : at + SLAB] = result[:, slab * PART : slab * PART + SLAB]
        while len(out_copies) < 5 and (len(out_copies) + 1) * OUT_PART <= (pair + 1) * 2 * SLAB:
            part = pl.ds(len(out_copies) * OUT_PART, OUT_PART)
            out_copies.append(pltpu.make_async_copy(out_ref.at[:, part], out_hbm.at[:, part], out_done.at[len(out_copies)]))
            out_copies[-1].start()
    for copy in out_copies:
        copy.wait()


def tail(early, own, got, take, good, commons, member, high, low, filters):
    back_high, back_low = two_halves(wire_tables()[1])
    tick, untick, twist = tick_tables()
    tables = (twist, *two_halves(tick), *two_halves(untick), back_high, back_low)
    moved = (early, *own, *got, commons)
    operands = (*moved, take, good, member, high, low, *filters, *tables)
    far = [pl.BlockSpec(memory_space=pltpu.HBM)]
    return pl.pallas_call(
        tail_kernel,
        in_specs=far * 6 + whole(5) + far * 2 + whole(len(tables)),
        out_specs=far[0],
        out_shape=jax.ShapeDtypeStruct((WIRES, TICKS), jnp.float32),
        scratch_shapes=[pltpu.VMEM(value.shape, jnp.float32) for value in moved]
        + [
            pltpu.VMEM((SLABS // 2, WIRES, HALF), jnp.float32),
            pltpu.VMEM((SLABS, 2, HALF, PART), jnp.float32),
            pltpu.VMEM((WIRES, HALF), jnp.float32),
            pltpu.VMEM((commons.shape[1], HALF), jnp.float32),
            pltpu.VMEM((SLABS, 2, 8, PART), jnp.float32),
            pltpu.VMEM((SLABS, HALF, PART), jnp.float32),
            pltpu.VMEM((SLABS, HALF, PART), jnp.float32),
            pltpu.VMEM((WIRES, TICKS), jnp.float32),
            pltpu.SemaphoreType.DMA((6, 4)),
            pltpu.SemaphoreType.DMA((2,)),
            pltpu.SemaphoreType.DMA((5,)),
        ],
        compiler_params=roomy(60),
        name="deconvolve",
    )(*operands)


def make_filter(wire_kernel, time_kernel):
    forward, _ = wire_tables()
    wire_resp = jnp.dot(forward.astype(np.float32), wire_kernel, precision=highest).reshape(2, 1, HALF, 1)
    first = np.arange(SLABS)
    angle = 2.0 * np.pi * (np.outer(first, first) % SLABS) / SLABS
    slabs = time_kernel.reshape(SLABS, SLAB)
    real = jnp.dot(np.cos(angle).astype(np.float32), slabs, precision=highest)
    imag = jnp.dot(-np.sin(angle).astype(np.float32), slabs, precision=highest)
    twist = 2.0 * np.pi * np.outer(first, np.arange(SLAB)) / TICKS
    cosine, sine = np.cos(twist).astype(np.float32), np.sin(twist).astype(np.float32)
    real, imag = real * cosine + imag * sine, imag * cosine - real * sine
    inner = np.arange(SLAB)
    angle = 2.0 * np.pi * (np.outer(inner, inner) % SLAB) / SLAB
    cosine, sine = np.cos(angle).astype(np.float32), np.sin(angle).astype(np.float32)
    both = jnp.dot(
        jnp.concatenate([real, imag], axis=1),
        np.block([[cosine, -sine], [sine, cosine]]).astype(np.float32),
        precision=highest,
    )
    time_resp = jnp.pad(both.reshape(SLABS, 2, SLAB), ((0, 0), (0, 0), (0, PART - SLAB)))
    time_real, time_imag = time_resp[:, 0][:, None, :], time_resp[:, 1][:, None, :]
    real = wire_resp[0] * time_real - wire_resp[1] * time_imag
    imag = wire_resp[0] * time_imag + wire_resp[1] * time_real
    denominator = real * real + imag * imag + regular_term
    return real / denominator, -imag / denominator


def picked_tables(wires):
    wire_high, wire_low = two_halves(wire_tables()[0])
    picked = (jnp.arange(WIRES, dtype=jnp.int32)[:, None] == wires[None, :]).astype(jnp.bfloat16)
    return dot(jnp.asarray(wire_high), picked).astype(jnp.bfloat16), dot(jnp.asarray(wire_low), picked).astype(
        jnp.bfloat16
    )


def shards(raw, bad, group_id, chan_plane, chan_wire, plane_offset, wire_kernel, time_kernel):
    chan_count = raw.shape[0]
    group_count = chan_count // GROUP
    apa_index = lax.axis_index("apa")
    tick_index = lax.axis_index("tick")
    parity = apa_index % 2
    swap = [(i, i ^ 1) for i in range(lax.axis_size("apa"))]
    raw_turned = raw.T
    local_group = group_id - apa_index * group_count
    good_mask = 1.0 - bad.astype(jnp.float32)
    pair_base = (apa_index // 2 * 2 * SLABS).astype(jnp.int32)
    early_sent, chan_plane = lax.optimization_barrier((early_ticks(raw_turned), chan_plane))
    early_got = lax.ppermute(early_sent, "apa", swap)
    place, cross_count = rank_rows(chan_plane, pair_base, (1 - parity).astype(jnp.int32))
    late0, rows = pack_rows(place, raw_turned)
    late0, later_place, later_raw = lax.optimization_barrier((late0, place, raw_turned))
    place_got = lax.ppermute(later_place, "apa", swap)
    common = sum_groups(later_raw, local_group, good_mask)
    late1 = lay_late(rows, 1)

    def over_ticks(value):
        return lax.all_to_all(value, "tick", split_axis=0, concat_axis=0, tiled=True)

    own0 = over_ticks(late0)
    common_got = lax.ppermute(common, "apa", swap)
    facts = jnp.stack([chan_wire >> 5, chan_wire & 31, local_group, bad, chan_plane - pair_base])
    facts = pick_facts(later_place - tick_index * WIRES, facts.astype(jnp.float32)).astype(jnp.int32)
    own0, late1, early_got, common_got, facts, place_got = lax.optimization_barrier(
        (own0, late1, early_got, common_got, facts, place_got)
    )
    first = jnp.where(parity == 0, common, common_got)
    second = jnp.where(parity == 0, common_got, common)
    commons = lax.all_gather(jnp.concatenate([first, second], axis=0), "tick")
    own1 = over_ticks(late1)
    got0 = lax.ppermute(own0[:, : SENT[0]], "apa", swap)
    take = jnp.asarray(row_order()) < cross_count
    row_take = take.astype(jnp.float32)[:, None]
    early = merge_rows(place_got, early_got, rows, row_take)
    facts_got = lax.ppermute(facts, "apa", swap)
    early, got0, facts, facts_got, late_sent = lax.optimization_barrier(
        (early, got0, facts, facts_got, own1[:, : SENT[1]])
    )
    got1 = lax.ppermute(late_sent, "apa", swap)
    early = over_ticks(early)
    row_side = jnp.where(take, 1 - parity, parity)
    facts = jnp.where(take[None, :], facts_got, facts)
    row_offset = jnp.take(plane_offset, facts[4] + pair_base)
    row_wire = (facts[0] * 32 + facts[1] + row_offset) % WIRES
    row_group = facts[2] + row_side * group_count
    row_good = 1.0 - facts[3].astype(jnp.float32)[:, None]
    member = (row_group[:, None] == jnp.arange(2 * group_count, dtype=jnp.int32)[None, :]).astype(jnp.bfloat16)
    high, low = picked_tables(row_wire)
    filters = make_filter(wire_kernel, time_kernel)
    return tail(early, (own0, own1), (got0, got1), row_take, row_good, commons, member, high, low, filters)[None]


def solution(mesh):
    placed = (P("apa", "tick"), P("apa"), P("apa"), P("apa"), P("apa"), P(), P(), P())
    return jax.shard_map(
        shards,
        mesh=mesh,
        in_specs=placed,
        out_specs=P(("apa", "tick"), None, None),
        check_vma=False,
    )
```
